128 devices in a mesh: fsdp: 8 (over z, core), emb: 16 (over y, x).
Axes of the slice: x: 4, y: 4, z: 4, core: 2. Of those that a mesh axis runs over, the one named last changes fastest.
Arguments:
- item_table: float32 [524288, 256], P(('fsdp', 'emb')), may hold values from -6 to 6
- item_owner: int32 [128, 1024, 1], P(('fsdp', 'emb')), may hold values from 0 to 127; in each aligned block of 1024 rows (0 to 1023, 1024 to 2047, ..., all dimensions but the last counted through in order) at most 16 rows name the same one
- item_row: int32 [128, 1024], P(('fsdp', 'emb')), may hold values from 0 to 4095
- staleness: int32 [524288], P(('fsdp', 'emb')), may hold values from 0 to 3
- w_proj: bfloat16 [2, 256, 1024], P(None, 'fsdp'), may hold values from -0.375 to 0.375
- w_out: bfloat16 [2, 256, 256], P(None, 'fsdp'), may hold values from -0.375 to 0.375
- out_grad: bfloat16 [128, 1024, 256], P(('fsdp', 'emb')), may hold values from -6 to 6
Outputs:
- new_table: float32 [524288, 256], P(('fsdp', 'emb'))
- w_proj_grad: float32 [2, 256, 1024], P(None, 'fsdp')
- w_out_grad: float32 [2, 256, 256], P(None, 'fsdp')
The draws below stay inside these ranges and needn't reach their ends.
Inputs may be any that keep to these rules, and one draw needn't show every extreme that they name: `item_owner`: in each user's history no owner is named more than 16 times, a bound that some block reaches in every draw.
All inputs are finite; a program needn't handle non-finite values.
Results may differ from the reference program's by a relative error of at most 0.023.
Values may be sent and summed in bfloat16 or wider, within the bound.
A program may use at most 128 MiB of HBM per device.

```python
import math
import jax
import jax.numpy as jnp
import numpy as np
from jax import lax

D = 256
HEADS = 4
DH = 64
HD = 256
LAYERS = 2
SEQ = 1024
ROWS_OWN = 4096
USERS = 128
CAP = 16
ITEMS = 524288
N_FSDP = 8
N_EMB = 16


def set_ends(array, stream_key, low, largest):
    spot = [jax.random.randint(jax.random.fold_in(stream_key, axis), (), 0, length) for axis, length in enumerate(array.shape)]
    longest = array.shape.index(max(array.shape))
    next_to = spot[:longest] + [(spot[longest] + 1) % array.shape[longest]] + spot[longest + 1:]
    return array.at[tuple(spot)].set(low).at[tuple(next_to)].set(largest)


def steps_of(key, dims, split, least, largest):
    gain, own = 1.0, jax.random.fold_in(key, 6)
    for axis_at, blocks in split:
        steps = jnp.exp(jax.random.uniform(jax.random.fold_in(own, axis_at), (blocks,), jnp.float32, least / len(split), largest / len(split)))
        gain = gain * jnp.repeat(steps, dims[axis_at] // blocks).reshape([-1 if axis == axis_at else 1 for axis in range(len(dims))])
    return gain


def rank_table(amount, slope):
    weights = [(1 << 20) // math.isqrt(grade ** slope) + 1 for grade in range(1, amount + 1)]
    deviation = 1 + sum(weights) // (1 << 30)
    return np.cumsum(np.array([max(1, weight // deviation) for weight in weights]))


def skewed_ids(key, extent, amount, skew):
    grid = rank_table(amount, skew)
    pick = jax.random.randint(jax.random.fold_in(key, 1), extent, 0, int(grid[amount - 1]))
    rank = jnp.searchsorted(jnp.asarray(grid, jnp.int32), pick, side="right")
    return jax.random.permutation(jax.random.fold_in(key, 2), amount)[rank].astype(jnp.int32)


def deal_out(rng, own, number, rows, number_of, top, bound, skew):
    order = jax.random.permutation(rng, number_of)
    crowded, ordinary = shares(number_of, rows * top, bound, skew, True), shares(number_of, rows * top, bound, skew, False)
    places = jnp.arange(number_of)

    def named(sizes, turn):
        used = int((sizes > 0).sum())
        fixed = max(1, used // 4)
        moved = fixed + (places - fixed + turn * (used - fixed)) % max(1, number_of - fixed)
        return jnp.zeros((number_of,), jnp.int32).at[order[jnp.where(places < fixed, places, moved)]].set(jnp.asarray(sizes, jnp.int32))

    sizes = jnp.where(number % 4 == 0, named(crowded, number // 4), named(ordinary, number - number // 4 - 1))
    mixed = jax.random.permutation(jax.random.fold_in(own, 3), number_of)
    donor, taker = mixed[0:number_of // 2 * 2:2], mixed[1:number_of // 2 * 2:2]
    room = jnp.minimum(sizes[donor] - 1, bound - sizes[taker]) // 2
    room = jnp.where((donor == order[0]) | (taker == order[0]) | (sizes[taker] == 0), 0, jnp.maximum(room, 0))
    moved = jax.random.randint(jax.random.fold_in(own, 4), (number_of // 2,), 0, 1 << 20) % (room + 1)
    sizes = sizes.at[donor].add(-moved).at[taker].add(moved)
    members = jnp.searchsorted(jnp.cumsum(sizes), jnp.arange(rows * top), side="right").astype(jnp.int32)
    table = members.reshape(top, rows).T
    table = table[jax.random.permutation(jax.random.fold_in(own, 1), rows)]
    turn = jax.random.randint(jax.random.fold_in(own, 2), (rows, 1), 0, top)
    return jnp.take_along_axis(table, (jnp.arange(top)[None, :] + turn) % top, axis=1)


def shares(amount, total, bound, slope, full):
    portions = [(1 << 20) // math.isqrt(standing ** slope) + 1 for standing in range(1, amount + 1)]
    largest = bound if full else min(bound, max(-(-total // amount), total * portions[0] // sum(portions)))
    least = 1 if total - largest >= amount - 1 else 0
    holding, surplus = [largest] + [least] * (amount - 1), total - largest - least * (amount - 1)
    while surplus > 0:
        movable = [i for i in range(1, amount) if holding[i] < largest] or [i for i in range(1, amount) if holding[i] < bound]
        pool, remaining = sum([portions[i] for i in movable]), surplus
        for i in movable:
            addition = min(bound - holding[i], max(1, remaining * portions[i] // pool), surplus)
            holding[i] = holding[i] + addition
            surplus = surplus - addition
    return np.array(holding)


def centred(rng, dims, deviation, limit, cuts=(), kind=jnp.bfloat16):
    gain = steps_of(rng, dims, cuts, -0.22, 0.18) if cuts else 1.0
    result = jax.random.normal(rng, dims, jnp.float32) * deviation * gain
    return jnp.minimum(jnp.maximum(result, -limit), limit).astype(kind)


def setup_inputs(seed: int = 0) -> dict:
    key_list = jax.random.split(jax.random.key(seed), 8)
    item_table = centred(key_list[0], (ITEMS, D), 1.0, 6.0, ((0, 128),), jnp.float32)
    item_owner_keys = jax.random.split(jax.random.fold_in(key_list[1], 1), USERS * SEQ // SEQ)
    item_owner_turns = jax.random.permutation(jax.random.fold_in(key_list[1], 3), USERS * SEQ // SEQ)
    item_owner = jax.vmap(lambda own, number: deal_out(jax.random.fold_in(key_list[1], 2), own, number, SEQ, USERS, 1, CAP, 2))(item_owner_keys, item_owner_turns).reshape((USERS, SEQ, 1))
    item_row = set_ends(skewed_ids(key_list[2], (USERS, SEQ), ROWS_OWN, 2), jax.random.fold_in(key_list[2], 3), 0, ROWS_OWN - 1).astype(jnp.int32)
    staleness = set_ends(jax.random.randint(key_list[3], (ITEMS,), 0, 4), jax.random.fold_in(key_list[3], 1), 0, 3).astype(jnp.int32)
    w_proj = centred(key_list[4], (LAYERS, D, 4 * HD), D ** -0.5, 0.375, ((1, 8),))
    w_out = centred(key_list[5], (LAYERS, HD, D), HD ** -0.5, 0.375, ((1, 8),))
    out_grad = centred(key_list[6], (USERS, SEQ, D), 1.0, 6.0, ((0, 128),))
    return dict(item_table=item_table, item_owner=item_owner, item_row=item_row, staleness=staleness, w_proj=w_proj, w_out=w_out, out_grad=out_grad)


EPSILON = 1e-05

def rounded(value):
    return lax.optimization_barrier(value.astype(jnp.bfloat16))

def normalize(value):
    center = value - lax.optimization_barrier(jnp.mean(value, axis=-1, keepdims=True))
    inverse = lax.rsqrt(lax.optimization_barrier(jnp.mean(center * center, axis=-1, keepdims=True)) + EPSILON)
    return (center * inverse, inverse)

def norm_back(gradient, normed, inverse):
    return inverse * (gradient - lax.optimization_barrier(jnp.mean(gradient, axis=-1, keepdims=True)) - normed * lax.optimization_barrier(jnp.mean(gradient * normed, axis=-1, keepdims=True)))

def silu_slope(value):
    logistic = jax.nn.sigmoid(value)
    return logistic * (1.0 + value * (1.0 - logistic))

def causal(first_row, block_rows, length):
    query_pos = first_row + lax.broadcasted_iota(jnp.int32, (block_rows, length), 0)
    key_pos = lax.broadcasted_iota(jnp.int32, (block_rows, length), 1)
    return key_pos <= query_pos

def layer_parts(hidden, proj_weight, out_weight):
    length = hidden.shape[0]
    hidden_float = hidden.astype(jnp.float32)
    normed_float, inverse_hidden = normalize(hidden_float)
    normed = rounded(normed_float)
    pre_act = jnp.dot(normed, proj_weight, preferred_element_type=jnp.float32)
    projected = rounded(jax.nn.silu(pre_act))
    width = out_weight.shape[0]
    gating = projected[:, :width]
    values = projected[:, width:2 * width].reshape(length, HEADS, DH)
    queries = projected[:, 2 * width:3 * width].reshape(length, HEADS, DH)
    key_rows = projected[:, 3 * width:].reshape(length, HEADS, DH)
    score_scale = DH ** (-0.5)
    scores = jnp.einsum('qhd,khd->hqk', queries.astype(jnp.float32), key_rows.astype(jnp.float32)) * score_scale
    visible = causal(0, length, length)[None]
    attn = rounded(jnp.where(visible, jax.nn.silu(scores), 0.0))
    mixture = jnp.einsum('hqk,khd->qhd', attn.astype(jnp.float32), values.astype(jnp.float32)).reshape(length, width)
    mix_normed, inverse_mix = normalize(mixture)
    gated_out = rounded(mix_normed * gating.astype(jnp.float32))
    return dict(hidden_float=hidden_float, normed_float=normed_float, inverse_hidden=inverse_hidden, normed=normed, pre_act=pre_act, gating=gating, values=values, queries=queries, key_rows=key_rows, scores=scores, visible=visible, attn=attn, mix_normed=mix_normed, inverse_mix=inverse_mix, gated_out=gated_out)

def layer_forward(hidden, proj_weight, out_weight):
    parts = layer_parts(hidden, proj_weight, out_weight)
    return rounded(parts['hidden_float'] + jnp.dot(parts['gated_out'], out_weight, preferred_element_type=jnp.float32))

def layer_backward(hidden, grad_out, proj_weight, out_weight):
    parts = layer_parts(hidden, proj_weight, out_weight)
    length = hidden.shape[0]
    width = out_weight.shape[0]
    score_scale = DH ** (-0.5)
    grad_round = rounded(grad_out)
    gw_out = jnp.dot(parts['gated_out'].T, grad_round, preferred_element_type=jnp.float32)
    grad_gated = jnp.dot(grad_round, out_weight.T, preferred_element_type=jnp.float32)
    grad_gate = grad_gated * parts['mix_normed']
    grad_mixture = norm_back(grad_gated * parts['gating'].astype(jnp.float32), parts['mix_normed'], parts['inverse_mix'])
    grad_mix = rounded(grad_mixture).reshape(length, HEADS, DH).astype(jnp.float32)
    values = parts['values'].astype(jnp.float32)
    queries = parts['queries'].astype(jnp.float32)
    key_rows = parts['key_rows'].astype(jnp.float32)
    grad_attn = jnp.einsum('qhd,khd->hqk', grad_mix, values)
    grad_values = jnp.einsum('hqk,qhd->khd', parts['attn'].astype(jnp.float32), grad_mix)
    grad_scores = rounded(jnp.where(parts['visible'], grad_attn * silu_slope(parts['scores']), 0.0)).astype(jnp.float32)
    grad_queries = jnp.einsum('hqk,khd->qhd', grad_scores, key_rows) * score_scale
    grad_keys = jnp.einsum('hqk,qhd->khd', grad_scores, queries) * score_scale
    grad_proj = jnp.concatenate([grad_gate, grad_values.reshape(length, width), grad_queries.reshape(length, width), grad_keys.reshape(length, width)], axis=1)
    grad_pre = rounded(grad_proj * silu_slope(parts['pre_act']))
    gw_proj = jnp.dot(parts['normed'].T, grad_pre, preferred_element_type=jnp.float32)
    grad_normed = jnp.dot(grad_pre, proj_weight.T, preferred_element_type=jnp.float32)
    grad_in = grad_out + norm_back(grad_normed, parts['normed_float'], parts['inverse_hidden'])
    return (grad_in, gw_proj, gw_out)

def reference(item_table, item_owner, item_row, staleness, w_proj, w_out, out_grad):
    ids = (item_owner[:, :, 0] * ROWS_OWN + item_row).astype(jnp.int32)
    item_rows = item_table[ids].astype(jnp.bfloat16)

    def one_user(totals, pieces):
        hidden, grad_last = pieces
        inputs = [hidden]
        for layer_index in range(LAYERS - 1):
            inputs.append(layer_forward(inputs[-1], w_proj[layer_index], w_out[layer_index]))
        gradient = grad_last.astype(jnp.float32)
        proj_list = []
        out_list = []
        for layer_index in reversed(range(LAYERS)):
            gradient, gw_proj, gw_out = layer_backward(inputs[layer_index], gradient, w_proj[layer_index], w_out[layer_index])
            proj_list.insert(0, gw_proj)
            out_list.insert(0, gw_out)
        new_totals = (totals[0] + jnp.stack(proj_list), totals[1] + jnp.stack(out_list))
        return (new_totals, gradient)
    start_totals = (jnp.zeros(w_proj.shape, jnp.float32), jnp.zeros(w_out.shape, jnp.float32))
    (proj_total, out_total), row_grad = lax.scan(one_user, start_totals, (item_rows, out_grad))
    table_grad = jnp.zeros(item_table.shape, jnp.float32).at[ids.reshape(-1)].add(row_grad.reshape(-1, D))
    step_rate = 0.5 / (1.0 + staleness.astype(jnp.float32))
    new_table = item_table - step_rate[:, None] * table_grad
    norm_scale = (N_FSDP * N_EMB * SEQ) ** (-0.5)
    return (new_table, proj_total * norm_scale, out_total * norm_scale)
```

```python
import functools

import jax
import jax.numpy as jnp
from jax import lax
from jax.experimental import pallas as pl
from jax.experimental.pallas import tpu as pltpu
from jax.sharding import PartitionSpec as P

MESH = pl.DeviceIdType.MESH

DH = 64


EPSILON = 1e-05


def normalize(value):
    center = value - jnp.mean(value, axis=-1, keepdims=True)
    inverse = lax.rsqrt(jnp.mean(center * center, axis=-1, keepdims=True) + EPSILON)
    return (center * inverse, inverse)


def norm_back(gradient, normed, inverse):
    return inverse * (
        gradient
        - jnp.mean(gradient, axis=-1, keepdims=True)
        - normed * jnp.mean(gradient * normed, axis=-1, keepdims=True)
    )


def silu_slope(value):
    logistic = jax.nn.sigmoid(value)
    return logistic * (1.0 + value * (1.0 - logistic))


def causal(first_row, block_rows, length):
    query_pos = first_row + lax.broadcasted_iota(jnp.int32, (block_rows, length), 0)
    key_pos = lax.broadcasted_iota(jnp.int32, (block_rows, length), 1)
    return key_pos <= query_pos


def attend(queries, key_rows, values, block_rows, score_scale):
    length = queries.shape[0]
    results = []
    for block_index in range(length // block_rows):
        first_row = block_index * block_rows
        end_row = first_row + block_rows
        query_part = queries[first_row:end_row]
        scores = (
            jnp.einsum(
                "qhd,khd->hqk", query_part, key_rows[:end_row], preferred_element_type=jnp.float32
            )
            * score_scale
        )
        visible = causal(first_row, block_rows, end_row)[None]
        attn = jnp.where(visible, jax.nn.silu(scores), 0.0).astype(jnp.bfloat16)
        results.append(
            jnp.einsum("hqk,khd->qhd", attn, values[:end_row], preferred_element_type=jnp.float32)
        )
    mixture = jnp.concatenate(results, axis=0)
    return mixture.reshape(length, -1)


def attend_back(queries, key_rows, values, grad_mix, block_rows, score_scale):
    length = queries.shape[0]
    grad_keys = jnp.zeros(queries.shape, jnp.float32)
    grad_values = jnp.zeros(queries.shape, jnp.float32)
    query_grads = []
    for block_index in range(length // block_rows):
        first_row = block_index * block_rows
        end_row = first_row + block_rows
        query_part = queries[first_row:end_row]
        grad_part = grad_mix[first_row:end_row]
        key_part = key_rows[:end_row]
        value_part = values[:end_row]
        scores = (
            jnp.einsum("qhd,khd->hqk", query_part, key_part, preferred_element_type=jnp.float32)
            * score_scale
        )
        visible = causal(first_row, block_rows, end_row)[None]
        attn = jnp.where(visible, jax.nn.silu(scores), 0.0).astype(jnp.bfloat16)
        grad_attn = jnp.einsum(
            "qhd,khd->hqk", grad_part, value_part, preferred_element_type=jnp.float32
        )
        grad_values = grad_values.at[:end_row].add(
            jnp.einsum("hqk,qhd->khd", attn, grad_part, preferred_element_type=jnp.float32)
        )
        grad_scores = jnp.where(visible, grad_attn * silu_slope(scores), 0.0).astype(jnp.bfloat16)
        query_grads.append(
            jnp.einsum("hqk,khd->qhd", grad_scores, key_part, preferred_element_type=jnp.float32)
            * score_scale
        )
        grad_keys = grad_keys.at[:end_row].add(
            jnp.einsum("hqk,qhd->khd", grad_scores, query_part, preferred_element_type=jnp.float32)
            * score_scale
        )
    grad_queries = jnp.concatenate(query_grads, axis=0)
    return (
        grad_queries.reshape(length, -1),
        grad_keys.reshape(length, -1),
        grad_values.reshape(length, -1),
    )


def layer_parts(hidden, proj_weight, out_weight, block_rows):
    length = hidden.shape[0]
    width = out_weight.shape[0]
    head_count = width // DH
    hidden_float = hidden.astype(jnp.float32)
    normed_float, inverse_hidden = normalize(hidden_float)
    normed = normed_float.astype(jnp.bfloat16)
    pre_act = jnp.dot(normed, proj_weight, preferred_element_type=jnp.float32)
    projected = jax.nn.silu(pre_act).astype(jnp.bfloat16)
    gating = projected[:, :width]
    values = projected[:, width : 2 * width].reshape(length, head_count, DH)
    queries = projected[:, 2 * width : 3 * width].reshape(length, head_count, DH)
    key_rows = projected[:, 3 * width :].reshape(length, head_count, DH)
    mixture = attend(queries, key_rows, values, block_rows, DH ** (-0.5))
    mix_normed, inverse_mix = normalize(mixture)
    gated_out = (mix_normed * gating.astype(jnp.float32)).astype(jnp.bfloat16)
    return dict(
        hidden_float=hidden_float,
        normed_float=normed_float,
        inverse_hidden=inverse_hidden,
        normed=normed,
        pre_act=pre_act,
        gating=gating,
        values=values,
        queries=queries,
        key_rows=key_rows,
        mix_normed=mix_normed,
        inverse_mix=inverse_mix,
        gated_out=gated_out,
    )


def layer_forward(hidden, proj_weight, out_weight, block_rows):
    parts = layer_parts(hidden, proj_weight, out_weight, block_rows)
    branch = jnp.dot(parts["gated_out"], out_weight, preferred_element_type=jnp.float32)
    return ((parts["hidden_float"] + branch).astype(jnp.bfloat16), parts)


def layer_backward(hidden, grad_out, proj_weight, out_weight, block_rows, parts):
    if parts is None:
        parts = layer_parts(hidden, proj_weight, out_weight, block_rows)
    length = hidden.shape[0]
    width = out_weight.shape[0]
    grad_round = grad_out.astype(jnp.bfloat16)
    gw_out = jnp.dot(parts["gated_out"].T, grad_round, preferred_element_type=jnp.float32)
    grad_gated = jnp.dot(grad_round, out_weight.T, preferred_element_type=jnp.float32)
    grad_gate = grad_gated * parts["mix_normed"]
    grad_mixture = norm_back(
        grad_gated * parts["gating"].astype(jnp.float32), parts["mix_normed"], parts["inverse_mix"]
    )
    grad_mix = grad_mixture.astype(jnp.bfloat16).reshape(length, width // DH, DH)
    grad_queries, grad_keys, grad_values = attend_back(
        parts["queries"], parts["key_rows"], parts["values"], grad_mix, block_rows, DH ** (-0.5)
    )
    grad_proj = jnp.concatenate([grad_gate, grad_values, grad_queries, grad_keys], axis=1)
    grad_pre = (grad_proj * silu_slope(parts["pre_act"])).astype(jnp.bfloat16)
    gw_proj = jnp.dot(parts["normed"].T, grad_pre, preferred_element_type=jnp.float32)
    grad_normed = jnp.dot(grad_pre, proj_weight.T, preferred_element_type=jnp.float32)
    grad_in = grad_out + norm_back(grad_normed, parts["normed_float"], parts["inverse_hidden"])
    return (grad_in, gw_proj, gw_out)


def ask_owners(payload):
    return lax.all_to_all(payload, ("fsdp", "emb"), split_axis=0, concat_axis=0, tiled=True)


def return_rows(payload):
    return lax.all_to_all(payload, ("fsdp", "emb"), split_axis=0, concat_axis=0, tiled=True)


def device_of(index, emb_count):
    return (index // emb_count, lax.rem(index, emb_count))


def greet(me, owners, emb_count):
    barrier = pltpu.get_barrier_semaphore()

    def hello(step, carry):
        other = lax.rem(me + step, owners)
        pl.semaphore_signal(
            barrier, inc=1, device_id=device_of(other, emb_count), device_id_type=MESH
        )
        return carry

    lax.fori_loop(1, owners, hello, 0)
    return barrier


def collect_kernel(
    owners,
    emb_count,
    capacity,
    outgoing_ref,
    grads_ref,
    incoming_ref,
    total_ref,
    pair_in,
    pair_sum,
    z_in,
    z_sum,
    x_in,
    y_all,
    x_all,
    row_send,
    row_recv,
    own_sem,
    pair_sems,
    z_send,
    z_recv,
    x_send,
    x_recv,
    y_send,
    y_recv,
    g_send,
    g_recv,
):
    fsdp_at = lax.axis_index("fsdp")
    emb_at = lax.axis_index("emb")
    me = fsdp_at * emb_count + emb_at
    z_at = fsdp_at // 2
    core = lax.rem(fsdp_at, 2)
    y_at = emb_at // 4
    x_at = lax.rem(emb_at, 4)
    barrier = greet(me, owners, emb_count)
    pl.semaphore_wait(barrier, owners - 1)

    pair = pltpu.make_async_remote_copy(
        src_ref=grads_ref.at[1 - core],
        dst_ref=pair_in,
        send_sem=pair_sems.at[0],
        recv_sem=pair_sems.at[1],
        device_id=(z_at * 2 + 1 - core, emb_at),
        device_id_type=MESH,
    )
    pair.start()

    def send_rows(step, carry):
        other = lax.rem(me + step, owners)
        pltpu.make_async_remote_copy(
            src_ref=outgoing_ref.at[pl.ds(other * capacity, capacity)],
            dst_ref=incoming_ref.at[pl.ds(me * capacity, capacity)],
            send_sem=row_send,
            recv_sem=row_recv,
            device_id=device_of(other, emb_count),
            device_id_type=MESH,
        ).start()
        return carry

    lax.fori_loop(1, owners, send_rows, 0)
    own_rows = pl.ds(me * capacity, capacity)
    own = pltpu.make_async_copy(outgoing_ref.at[own_rows], incoming_ref.at[own_rows], own_sem)
    own.start()

    pair.wait()
    for z in range(4):
        for layer in range(2):
            pair_sum[z, layer] = (
                grads_ref[core, z, layer].astype(jnp.float32)
                + pair_in[z, layer].astype(jnp.float32)
            ).astype(jnp.bfloat16)
    z_copies = []
    for k in range(3):
        to = lax.rem(z_at + k + 1, 4)
        copy = pltpu.make_async_remote_copy(
            src_ref=pair_sum.at[to],
            dst_ref=z_in.at[k],
            send_sem=z_send.at[k],
            recv_sem=z_recv.at[k],
            device_id=(to * 2 + core, emb_at),
            device_id_type=MESH,
        )
        copy.start()
        z_copies.append(copy)
    for copy in z_copies:
        copy.wait()
    for part in range(4):
        rows = slice(part % 2 * 16, part % 2 * 16 + 16)
        value = pair_sum[z_at, part // 2, rows].astype(jnp.float32)
        for k in range(3):
            value += z_in[k, part // 2, rows].astype(jnp.float32)
        z_sum[part] = value.astype(jnp.bfloat16)

    x_copies = []
    for k in range(3):
        to = lax.rem(x_at + k + 1, 4)
        copy = pltpu.make_async_remote_copy(
            src_ref=z_sum.at[to],
            dst_ref=x_in.at[k],
            send_sem=x_send.at[k],
            recv_sem=x_recv.at[k],
            device_id=(fsdp_at, y_at * 4 + to),
            device_id_type=MESH,
        )
        copy.start()
        x_copies.append(copy)
    for copy in x_copies:
        copy.wait()
    value = z_sum[x_at].astype(jnp.float32)
    for k in range(3):
        value += x_in[k].astype(jnp.float32)
    y_all[y_at] = value.astype(jnp.bfloat16)

    y_copies = []
    for k in range(3):
        to = lax.rem(y_at + k + 1, 4)
        copy = pltpu.make_async_remote_copy(
            src_ref=y_all.at[y_at],
            dst_ref=y_all.at[y_at],
            send_sem=y_send.at[k],
            recv_sem=y_recv.at[k],
            device_id=(fsdp_at, to * 4 + x_at),
            device_id_type=MESH,
        )
        copy.start()
        y_copies.append(copy)
    for copy in y_copies:
        copy.wait()
    value = y_all[0].astype(jnp.float32)
    for y in range(1, 4):
        value += y_all[y].astype(jnp.float32)
    x_all[x_at] = value.astype(jnp.bfloat16)

    g_copies = []
    for k in range(3):
        to = lax.rem(x_at + k + 1, 4)
        copy = pltpu.make_async_remote_copy(
            src_ref=x_all.at[x_at],
            dst_ref=x_all.at[x_at],
            send_sem=g_send.at[k],
            recv_sem=g_recv.at[k],
            device_id=(fsdp_at, y_at * 4 + to),
            device_id_type=MESH,
        )
        copy.start()
        g_copies.append(copy)
    for copy in g_copies:
        copy.wait()
    for part in range(4):
        total_ref[part] = x_all[part]

    others = pl.ds(0, (owners - 1) * capacity)
    pltpu.make_async_copy(outgoing_ref.at[others], outgoing_ref.at[others], row_send).wait()
    pltpu.make_async_copy(incoming_ref.at[others], incoming_ref.at[others], row_recv).wait()
    own.wait()


def collect(outgoing, grads, owners, emb_count, capacity):
    columns = grads.shape[-1]
    depth = grads.shape[-2]
    bf16 = jnp.bfloat16
    vmem = pl.BlockSpec(memory_space=pltpu.VMEM)
    three = pltpu.SemaphoreType.DMA((3,))
    return pl.pallas_call(
        functools.partial(collect_kernel, owners, emb_count, capacity),
        out_shape=(
            jax.ShapeDtypeStruct(outgoing.shape, bf16),
            jax.ShapeDtypeStruct((4, 16, columns), bf16),
        ),
        in_specs=[vmem, vmem],
        out_specs=(vmem, vmem),
        scratch_shapes=[
            pltpu.VMEM((4, 2, depth, columns), bf16),
            pltpu.VMEM((4, 2, depth, columns), bf16),
            pltpu.VMEM((3, 2, depth, columns), bf16),
            pltpu.VMEM((4, 16, columns), bf16),
            pltpu.VMEM((3, 16, columns), bf16),
            pltpu.VMEM((4, 16, columns), bf16),
            pltpu.VMEM((4, 16, columns), bf16),
            pltpu.SemaphoreType.DMA,
            pltpu.SemaphoreType.DMA,
            pltpu.SemaphoreType.DMA,
            pltpu.SemaphoreType.DMA((2,)),
            three,
            three,
            three,
            three,
            three,
            three,
            three,
            three,
        ],
        compiler_params=pltpu.CompilerParams(
            collective_id=1, has_side_effects=True, vmem_limit_bytes=32 << 20
        ),
        name="collect",
    )(outgoing, grads)


def update_kernel(block, table_ref, requested_ref, stale_ref, incoming_ref, new_ref):
    count = requested_ref.shape[1]
    first = pl.program_id(0) * block
    row = first + lax.broadcasted_iota(jnp.int32, (block, count), 0)
    pick = (row == requested_ref[...]).astype(jnp.float32).astype(jnp.bfloat16)
    grad = jnp.dot(pick, incoming_ref[...], preferred_element_type=jnp.float32)
    rate = 0.5 / (1.0 + stale_ref[...].astype(jnp.float32))
    same = lax.broadcasted_iota(jnp.int32, (128, 128), 0) == lax.broadcasted_iota(
        jnp.int32, (128, 128), 1
    )
    for part in range(block // 128):
        rows = slice(part * 128, part * 128 + 128)
        spread = jnp.where(same, rate[0, part : part + 1, :], 0.0)
        column = jnp.sum(spread, axis=1, keepdims=True)
        new_ref[rows, :] = table_ref[rows, :] - column * grad[rows, :]


def update_table(table, requested, staleness, incoming):
    rows, width = table.shape
    block = 512
    count = incoming.shape[0]
    parts = block // 128
    return pl.pallas_call(
        functools.partial(update_kernel, block),
        out_shape=jax.ShapeDtypeStruct(table.shape, jnp.float32),
        grid=(rows // block,),
        in_specs=[
            pl.BlockSpec((block, width), lambda i: (i, 0)),
            pl.BlockSpec((1, count), lambda i: (0, 0)),
            pl.BlockSpec((1, parts, 128), lambda i: (i, 0, 0)),
            pl.BlockSpec((count, width), lambda i: (0, 0)),
        ],
        out_specs=pl.BlockSpec((block, width), lambda i: (i, 0)),
        compiler_params=pltpu.CompilerParams(vmem_limit_bytes=48 << 20),
        name="update_table",
    )(
        table,
        requested.reshape(1, count),
        staleness.reshape(rows // block, parts, 128),
        incoming,
    )


def local(item_table, item_owner, item_row, staleness, w_proj, w_out, out_grad):
    fsdp_count = lax.axis_size("fsdp")
    emb_count = lax.axis_size("emb")
    owners = fsdp_count * emb_count
    length = item_row.shape[1]
    capacity = 2 * length // owners
    width = item_table.shape[1]
    owner_of = item_owner[0, :, 0]
    offset = item_row[0]
    member = (owner_of[:, None] == jnp.arange(owners, dtype=jnp.int32)[None, :]).astype(jnp.int32)
    earlier = jnp.cumsum(member, axis=0) - member
    slot_index = jnp.sum(earlier * member, axis=1)
    target = owner_of * capacity + slot_index
    request = (
        jnp.full((owners * capacity,), -1, jnp.int32)
        .at[target]
        .set(offset)
        .reshape(owners, capacity)
    )
    requested = ask_owners(request)
    present = requested >= 0
    safe_rows = jnp.where(present, requested, 0)
    looked_up = jnp.where(present[:, :, None], item_table[safe_rows], 0.0).astype(jnp.bfloat16)
    returned = return_rows(looked_up)
    item_rows = returned.reshape(owners * capacity, width)[target]
    proj_all, out_all = (
        lax.all_gather(w_proj, "fsdp", axis=1, tiled=True),
        lax.all_gather(w_out, "fsdp", axis=1, tiled=True),
    )
    layer_count = w_proj.shape[0]
    block_rows = min(512, length)
    inputs = [item_rows]
    saved_parts = []
    layer_index = 0
    next_hidden, parts = layer_forward(
        inputs[-1], proj_all[layer_index], out_all[layer_index], block_rows
    )
    inputs.append(next_hidden)
    saved_parts.append(parts)
    saved_parts.append(None)
    gradient = out_grad[0].astype(jnp.float32)
    proj_list = []
    out_list = []
    for layer_index in reversed(range(layer_count)):
        gradient, gw_proj, gw_out = layer_backward(
            inputs[layer_index],
            gradient,
            proj_all[layer_index],
            out_all[layer_index],
            block_rows,
            saved_parts[layer_index],
        )
        proj_list.insert(0, gw_proj)
        out_list.insert(0, gw_out)
    proj_grads = jnp.stack(proj_list)
    out_grads = jnp.stack(out_list)
    outgoing = (
        jnp.zeros((owners * capacity, width), jnp.float32)
        .at[target]
        .set(gradient)
        .astype(jnp.bfloat16)
    )
    layer_count, depth = w_proj.shape[:2]
    grads = jnp.concatenate([proj_grads, out_grads], axis=2).astype(jnp.bfloat16)
    columns = grads.shape[-1]
    grads = grads.reshape(layer_count, fsdp_count // 2, 2, depth, columns).transpose(2, 1, 0, 3, 4)
    incoming, total = collect(outgoing, grads, owners, emb_count, capacity)
    new_table = update_table(item_table, requested, staleness, incoming)
    norm_scale = (owners * length) ** (-0.5)
    total = total.reshape(layer_count, depth, columns).astype(jnp.float32) * norm_scale
    split = w_proj.shape[-1]
    return (new_table, total[:, :, :split], total[:, :, split:])


def solution(mesh):
    return jax.shard_map(
        local,
        mesh=mesh,
        in_specs=(
            P(("fsdp", "emb"), None),
            P(("fsdp", "emb"), None, None),
            P(("fsdp", "emb"), None),
            P(("fsdp", "emb")),
            P(None, "fsdp", None),
            P(None, "fsdp", None),
            P(("fsdp", "emb"), None, None),
        ),
        out_specs=(P(("fsdp", "emb"), None), P(None, "fsdp", None), P(None, "fsdp", None)),
        check_vma=False,
    )
```

```python
import functools

import jax
import jax.numpy as jnp
from jax import lax
from jax.experimental import pallas as pl
from jax.experimental.pallas import tpu as pltpu
from jax.sharding import PartitionSpec as P

MESH = pl.DeviceIdType.MESH

DH = 64


EPSILON = 1e-05


NT = (((1,), (1,)), ((), ()))


def matmul(left, right):
    return jnp.dot(left, right, preferred_element_type=jnp.float32)


def matmul_nt(left, right):
    return lax.dot_general(left, right, NT, preferred_element_type=jnp.float32)


def to_column(row):
    same = lax.broadcasted_iota(jnp.int32, (128, 128), 0) == lax.broadcasted_iota(
        jnp.int32, (128, 128), 1
    )
    parts = [
        jnp.sum(jnp.where(same, row[:, at : at + 128], 0.0), axis=1, keepdims=True)
        for at in range(0, row.shape[1], 128)
    ]
    return parts[0] if len(parts) == 1 else jnp.concatenate(parts, axis=0)


def layers_kernel(
    target_ref,
    returned_ref,
    proj_ref,
    out_ref,
    cotangent_ref,
    outgoing_ref,
    grads_ref,
    hidden,
    hidden_inv,
    normed,
    slope,
    gate,
    queries,
    key_heads,
    value_heads,
    attn,
    score_slope,
    mix_normed,
    mix_inv,
    gated,
    gradient,
    mixture,
    grad_mix,
    grad_pre,
    grad_mix_t,
    normed_t,
    queries_t,
):
    f32, bf16 = jnp.float32, jnp.bfloat16
    block = 256
    length, width = cotangent_ref.shape
    blocks = length // block
    heads = width // DH
    slots = returned_ref.shape[0]
    layer_count = proj_ref.shape[0]
    head_of = lax.broadcasted_iota(jnp.int32, (heads, width), 1) // DH
    head_mask = (head_of == lax.broadcasted_iota(jnp.int32, (heads, width), 0)).astype(f32)
    head_mask = head_mask.astype(bf16)

    def rows(index):
        return pl.ds(pl.multiple_of(index * block, block), block)

    def head_rows(index):
        return pl.ds(pl.multiple_of(index * block * heads, block * heads), block * heads)

    def pair_of(query, key):
        return query * (query + 1) // 2 + key

    def fetch(index, carry):
        at = pl.multiple_of(index * 128, 128)
        column = to_column(target_ref[:, pl.ds(at, 128)].astype(f32))
        total = jnp.zeros((128, width), f32)
        for first in range(0, slots, 256):
            lane = lax.broadcasted_iota(jnp.int32, (128, 256), 1).astype(f32) + float(first)
            pick = (lane == column).astype(f32).astype(bf16)
            total += matmul(pick, returned_ref[first : first + 256, :])
        hidden[0, pl.ds(at, 128), :] = total.astype(bf16)
        return carry

    lax.fori_loop(0, length // 128, fetch, 0)

    def forward(layer, carry):
        def project(index, carry):
            at = rows(index)
            value = hidden[layer, at, :].astype(f32)
            center = value - jnp.mean(value, axis=1, keepdims=True)
            inverse = lax.rsqrt(jnp.mean(center * center, axis=1, keepdims=True) + EPSILON)
            norm = (center * inverse).astype(bf16)
            hidden_inv[layer, at, :] = inverse
            normed[layer, at, :] = norm
            for part in range(4):
                columns = slice(part * width, part * width + width)
                pre = matmul(norm, proj_ref[layer, :, columns])
                logistic = 0.5 + 0.5 * jnp.tanh(0.5 * pre)
                act = pre * logistic
                slope[layer, at, columns] = (logistic + act - act * logistic).astype(bf16)
                act = act.astype(bf16)
                if part == 0:
                    gate[layer, at, :] = act
                elif part == 2:
                    queries[layer, at, :] = act * jnp.asarray(0.0625, bf16)
                else:
                    store = value_heads if part == 1 else key_heads
                    for head in range(heads):
                        spot = pl.ds(
                            pl.multiple_of((index * heads + head) * block, block), block
                        )
                        store[layer, spot, :] = act * head_mask[head : head + 1, :]
            return carry

        lax.fori_loop(0, blocks, project, 0)

        def scores(query, key, masked):
            pair = pair_of(query, key)
            query_part = queries[layer, rows(query), :]
            if masked:
                visible = lax.broadcasted_iota(
                    jnp.int32, (block, block), 1
                ) <= lax.broadcasted_iota(jnp.int32, (block, block), 0)
            for head in range(heads):
                spot = pl.ds(pl.multiple_of((key * heads + head) * block, block), block)
                half = matmul_nt(query_part, key_heads[layer, spot, :])
                bend = jnp.tanh(half)
                lift = 1.0 + bend
                if masked:
                    lift = jnp.where(visible, lift, 0.0)
                columns = slice(head * block, head * block + block)
                attn[layer, pair, :, columns] = (half * lift).astype(bf16)
                score_slope[layer, pair, :, columns] = (
                    lift * (1.0 + (half - half * bend))
                ).astype(bf16)

        def attend_rows(query, carry):
            def before(key, carry):
                scores(query, key, False)
                return carry

            lax.fori_loop(0, query, before, 0)
            scores(query, query, True)
            mixture[...] = matmul(
                attn[layer, pair_of(query, query)], value_heads[layer, head_rows(query), :]
            )

            def gather_values(key, carry):
                mixture[...] += matmul(
                    attn[layer, pair_of(query, key)], value_heads[layer, head_rows(key), :]
                )
                return carry

            lax.fori_loop(0, query, gather_values, 0)
            at = rows(query)
            value = mixture[...]
            center = value - jnp.mean(value, axis=1, keepdims=True)
            inverse = lax.rsqrt(jnp.mean(center * center, axis=1, keepdims=True) + EPSILON)
            norm = center * inverse
            mix_normed[layer, at, :] = norm
            mix_inv[layer, at, :] = inverse
            gated_part = (norm * gate[layer, at, :].astype(f32)).astype(bf16)
            gated[layer, at, :] = gated_part

            @pl.when(layer < layer_count - 1)
            def _():
                branch = matmul(gated_part, out_ref[layer])
                hidden[layer + 1, at, :] = (hidden[layer, at, :].astype(f32) + branch).astype(bf16)

            return carry

        lax.fori_loop(0, blocks, attend_rows, 0)
        return carry

    lax.fori_loop(0, layer_count, forward, 0)

    gradient[...] = cotangent_ref[...].astype(f32)

    def backward(step, carry):
        layer = layer_count - 1 - step

        def through_gate(index, carry):
            at = rows(index)
            grad_round = gradient[at, :].astype(bf16)
            grad_gated = matmul_nt(grad_round, out_ref[layer])
            norm = mix_normed[layer, at, :]
            first = slope[layer, at, :width].astype(f32)
            grad_pre[at, :width] = (grad_gated * norm * first).astype(bf16)
            inner = grad_gated * gate[layer, at, :].astype(f32)
            grad = mix_inv[layer, at, :] * (
                inner
                - jnp.mean(inner, axis=1, keepdims=True)
                - norm * jnp.mean(inner * norm, axis=1, keepdims=True)
            )
            grad_mix[at, :] = grad.astype(bf16)
            grad_mix_t[:, at] = grad.T.astype(bf16)
            normed_t[:, at] = normed[layer, at, :].T
            queries_t[:, at] = queries[layer, at, :].T
            return carry

        lax.fori_loop(0, blocks, through_gate, 0)

        gw_out = lax.dot_general(
            gated[layer],
            gradient[...].astype(bf16),
            (((0,), (0,)), ((), ())),
            preferred_element_type=jnp.float32,
        ).astype(bf16)
        depth = grads_ref.shape[3]
        for part in range(8):
            grads_ref[part % 2, part // 2, layer, :, 4 * width :] = gw_out[
                part * depth : part * depth + depth
            ]

        def through_scores(query, carry):
            def one(key, carry):
                pair = pair_of(query, key)
                grad_part = grad_mix[rows(query), :]
                for head in range(heads):
                    spot = pl.ds(pl.multiple_of((key * heads + head) * block, block), block)
                    columns = slice(head * block, head * block + block)
                    grad = matmul_nt(grad_part, value_heads[layer, spot, :])
                    score_slope[layer, pair, :, columns] = (
                        grad * score_slope[layer, pair, :, columns].astype(f32)
                    ).astype(bf16)
                return carry

            lax.fori_loop(0, query + 1, one, 0)
            mixture[...] = jnp.zeros_like(mixture)

            def gather_keys(key, carry):
                mixture[...] += matmul(
                    score_slope[layer, pair_of(query, key)], key_heads[layer, head_rows(key), :]
                )
                return carry

            lax.fori_loop(0, query + 1, gather_keys, 0)
            at = rows(query)
            third = slope[layer, at, 2 * width : 3 * width].astype(f32)
            grad_pre[at, 2 * width : 3 * width] = (mixture[...] * 0.0625 * third).astype(bf16)
            return carry

        lax.fori_loop(0, blocks, through_scores, 0)

        def through_keys(key, carry):
            at = rows(key)
            for which in range(2):
                left = (grad_mix_t, queries_t)[which]
                right = (attn, score_slope)[which]
                for head in range(heads):
                    columns = slice(head * block, head * block + block)
                    lines = slice(head * DH, head * DH + DH)

                    def add(query, total):
                        return total + matmul(
                            left[lines, rows(query)],
                            right[layer, pair_of(query, key), :, columns],
                        )

                    total = lax.fori_loop(key, blocks, add, jnp.zeros((DH, block), f32))
                    mixture[lines, :] = total
                part = (1, 3)[which]
                span = slice(part * width, part * width + width)
                grad_pre[at, span] = (mixture[...].T * slope[layer, at, span].astype(f32)).astype(
                    bf16
                )
            return carry

        lax.fori_loop(0, blocks, through_keys, 0)

        for part in range(4):
            span = slice(part * width, part * width + width)
            gw_proj = matmul(normed_t[...], grad_pre[:, span]).astype(bf16)
            for piece in range(8):
                grads_ref[piece % 2, piece // 2, layer, :, span] = gw_proj[
                    piece * depth : piece * depth + depth
                ]

        def through_norm(index, carry):
            at = rows(index)
            grad_normed = matmul_nt(grad_pre[at, :], proj_ref[layer])
            norm = normed[layer, at, :].astype(f32)
            gradient[at, :] = gradient[at, :] + hidden_inv[layer, at, :] * (
                grad_normed
                - jnp.mean(grad_normed, axis=1, keepdims=True)
                - norm * jnp.mean(grad_normed * norm, axis=1, keepdims=True)
            )
            return carry

        lax.fori_loop(0, blocks, through_norm, 0)
        return carry

    lax.fori_loop(0, layer_count, backward, 0)

    def give_back(index, carry):
        at = pl.ds(pl.multiple_of(index * 128, 128), 128)
        total = jnp.zeros((128, width), f32)
        for first in range(0, length, 256):
            spot = lax.broadcasted_iota(jnp.int32, (128, 256), 0) + index * 128
            pick = (spot == target_ref[:, first : first + 256]).astype(f32).astype(bf16)
            total += matmul(pick, gradient[first : first + 256, :].astype(bf16))
        outgoing_ref[at, :] = total.astype(bf16)
        return carry

    lax.fori_loop(0, slots // 128, give_back, 0)


def run_layers(target, returned, proj_all, out_all, cotangent, depth):
    layer_count, width, columns = proj_all.shape
    length = cotangent.shape[0]
    blocks = length // 256
    pairs = blocks * (blocks + 1) // 2
    heads = width // DH
    f32, bf16 = jnp.float32, jnp.bfloat16
    vmem = pl.BlockSpec(memory_space=pltpu.VMEM)
    return pl.pallas_call(
        layers_kernel,
        out_shape=(
            jax.ShapeDtypeStruct(returned.shape, bf16),
            jax.ShapeDtypeStruct((2, 4, layer_count, depth, columns + width), bf16),
        ),
        in_specs=[vmem] * 5,
        out_specs=(vmem, vmem),
        scratch_shapes=[
            pltpu.VMEM((layer_count, length, width), bf16),
            pltpu.VMEM((layer_count, length, 1), f32),
            pltpu.VMEM((layer_count, length, width), bf16),
            pltpu.VMEM((layer_count, length, columns), bf16),
            pltpu.VMEM((layer_count, length, width), bf16),
            pltpu.VMEM((layer_count, length, width), bf16),
            pltpu.VMEM((layer_count, length * heads, width), bf16),
            pltpu.VMEM((layer_count, length * heads, width), bf16),
            pltpu.VMEM((layer_count, pairs, 256, 256 * heads), bf16),
            pltpu.VMEM((layer_count, pairs, 256, 256 * heads), bf16),
            pltpu.VMEM((layer_count, length, width), f32),
            pltpu.VMEM((layer_count, length, 1), f32),
            pltpu.VMEM((layer_count, length, width), bf16),
            pltpu.VMEM((length, width), f32),
            pltpu.VMEM((256, width), f32),
            pltpu.VMEM((length, width), bf16),
            pltpu.VMEM((length, columns), bf16),
            pltpu.VMEM((width, length), bf16),
            pltpu.VMEM((width, length), bf16),
            pltpu.VMEM((width, length), bf16),
        ],
        compiler_params=pltpu.CompilerParams(vmem_limit_bytes=60 << 20),
        name="layers",
    )(target, returned, proj_all, out_all, cotangent)


def ask_owners(payload):
    return lax.all_to_all(payload, ("fsdp", "emb"), split_axis=0, concat_axis=0, tiled=True)


def return_rows(payload):
    return lax.all_to_all(payload, ("fsdp", "emb"), split_axis=0, concat_axis=0, tiled=True)


def device_of(index, emb_count):
    return (index // emb_count, lax.rem(index, emb_count))


def greet(me, owners, emb_count):
    barrier = pltpu.get_barrier_semaphore()

    def hello(step, carry):
        other = lax.rem(me + step, owners)
        pl.semaphore_signal(
            barrier, inc=1, device_id=device_of(other, emb_count), device_id_type=MESH
        )
        return carry

    lax.fori_loop(1, owners, hello, 0)
    return barrier


def collect_kernel(
    owners,
    emb_count,
    capacity,
    outgoing_ref,
    grads_ref,
    incoming_ref,
    total_ref,
    pair_in,
    pair_sum,
    z_in,
    z_sum,
    x_in,
    y_all,
    x_all,
    row_send,
    row_recv,
    own_sem,
    pair_sems,
    z_send,
    z_recv,
    x_send,
    x_recv,
    y_send,
    y_recv,
    g_send,
    g_recv,
):
    fsdp_at = lax.axis_index("fsdp")
    emb_at = lax.axis_index("emb")
    me = fsdp_at * emb_count + emb_at
    z_at = fsdp_at // 2
    core = lax.rem(fsdp_at, 2)
    y_at = emb_at // 4
    x_at = lax.rem(emb_at, 4)
    barrier = greet(me, owners, emb_count)
    pl.semaphore_wait(barrier, owners - 1)

    pair = pltpu.make_async_remote_copy(
        src_ref=grads_ref.at[1 - core],
        dst_ref=pair_in,
        send_sem=pair_sems.at[0],
        recv_sem=pair_sems.at[1],
        device_id=(z_at * 2 + 1 - core, emb_at),
        device_id_type=MESH,
    )
    pair.start()

    def send_rows(step, carry):
        other = lax.rem(me + step, owners)
        pltpu.make_async_remote_copy(
            src_ref=outgoing_ref.at[pl.ds(other * capacity, capacity)],
            dst_ref=incoming_ref.at[pl.ds(me * capacity, capacity)],
            send_sem=row_send,
            recv_sem=row_recv,
            device_id=device_of(other, emb_count),
            device_id_type=MESH,
        ).start()
        return carry

    lax.fori_loop(1, owners, send_rows, 0)
    own_rows = pl.ds(me * capacity, capacity)
    own = pltpu.make_async_copy(outgoing_ref.at[own_rows], incoming_ref.at[own_rows], own_sem)
    own.start()

    pair.wait()
    for z in range(4):
        for layer in range(2):
            pair_sum[z, layer] = (
                grads_ref[core, z, layer].astype(jnp.float32)
                + pair_in[z, layer].astype(jnp.float32)
            ).astype(jnp.bfloat16)
    z_copies = []
    for k in range(3):
        to = lax.rem(z_at + k + 1, 4)
        copy = pltpu.make_async_remote_copy(
            src_ref=pair_sum.at[to],
            dst_ref=z_in.at[k],
            send_sem=z_send.at[k],
            recv_sem=z_recv.at[k],
            device_id=(to * 2 + core, emb_at),
            device_id_type=MESH,
        )
        copy.start()
        z_copies.append(copy)
    for copy in z_copies:
        copy.wait()
    for part in range(4):
        rows = slice(part % 2 * 16, part % 2 * 16 + 16)
        value = pair_sum[z_at, part // 2, rows].astype(jnp.float32)
        for k in range(3):
            value += z_in[k, part // 2, rows].astype(jnp.float32)
        z_sum[part] = value.astype(jnp.bfloat16)

    x_copies = []
    for k in range(3):
        to = lax.rem(x_at + k + 1, 4)
        copy = pltpu.make_async_remote_copy(
            src_ref=z_sum.at[to],
            dst_ref=x_in.at[k],
            send_sem=x_send.at[k],
            recv_sem=x_recv.at[k],
            device_id=(fsdp_at, y_at * 4 + to),
            device_id_type=MESH,
        )
        copy.start()
        x_copies.append(copy)
    for copy in x_copies:
        copy.wait()
    value = z_sum[x_at].astype(jnp.float32)
    for k in range(3):
        value += x_in[k].astype(jnp.float32)
    y_all[y_at] = value.astype(jnp.bfloat16)

    y_copies = []
    for k in range(3):
        to = lax.rem(y_at + k + 1, 4)
        copy = pltpu.make_async_remote_copy(
            src_ref=y_all.at[y_at],
            dst_ref=y_all.at[y_at],
            send_sem=y_send.at[k],
            recv_sem=y_recv.at[k],
            device_id=(fsdp_at, to * 4 + x_at),
            device_id_type=MESH,
        )
        copy.start()
        y_copies.append(copy)
    for copy in y_copies:
        copy.wait()
    value = y_all[0].astype(jnp.float32)
    for y in range(1, 4):
        value += y_all[y].astype(jnp.float32)
    x_all[x_at] = value.astype(jnp.bfloat16)

    g_copies = []
    for k in range(3):
        to = lax.rem(x_at + k + 1, 4)
        copy = pltpu.make_async_remote_copy(
            src_ref=x_all.at[x_at],
            dst_ref=x_all.at[x_at],
            send_sem=g_send.at[k],
            recv_sem=g_recv.at[k],
            device_id=(fsdp_at, y_at * 4 + to),
            device_id_type=MESH,
        )
        copy.start()
        g_copies.append(copy)
    for copy in g_copies:
        copy.wait()
    for part in range(4):
        total_ref[part] = x_all[part]

    others = pl.ds(0, (owners - 1) * capacity)
    pltpu.make_async_copy(outgoing_ref.at[others], outgoing_ref.at[others], row_send).wait()
    pltpu.make_async_copy(incoming_ref.at[others], incoming_ref.at[others], row_recv).wait()
    own.wait()


def collect(outgoing, grads, owners, emb_count, capacity):
    columns = grads.shape[-1]
    depth = grads.shape[-2]
    bf16 = jnp.bfloat16
    vmem = pl.BlockSpec(memory_space=pltpu.VMEM)
    three = pltpu.SemaphoreType.DMA((3,))
    return pl.pallas_call(
        functools.partial(collect_kernel, owners, emb_count, capacity),
        out_shape=(
            jax.ShapeDtypeStruct(outgoing.shape, bf16),
            jax.ShapeDtypeStruct((4, 16, columns), bf16),
        ),
        in_specs=[vmem, vmem],
        out_specs=(vmem, vmem),
        scratch_shapes=[
            pltpu.VMEM((4, 2, depth, columns), bf16),
            pltpu.VMEM((4, 2, depth, columns), bf16),
            pltpu.VMEM((3, 2, depth, columns), bf16),
            pltpu.VMEM((4, 16, columns), bf16),
            pltpu.VMEM((3, 16, columns), bf16),
            pltpu.VMEM((4, 16, columns), bf16),
            pltpu.VMEM((4, 16, columns), bf16),
            pltpu.SemaphoreType.DMA,
            pltpu.SemaphoreType.DMA,
            pltpu.SemaphoreType.DMA,
            pltpu.SemaphoreType.DMA((2,)),
            three,
            three,
            three,
            three,
            three,
            three,
            three,
            three,
        ],
        compiler_params=pltpu.CompilerParams(
            collective_id=1, has_side_effects=True, vmem_limit_bytes=32 << 20
        ),
        name="collect",
    )(outgoing, grads)


def update_kernel(block, table_ref, requested_ref, stale_ref, incoming_ref, new_ref):
    count = requested_ref.shape[1]
    first = pl.program_id(0) * block
    row = first + lax.broadcasted_iota(jnp.int32, (block, count), 0)
    pick = (row == requested_ref[...]).astype(jnp.float32).astype(jnp.bfloat16)
    grad = jnp.dot(pick, incoming_ref[...], preferred_element_type=jnp.float32)
    rate = 0.5 / (1.0 + stale_ref[...].astype(jnp.float32))
    same = lax.broadcasted_iota(jnp.int32, (128, 128), 0) == lax.broadcasted_iota(
        jnp.int32, (128, 128), 1
    )
    for part in range(block // 128):
        rows = slice(part * 128, part * 128 + 128)
        spread = jnp.where(same, rate[0, part : part + 1, :], 0.0)
        column = jnp.sum(spread, axis=1, keepdims=True)
        new_ref[rows, :] = table_ref[rows, :] - column * grad[rows, :]


def update_table(table, requested, staleness, incoming):
    rows, width = table.shape
    block = 512
    count = incoming.shape[0]
    parts = block // 128
    return pl.pallas_call(
        functools.partial(update_kernel, block),
        out_shape=jax.ShapeDtypeStruct(table.shape, jnp.float32),
        grid=(rows // block,),
        in_specs=[
            pl.BlockSpec((block, width), lambda i: (i, 0)),
            pl.BlockSpec((1, count), lambda i: (0, 0)),
            pl.BlockSpec((1, parts, 128), lambda i: (i, 0, 0)),
            pl.BlockSpec((count, width), lambda i: (0, 0)),
        ],
        out_specs=pl.BlockSpec((block, width), lambda i: (i, 0)),
        compiler_params=pltpu.CompilerParams(vmem_limit_bytes=48 << 20),
        name="update_table",
    )(
        table,
        requested.reshape(1, count),
        staleness.reshape(rows // block, parts, 128),
        incoming,
    )


def local(item_table, item_owner, item_row, staleness, w_proj, w_out, out_grad):
    fsdp_count = lax.axis_size("fsdp")
    emb_count = lax.axis_size("emb")
    owners = fsdp_count * emb_count
    length = item_row.shape[1]
    capacity = 2 * length // owners
    width = item_table.shape[1]
    owner_of = item_owner[0, :, 0]
    offset = item_row[0]
    member = (owner_of[:, None] == jnp.arange(owners, dtype=jnp.int32)[None, :]).astype(jnp.int32)
    earlier = jnp.cumsum(member, axis=0) - member
    slot_index = jnp.sum(earlier * member, axis=1)
    target = owner_of * capacity + slot_index
    request = (
        jnp.full((owners * capacity,), -1, jnp.int32)
        .at[target]
        .set(offset)
        .reshape(owners, capacity)
    )
    requested = ask_owners(request)
    present = requested >= 0
    safe_rows = jnp.where(present, requested, 0)
    looked_up = jnp.where(present[:, :, None], item_table[safe_rows], 0.0).astype(jnp.bfloat16)
    returned = return_rows(looked_up)
    proj_all, out_all = (
        lax.all_gather(w_proj, "fsdp", axis=1, tiled=True),
        lax.all_gather(w_out, "fsdp", axis=1, tiled=True),
    )
    layer_count, depth = w_proj.shape[:2]
    outgoing, grads = run_layers(
        target.reshape(1, length),
        returned.reshape(owners * capacity, width),
        proj_all,
        out_all,
        out_grad[0],
        depth,
    )
    columns = grads.shape[-1]
    incoming, total = collect(outgoing, grads, owners, emb_count, capacity)
    new_table = update_table(item_table, requested, staleness, incoming)
    norm_scale = (owners * length) ** (-0.5)
    total = total.reshape(layer_count, depth, columns).astype(jnp.float32) * norm_scale
    split = w_proj.shape[-1]
    return (new_table, total[:, :, :split], total[:, :, split:])


def solution(mesh):
    return jax.shard_map(
        local,
        mesh=mesh,
        in_specs=(
            P(("fsdp", "emb"), None),
            P(("fsdp", "emb"), None, None),
            P(("fsdp", "emb"), None),
            P(("fsdp", "emb")),
            P(None, "fsdp", None),
            P(None, "fsdp", None),
            P(("fsdp", "emb"), None, None),
        ),
        out_specs=(P(("fsdp", "emb"), None), P(None, "fsdp", None), P(None, "fsdp", None)),
        check_vma=False,
    )
```

```python
import functools

import jax
import jax.numpy as jnp
from jax import lax
from jax.experimental import pallas as pl
from jax.experimental.pallas import tpu as pltpu
from jax.sharding import PartitionSpec as P

MESH = pl.DeviceIdType.MESH

DH = 64


EPSILON = 1e-05


NT = (((1,), (1,)), ((), ()))


def matmul(left, right):
    return jnp.dot(left, right, preferred_element_type=jnp.float32)


def matmul_nt(left, right):
    return lax.dot_general(left, right, NT, preferred_element_type=jnp.float32)


def to_column(row):
    same = lax.broadcasted_iota(jnp.int32, (128, 128), 0) == lax.broadcasted_iota(
        jnp.int32, (128, 128), 1
    )
    parts = [
        jnp.sum(jnp.where(same, row[:, at : at + 128], 0.0), axis=1, keepdims=True)
        for at in range(0, row.shape[1], 128)
    ]
    return parts[0] if len(parts) == 1 else jnp.concatenate(parts, axis=0)


def layers_kernel(
    target_ref,
    returned_ref,
    weights_ref,
    cotangent_ref,
    outgoing_ref,
    grads_ref,
    hidden,
    hidden_inv,
    normed,
    slope,
    gate,
    queries,
    key_heads,
    value_heads,
    attn,
    score_slope,
    mix_normed,
    mix_inv,
    gated,
    gradient,
    mixture,
    grad_mix,
    grad_pre,
    grad_mix_t,
    normed_t,
    queries_t,
    keys_t,
    values_t,
):
    f32, bf16 = jnp.float32, jnp.bfloat16
    block = 256
    length, width = cotangent_ref.shape
    blocks = length // block
    heads = width // DH
    slots = returned_ref.shape[0]
    layer_count = weights_ref.shape[0]
    head_of = lax.broadcasted_iota(jnp.int32, (heads, width), 1) // DH
    head_mask = (head_of == lax.broadcasted_iota(jnp.int32, (heads, width), 0)).astype(f32)
    head_mask = head_mask.astype(bf16)

    def rows(index):
        return pl.ds(pl.multiple_of(index * block, block), block)

    def head_rows(index):
        return pl.ds(pl.multiple_of(index * block * heads, block * heads), block * heads)

    def pair_of(query, key):
        return query * (query + 1) // 2 + key

    def fetch(index, carry):
        at = pl.multiple_of(index * 128, 128)
        column = to_column(target_ref[:, pl.ds(at, 128)].astype(f32))
        total = jnp.zeros((128, width), f32)
        for first in range(0, slots, 256):
            lane = lax.broadcasted_iota(jnp.int32, (128, 256), 1).astype(f32) + float(first)
            pick = (lane == column).astype(f32).astype(bf16)
            total += matmul(pick, returned_ref[first : first + 256, :])
        hidden[0, pl.ds(at, 128), :] = total.astype(bf16)
        return carry

    lax.fori_loop(0, length // 128, fetch, 0)

    def forward(layer, carry):
        def project(index, carry):
            at = rows(index)
            value = hidden[layer, at, :].astype(f32)
            center = value - jnp.mean(value, axis=1, keepdims=True)
            inverse = lax.rsqrt(jnp.mean(center * center, axis=1, keepdims=True) + EPSILON)
            norm = (center * inverse).astype(bf16)
            hidden_inv[layer, at, :] = inverse
            normed[layer, at, :] = norm
            for part in range(4):
                columns = slice(part * width, part * width + width)
                pre = matmul(norm, weights_ref[layer, :, columns])
                logistic = 0.5 + 0.5 * jnp.tanh(0.5 * pre)
                act = pre * logistic
                slope[layer, at, columns] = (logistic + act - act * logistic).astype(bf16)
                act = act.astype(bf16)
                if part == 0:
                    gate[layer, at, :] = act
                elif part == 2:
                    queries[layer, at, :] = act * jnp.asarray(0.0625, bf16)
                else:
                    store = value_heads if part == 1 else key_heads
                    for head in range(heads):
                        spot = pl.ds(
                            pl.multiple_of((index * heads + head) * block, block), block
                        )
                        store[layer, spot, :] = act * head_mask[head : head + 1, :]
            return carry

        lax.fori_loop(0, blocks, project, 0)

        def scores(query, key, masked):
            pair = pair_of(query, key)
            query_part = queries[layer, rows(query), :]
            if masked:
                visible = lax.broadcasted_iota(
                    jnp.int32, (block, block), 1
                ) <= lax.broadcasted_iota(jnp.int32, (block, block), 0)
            parts = []
            for head in range(heads):
                spot = pl.ds(pl.multiple_of((key * heads + head) * block, block), block)
                half = matmul_nt(query_part, key_heads[layer, spot, :])
                bend = jnp.tanh(half)
                lift = 1.0 + bend
                if masked:
                    lift = jnp.where(visible, lift, 0.0)
                columns = slice(head * block, head * block + block)
                part = (half * lift).astype(bf16)
                parts.append(part)
                attn[layer, pair, :, columns] = part
                score_slope[layer, pair, :, columns] = (
                    lift * (1.0 + (half - half * bend))
                ).astype(bf16)
            return matmul(
                jnp.concatenate(parts, axis=1), value_heads[layer, head_rows(key), :]
            )

        def attend_rows(query, carry):
            mixture[...] = scores(query, query, True)

            def before(key, carry):
                mixture[...] += scores(query, key, False)
                return carry

            lax.fori_loop(0, query, before, 0)
            at = rows(query)
            value = mixture[...]
            center = value - jnp.mean(value, axis=1, keepdims=True)
            inverse = lax.rsqrt(jnp.mean(center * center, axis=1, keepdims=True) + EPSILON)
            norm = center * inverse
            mix_normed[layer, at, :] = norm
            mix_inv[layer, at, :] = inverse
            gated_part = (norm * gate[layer, at, :].astype(f32)).astype(bf16)
            gated[layer, at, :] = gated_part

            @pl.when(layer < layer_count - 1)
            def _():
                branch = matmul(gated_part, weights_ref[layer, :, 4 * width :])
                hidden[layer + 1, at, :] = (hidden[layer, at, :].astype(f32) + branch).astype(bf16)

            return carry

        lax.fori_loop(0, blocks, attend_rows, 0)
        return carry

    lax.fori_loop(0, layer_count, forward, 0)

    gradient[...] = cotangent_ref[...].astype(f32)

    def backward(step, carry):
        layer = layer_count - 1 - step

        def through_gate(index, carry):
            at = rows(index)
            grad_round = gradient[at, :].astype(bf16)
            grad_gated = matmul_nt(grad_round, weights_ref[layer, :, 4 * width :])
            norm = mix_normed[layer, at, :]
            first = slope[layer, at, :width].astype(f32)
            grad_pre[at, :width] = (grad_gated * norm * first).astype(bf16)
            inner = grad_gated * gate[layer, at, :].astype(f32)
            grad = mix_inv[layer, at, :] * (
                inner
                - jnp.mean(inner, axis=1, keepdims=True)
                - norm * jnp.mean(inner * norm, axis=1, keepdims=True)
            )
            grad_mix[at, :] = grad.astype(bf16)
            grad_mix_t[:, at] = grad.T.astype(bf16)
            normed_t[:, at] = normed[layer, at, :].T
            queries_t[:, at] = queries[layer, at, :].T
            return carry

        lax.fori_loop(0, blocks, through_gate, 0)

        gw_out = lax.dot_general(
            gated[layer],
            gradient[...].astype(bf16),
            (((0,), (0,)), ((), ())),
            preferred_element_type=jnp.float32,
        ).astype(bf16)
        depth = grads_ref.shape[3]
        for part in range(8):
            grads_ref[part % 2, part // 2, layer, :, 4 * width :] = gw_out[
                part * depth : part * depth + depth
            ]

        keys_t[...] = jnp.zeros_like(keys_t)
        values_t[...] = jnp.zeros_like(values_t)

        def through_scores(query, carry):
            mixture[...] = jnp.zeros_like(mixture)

            def one(key, carry):
                pair = pair_of(query, key)
                here = rows(query)
                there = rows(key)
                grad_part = grad_mix[here, :]
                parts = []
                for head in range(heads):
                    spot = pl.ds(pl.multiple_of((key * heads + head) * block, block), block)
                    columns = slice(head * block, head * block + block)
                    lines = slice(head * DH, head * DH + DH)
                    grad = matmul_nt(grad_part, value_heads[layer, spot, :])
                    values_t[lines, there] += matmul(
                        grad_mix_t[lines, here], attn[layer, pair, :, columns]
                    )
                    part = (grad * score_slope[layer, pair, :, columns].astype(f32)).astype(bf16)
                    parts.append(part)
                    keys_t[lines, there] += matmul(queries_t[lines, here], part)
                mixture[...] += matmul(
                    jnp.concatenate(parts, axis=1), key_heads[layer, head_rows(key), :]
                )
                return carry

            lax.fori_loop(0, query + 1, one, 0)
            at = rows(query)
            third = slope[layer, at, 2 * width : 3 * width].astype(f32)
            grad_pre[at, 2 * width : 3 * width] = (mixture[...] * 0.0625 * third).astype(bf16)
            return carry

        lax.fori_loop(0, blocks, through_scores, 0)

        def through_keys(key, carry):
            at = rows(key)
            for part, total in ((1, values_t), (3, keys_t)):
                span = slice(part * width, part * width + width)
                grad_pre[at, span] = (total[:, at].T * slope[layer, at, span].astype(f32)).astype(
                    bf16
                )
            return carry

        lax.fori_loop(0, blocks, through_keys, 0)

        for part in range(4):
            span = slice(part * width, part * width + width)
            gw_proj = matmul(normed_t[...], grad_pre[:, span]).astype(bf16)
            for piece in range(8):
                grads_ref[piece % 2, piece // 2, layer, :, span] = gw_proj[
                    piece * depth : piece * depth + depth
                ]

        def through_norm(index, carry):
            at = rows(index)
            grad_normed = matmul_nt(grad_pre[at, :], weights_ref[layer, :, : 4 * width])
            norm = normed[layer, at, :].astype(f32)
            gradient[at, :] = gradient[at, :] + hidden_inv[layer, at, :] * (
                grad_normed
                - jnp.mean(grad_normed, axis=1, keepdims=True)
                - norm * jnp.mean(grad_normed * norm, axis=1, keepdims=True)
            )
            return carry

        lax.fori_loop(0, blocks, through_norm, 0)
        return carry

    lax.fori_loop(0, layer_count, backward, 0)

    def give_back(index, carry):
        at = pl.ds(pl.multiple_of(index * 128, 128), 128)
        total = jnp.zeros((128, width), f32)
        for first in range(0, length, 256):
            spot = lax.broadcasted_iota(jnp.int32, (128, 256), 0) + index * 128
            pick = (spot == target_ref[:, first : first + 256]).astype(f32).astype(bf16)
            total += matmul(pick, gradient[first : first + 256, :].astype(bf16))
        outgoing_ref[at, :] = total.astype(bf16)
        return carry

    lax.fori_loop(0, slots // 128, give_back, 0)


def run_layers(target, returned, weights, cotangent, depth):
    layer_count, width, columns = weights.shape
    columns -= width
    length = cotangent.shape[0]
    blocks = length // 256
    pairs = blocks * (blocks + 1) // 2
    heads = width // DH
    f32, bf16 = jnp.float32, jnp.bfloat16
    vmem = pl.BlockSpec(memory_space=pltpu.VMEM)
    return pl.pallas_call(
        layers_kernel,
        out_shape=(
            jax.ShapeDtypeStruct(returned.shape, bf16),
            jax.ShapeDtypeStruct((2, 4, layer_count, depth, columns + width), bf16),
        ),
        in_specs=[vmem] * 4,
        out_specs=(vmem, vmem),
        scratch_shapes=[
            pltpu.VMEM((layer_count, length, width), bf16),
            pltpu.VMEM((layer_count, length, 1), f32),
            pltpu.VMEM((layer_count, length, width), bf16),
            pltpu.VMEM((layer_count, length, columns), bf16),
            pltpu.VMEM((layer_count, length, width), bf16),
            pltpu.VMEM((layer_count, length, width), bf16),
            pltpu.VMEM((layer_count, length * heads, width), bf16),
            pltpu.VMEM((layer_count, length * heads, width), bf16),
            pltpu.VMEM((layer_count, pairs, 256, 256 * heads), bf16),
            pltpu.VMEM((layer_count, pairs, 256, 256 * heads), bf16),
            pltpu.VMEM((layer_count, length, width), f32),
            pltpu.VMEM((layer_count, length, 1), f32),
            pltpu.VMEM((layer_count, length, width), bf16),
            pltpu.VMEM((length, width), f32),
            pltpu.VMEM((256, width), f32),
            pltpu.VMEM((length, width), bf16),
            pltpu.VMEM((length, columns), bf16),
            pltpu.VMEM((width, length), bf16),
            pltpu.VMEM((width, length), bf16),
            pltpu.VMEM((width, length), bf16),
            pltpu.VMEM((width, length), f32),
            pltpu.VMEM((width, length), f32),
        ],
        compiler_params=pltpu.CompilerParams(vmem_limit_bytes=60 << 20),
        name="layers",
    )(target, returned, weights, cotangent)


def device_of(index, emb_count):
    return (index // emb_count, lax.rem(index, emb_count))


def greet(me, owners, emb_count):
    barrier = pltpu.get_barrier_semaphore()

    def hello(step, carry):
        other = lax.rem(me + step, owners)
        pl.semaphore_signal(
            barrier, inc=1, device_id=device_of(other, emb_count), device_id_type=MESH
        )
        return carry

    lax.fori_loop(1, owners, hello, 0)
    return barrier


def lookup_kernel(
    owners,
    emb_count,
    capacity,
    owner_ref,
    offset_ref,
    proj_ref,
    out_ref,
    table_ref,
    returned_ref,
    asked_ref,
    target_ref,
    weights_ref,
    table_wide,
    table,
    member,
    ask,
    found,
    table_sem,
    ask_send,
    ask_recv,
    row_send,
    row_recv,
    z_send,
    z_recv,
    pair_send,
    pair_recv,
):
    f32, bf16 = jnp.float32, jnp.bfloat16
    fsdp_at = lax.axis_index("fsdp")
    emb_at = lax.axis_index("emb")
    me = fsdp_at * emb_count + emb_at
    z_at = fsdp_at // 2
    core = lax.rem(fsdp_at, 2)
    barrier = greet(me, owners, emb_count)
    load = pltpu.make_async_copy(table_ref, table_wide, table_sem)
    load.start()

    split = proj_ref.shape[2]
    weights_ref[:, z_at, core, :, :split] = proj_ref[...]
    weights_ref[:, z_at, core, :, split:] = out_ref[...]

    length = owner_ref.shape[1]
    owner = owner_ref[...]
    value = offset_ref[...] + 1
    high = (value // 64).astype(f32)
    low = lax.rem(value, 64).astype(f32)
    row_at = lax.broadcasted_iota(jnp.int32, (owners, 256), 0)
    for at in range(0, length, 256):
        member[:, at : at + 256] = (
            (row_at == owner[:, at : at + 256]).astype(f32).astype(bf16)
        )
    slots = []
    for at in range(0, length, 256):
        earlier = jnp.zeros((owners, 256), f32)
        for first in range(0, at + 256, 256):
            before = (
                lax.broadcasted_iota(jnp.int32, (256, 256), 0) + (first - at)
                < lax.broadcasted_iota(jnp.int32, (256, 256), 1)
            )
            earlier += matmul(member[:, first : first + 256], before.astype(f32).astype(bf16))
        slots.append(
            jnp.sum(earlier * member[:, at : at + 256].astype(f32), axis=0, keepdims=True)
        )
    slot = jnp.concatenate(slots, axis=1)
    target_ref[...] = owner * capacity + slot.astype(jnp.int32)
    here = lax.broadcasted_iota(jnp.int32, (128, length), 0).astype(f32) == slot
    request = 64.0 * matmul_nt(member[...], jnp.where(here, high, 0.0).astype(bf16))
    request += matmul_nt(member[...], jnp.where(here, low, 0.0).astype(bf16))
    ask[...] = request.astype(jnp.int32).reshape(ask.shape)

    pl.semaphore_wait(barrier, owners - 1)

    def send_ask(step, carry):
        other = lax.rem(me + step, owners)
        pltpu.make_async_remote_copy(
            src_ref=ask.at[other],
            dst_ref=asked_ref.at[me],
            send_sem=ask_send,
            recv_sem=ask_recv,
            device_id=device_of(other, emb_count),
            device_id_type=MESH,
        ).start()
        return carry

    lax.fori_loop(1, owners, send_ask, 0)
    z_copies = []
    for k in range(3):
        to = lax.rem(z_at + k + 1, 4)
        copy = pltpu.make_async_remote_copy(
            src_ref=weights_ref.at[:, z_at, core],
            dst_ref=weights_ref.at[:, z_at, core],
            send_sem=z_send.at[k],
            recv_sem=z_recv.at[k],
            device_id=(to * 2 + core, emb_at),
            device_id_type=MESH,
        )
        copy.start()
        z_copies.append(copy)
    asked_ref[me] = ask[me]

    load.wait()
    rows = table.shape[0]

    def narrow(index, carry):
        at = pl.ds(pl.multiple_of(index * 512, 512), 512)
        table[at, :] = table_wide[at, :].astype(bf16)
        return carry

    lax.fori_loop(0, rows // 512, narrow, 0)

    others = pl.ds(0, owners - 1)
    pltpu.make_async_copy(ask.at[others], ask.at[others], ask_send).wait()
    pltpu.make_async_copy(asked_ref.at[others], asked_ref.at[others], ask_recv).wait()

    group = 256 // capacity
    groups = owners // group

    def find(step, carry):
        index = lax.rem(me // group + step, groups)
        first_user = index * group
        wanted = asked_ref[pl.ds(first_user, group)].astype(f32)
        wanted = jnp.broadcast_to(wanted, (group, capacity, 128))
        same = lax.broadcasted_iota(jnp.int32, wanted.shape, 1) == lax.broadcasted_iota(
            jnp.int32, wanted.shape, 2
        )
        column = jnp.sum(jnp.where(same, wanted, 0.0), axis=2, keepdims=True)
        column = column.reshape(256, 1) - 1.0
        lane = lax.broadcasted_iota(jnp.int32, (256, 256), 1).astype(f32)
        total = jnp.zeros((256, table.shape[1]), f32)
        for first in range(0, rows, 256):
            pick = (lane + float(first) == column).astype(f32).astype(bf16)
            total += matmul(pick, table[first : first + 256, :])
        found[pl.ds(pl.multiple_of(index * 256, 256), 256), :] = total.astype(bf16)

        def send_rows(turn, carry):
            user = first_user + lax.rem(me + turn, group)

            @pl.when(user != me)
            def _():
                pltpu.make_async_remote_copy(
                    src_ref=found.at[pl.ds(user * capacity, capacity)],
                    dst_ref=returned_ref.at[pl.ds(me * capacity, capacity)],
                    send_sem=row_send,
                    recv_sem=row_recv,
                    device_id=device_of(user, emb_count),
                    device_id_type=MESH,
                ).start()

            return carry

        lax.fori_loop(0, group, send_rows, 0)
        return carry

    lax.fori_loop(0, groups, find, 0)
    own = pl.ds(pl.multiple_of(me * capacity, capacity), capacity)
    returned_ref[own, :] = found[own, :]

    for copy in z_copies:
        copy.wait()
    pair_copies = []
    for z in range(4):
        copy = pltpu.make_async_remote_copy(
            src_ref=weights_ref.at[:, z, core],
            dst_ref=weights_ref.at[:, z, core],
            send_sem=pair_send.at[z],
            recv_sem=pair_recv.at[z],
            device_id=(z_at * 2 + 1 - core, emb_at),
            device_id_type=MESH,
        )
        copy.start()
        pair_copies.append(copy)
    for copy in pair_copies:
        copy.wait()
    lines = pl.ds(0, (owners - 1) * capacity)
    pltpu.make_async_copy(found.at[lines], found.at[lines], row_send).wait()
    pltpu.make_async_copy(returned_ref.at[lines], returned_ref.at[lines], row_recv).wait()


def look_up(owner, offset, w_proj, w_out, table, owners, emb_count, capacity):
    bf16 = jnp.bfloat16
    layer_count, depth, split = w_proj.shape
    columns = split + w_out.shape[2]
    rows, width = table.shape
    length = owner.shape[1]
    slots = owners * capacity
    vmem = pl.BlockSpec(memory_space=pltpu.VMEM)
    one = pltpu.SemaphoreType.DMA
    return pl.pallas_call(
        functools.partial(lookup_kernel, owners, emb_count, capacity),
        out_shape=(
            jax.ShapeDtypeStruct((slots, width), bf16),
            jax.ShapeDtypeStruct((owners, 1, 128), jnp.int32),
            jax.ShapeDtypeStruct((1, length), jnp.int32),
            jax.ShapeDtypeStruct((layer_count, 4, 2, depth, columns), bf16),
        ),
        in_specs=[vmem] * 4 + [pl.BlockSpec(memory_space=pl.ANY)],
        out_specs=(vmem,) * 4,
        scratch_shapes=[
            pltpu.VMEM((rows, width), jnp.float32),
            pltpu.VMEM((rows, width), bf16),
            pltpu.VMEM((owners, length), bf16),
            pltpu.VMEM((owners, 1, 128), jnp.int32),
            pltpu.VMEM((slots, width), bf16),
            one,
            one,
            one,
            one,
            one,
            one((3,)),
            one((3,)),
            one((4,)),
            one((4,)),
        ],
        compiler_params=pltpu.CompilerParams(
            collective_id=2, has_side_effects=True, vmem_limit_bytes=40 << 20
        ),
        name="look_up",
    )(owner, offset, w_proj, w_out, table)


def collect_kernel(
    owners,
    emb_count,
    capacity,
    outgoing_ref,
    grads_ref,
    incoming_ref,
    total_ref,
    pair_in,
    pair_sum,
    z_in,
    z_sum,
    x_in,
    y_all,
    x_all,
    row_send,
    row_recv,
    own_sem,
    pair_sems,
    z_send,
    z_recv,
    x_send,
    x_recv,
    y_send,
    y_recv,
    g_send,
    g_recv,
):
    fsdp_at = lax.axis_index("fsdp")
    emb_at = lax.axis_index("emb")
    me = fsdp_at * emb_count + emb_at
    z_at = fsdp_at // 2
    core = lax.rem(fsdp_at, 2)
    y_at = emb_at // 4
    x_at = lax.rem(emb_at, 4)
    barrier = greet(me, owners, emb_count)
    pl.semaphore_wait(barrier, owners - 1)

    pair = pltpu.make_async_remote_copy(
        src_ref=grads_ref.at[1 - core],
        dst_ref=pair_in,
        send_sem=pair_sems.at[0],
        recv_sem=pair_sems.at[1],
        device_id=(z_at * 2 + 1 - core, emb_at),
        device_id_type=MESH,
    )
    pair.start()

    def send_rows(step, carry):
        other = lax.rem(me + step, owners)
        pltpu.make_async_remote_copy(
            src_ref=outgoing_ref.at[pl.ds(other * capacity, capacity)],
            dst_ref=incoming_ref.at[pl.ds(me * capacity, capacity)],
            send_sem=row_send,
            recv_sem=row_recv,
            device_id=device_of(other, emb_count),
            device_id_type=MESH,
        ).start()
        return carry

    lax.fori_loop(1, owners, send_rows, 0)
    own_rows = pl.ds(me * capacity, capacity)
    own = pltpu.make_async_copy(outgoing_ref.at[own_rows], incoming_ref.at[own_rows], own_sem)
    own.start()

    pair.wait()
    for z in range(4):
        for layer in range(2):
            pair_sum[z, layer] = (
                grads_ref[core, z, layer].astype(jnp.float32)
                + pair_in[z, layer].astype(jnp.float32)
            ).astype(jnp.bfloat16)
    z_copies = []
    for k in range(3):
        to = lax.rem(z_at + k + 1, 4)
        copy = pltpu.make_async_remote_copy(
            src_ref=pair_sum.at[to],
            dst_ref=z_in.at[k],
            send_sem=z_send.at[k],
            recv_sem=z_recv.at[k],
            device_id=(to * 2 + core, emb_at),
            device_id_type=MESH,
        )
        copy.start()
        z_copies.append(copy)
    for copy in z_copies:
        copy.wait()
    for part in range(4):
        rows = slice(part % 2 * 16, part % 2 * 16 + 16)
        value = pair_sum[z_at, part // 2, rows].astype(jnp.float32)
        for k in range(3):
            value += z_in[k, part // 2, rows].astype(jnp.float32)
        z_sum[part] = value.astype(jnp.bfloat16)

    x_copies = []
    for k in range(3):
        to = lax.rem(x_at + k + 1, 4)
        copy = pltpu.make_async_remote_copy(
            src_ref=z_sum.at[to],
            dst_ref=x_in.at[k],
            send_sem=x_send.at[k],
            recv_sem=x_recv.at[k],
            device_id=(fsdp_at, y_at * 4 + to),
            device_id_type=MESH,
        )
        copy.start()
        x_copies.append(copy)
    for copy in x_copies:
        copy.wait()
    value = z_sum[x_at].astype(jnp.float32)
    for k in range(3):
        value += x_in[k].astype(jnp.float32)
    y_all[y_at] = value.astype(jnp.bfloat16)

    y_copies = []
    for k in range(3):
        to = lax.rem(y_at + k + 1, 4)
        copy = pltpu.make_async_remote_copy(
            src_ref=y_all.at[y_at],
            dst_ref=y_all.at[y_at],
            send_sem=y_send.at[k],
            recv_sem=y_recv.at[k],
            device_id=(fsdp_at, to * 4 + x_at),
            device_id_type=MESH,
        )
        copy.start()
        y_copies.append(copy)
    for copy in y_copies:
        copy.wait()
    value = y_all[0].astype(jnp.float32)
    for y in range(1, 4):
        value += y_all[y].astype(jnp.float32)
    x_all[x_at] = value.astype(jnp.bfloat16)

    g_copies = []
    for k in range(3):
        to = lax.rem(x_at + k + 1, 4)
        copy = pltpu.make_async_remote_copy(
            src_ref=x_all.at[x_at],
            dst_ref=x_all.at[x_at],
            send_sem=g_send.at[k],
            recv_sem=g_recv.at[k],
            device_id=(fsdp_at, y_at * 4 + to),
            device_id_type=MESH,
        )
        copy.start()
        g_copies.append(copy)
    for copy in g_copies:
        copy.wait()
    for part in range(4):
        total_ref[part] = x_all[part]

    others = pl.ds(0, (owners - 1) * capacity)
    pltpu.make_async_copy(outgoing_ref.at[others], outgoing_ref.at[others], row_send).wait()
    pltpu.make_async_copy(incoming_ref.at[others], incoming_ref.at[others], row_recv).wait()
    own.wait()


def collect(outgoing, grads, owners, emb_count, capacity):
    columns = grads.shape[-1]
    depth = grads.shape[-2]
    bf16 = jnp.bfloat16
    vmem = pl.BlockSpec(memory_space=pltpu.VMEM)
    three = pltpu.SemaphoreType.DMA((3,))
    return pl.pallas_call(
        functools.partial(collect_kernel, owners, emb_count, capacity),
        out_shape=(
            jax.ShapeDtypeStruct(outgoing.shape, bf16),
            jax.ShapeDtypeStruct((4, 16, columns), bf16),
        ),
        in_specs=[vmem, vmem],
        out_specs=(vmem, vmem),
        scratch_shapes=[
            pltpu.VMEM((4, 2, depth, columns), bf16),
            pltpu.VMEM((4, 2, depth, columns), bf16),
            pltpu.VMEM((3, 2, depth, columns), bf16),
            pltpu.VMEM((4, 16, columns), bf16),
            pltpu.VMEM((3, 16, columns), bf16),
            pltpu.VMEM((4, 16, columns), bf16),
            pltpu.VMEM((4, 16, columns), bf16),
            pltpu.SemaphoreType.DMA,
            pltpu.SemaphoreType.DMA,
            pltpu.SemaphoreType.DMA,
            pltpu.SemaphoreType.DMA((2,)),
            three,
            three,
            three,
            three,
            three,
            three,
            three,
            three,
        ],
        compiler_params=pltpu.CompilerParams(
            collective_id=1, has_side_effects=True, vmem_limit_bytes=32 << 20
        ),
        name="collect",
    )(outgoing, grads)


def update_kernel(block, table_ref, requested_ref, stale_ref, incoming_ref, new_ref):
    count = requested_ref.shape[1]
    first = pl.program_id(0) * block
    row = first + lax.broadcasted_iota(jnp.int32, (block, count), 0)
    pick = (row == requested_ref[...]).astype(jnp.float32).astype(jnp.bfloat16)
    grad = jnp.dot(pick, incoming_ref[...], preferred_element_type=jnp.float32)
    rate = 0.5 / (1.0 + stale_ref[...].astype(jnp.float32))
    same = lax.broadcasted_iota(jnp.int32, (128, 128), 0) == lax.broadcasted_iota(
        jnp.int32, (128, 128), 1
    )
    for part in range(block // 128):
        rows = slice(part * 128, part * 128 + 128)
        spread = jnp.where(same, rate[0, part : part + 1, :], 0.0)
        column = jnp.sum(spread, axis=1, keepdims=True)
        new_ref[rows, :] = table_ref[rows, :] - column * grad[rows, :]


def update_table(table, requested, staleness, incoming):
    rows, width = table.shape
    block = 512
    count = incoming.shape[0]
    parts = block // 128
    return pl.pallas_call(
        functools.partial(update_kernel, block),
        out_shape=jax.ShapeDtypeStruct(table.shape, jnp.float32),
        grid=(rows // block,),
        in_specs=[
            pl.BlockSpec((block, width), lambda i: (i, 0)),
            pl.BlockSpec((1, count), lambda i: (0, 0)),
            pl.BlockSpec((1, parts, 128), lambda i: (i, 0, 0)),
            pl.BlockSpec((count, width), lambda i: (0, 0)),
        ],
        out_specs=pl.BlockSpec((block, width), lambda i: (i, 0)),
        compiler_params=pltpu.CompilerParams(vmem_limit_bytes=48 << 20),
        name="update_table",
    )(
        table,
        requested.reshape(1, count),
        staleness.reshape(rows // block, parts, 128),
        incoming,
    )


def local(item_table, item_owner, item_row, staleness, w_proj, w_out, out_grad):
    fsdp_count = lax.axis_size("fsdp")
    emb_count = lax.axis_size("emb")
    owners = fsdp_count * emb_count
    length = item_row.shape[1]
    capacity = 2 * length // owners
    layer_count, depth, split = w_proj.shape
    returned, asked, target, weights = look_up(
        item_owner.reshape(1, length),
        item_row,
        w_proj,
        w_out,
        item_table,
        owners,
        emb_count,
        capacity,
    )
    columns = weights.shape[-1]
    weights = weights.reshape(layer_count, fsdp_count * depth, columns)
    outgoing, grads = run_layers(target, returned, weights, out_grad[0], depth)
    requested = asked[:, 0, :capacity] - 1
    incoming, total = collect(outgoing, grads, owners, emb_count, capacity)
    new_table = update_table(item_table, requested, staleness, incoming)
    norm_scale = (owners * length) ** (-0.5)
    total = total.reshape(layer_count, depth, columns).astype(jnp.float32) * norm_scale
    return (new_table, total[:, :, :split], total[:, :, split:])


def solution(mesh):
    return jax.shard_map(
        local,
        mesh=mesh,
        in_specs=(
            P(("fsdp", "emb"), None),
            P(("fsdp", "emb"), None, None),
            P(("fsdp", "emb"), None),
            P(("fsdp", "emb")),
            P(None, "fsdp", None),
            P(None, "fsdp", None),
            P(("fsdp", "emb"), None, None),
        ),
        out_specs=(P(("fsdp", "emb"), None), P(None, "fsdp", None), P(None, "fsdp", None)),
        check_vma=False,
    )
```

```python
import functools

import jax
import jax.numpy as jnp
from jax import lax
from jax.experimental import pallas as pl
from jax.experimental.pallas import tpu as pltpu
from jax.sharding import PartitionSpec as P

MESH = pl.DeviceIdType.MESH

DH = 64


EPSILON = 1e-05


NT = (((1,), (1,)), ((), ()))


def matmul(left, right):
    return jnp.dot(left, right, preferred_element_type=jnp.float32)


def matmul_nt(left, right):
    return lax.dot_general(left, right, NT, preferred_element_type=jnp.float32)


def to_column(row):
    same = lax.broadcasted_iota(jnp.int32, (128, 128), 0) == lax.broadcasted_iota(
        jnp.int32, (128, 128), 1
    )
    parts = [
        jnp.sum(jnp.where(same, row[:, at : at + 128], 0.0), axis=1, keepdims=True)
        for at in range(0, row.shape[1], 128)
    ]
    return parts[0] if len(parts) == 1 else jnp.concatenate(parts, axis=0)


def device_of(index, emb_count):
    return (index // emb_count, lax.rem(index, emb_count))


def greet(me, owners, emb_count):
    barrier = pltpu.get_barrier_semaphore()

    def hello(step, carry):
        other = lax.rem(me + step, owners)
        pl.semaphore_signal(
            barrier, inc=1, device_id=device_of(other, emb_count), device_id_type=MESH
        )
        return carry

    lax.fori_loop(1, owners, hello, 0)
    return barrier


def step_kernel(
    owners,
    emb_count,
    capacity,
    owner_hbm,
    offset_hbm,
    proj_hbm,
    out_hbm,
    table_hbm,
    cotangent_hbm,
    incoming_ref,
    asked_ref,
    total_ref,
    owner_ref,
    offset_ref,
    proj_ref,
    out_ref,
    cotangent_ref,
    returned_ref,
    target_ref,
    weights_ref,
    member,
    ask,
    found,
    hidden,
    hidden_inv,
    normed,
    slope,
    gate,
    queries,
    key_heads,
    value_heads,
    attn,
    score_slope,
    mix_normed,
    mix_inv,
    gated,
    gradient,
    mixture,
    grad_mix,
    grad_pre,
    grad_mix_t,
    normed_t,
    queries_t,
    keys_t,
    values_t,
    grads,
    pair_in,
    z_in,
    z_sum,
    x_in,
    y_all,
    load_sems,
    ask_send,
    ask_recv,
    row_send,
    row_recv,
    grad_send,
    grad_recv,
    z_send,
    z_recv,
    pair_send,
    pair_recv,
    reduce_send,
    reduce_recv,
):
    f32, bf16 = jnp.float32, jnp.bfloat16
    fsdp_at = lax.axis_index("fsdp")
    emb_at = lax.axis_index("emb")
    me = fsdp_at * emb_count + emb_at
    z_at = fsdp_at // 2
    core = lax.rem(fsdp_at, 2)
    y_at = emb_at // 4
    x_at = lax.rem(emb_at, 4)
    barrier = greet(me, owners, emb_count)
    loads = []
    for number, (source, place) in enumerate(
        ((owner_hbm, owner_ref), (offset_hbm, offset_ref), (proj_hbm, proj_ref), (out_hbm, out_ref))
    ):
        load = pltpu.make_async_copy(source, place, load_sems.at[number])
        load.start()
        loads.append(load)
    chunk = gradient.shape[0]
    wide = (gradient, mix_normed.at[0], mix_normed.at[1], gradient)
    table_loads = [
        pltpu.make_async_copy(
            table_hbm.at[pl.ds(number * chunk, chunk)], wide[number], load_sems.at[4 + number]
        )
        for number in range(4)
    ]
    for number in range(3):
        table_loads[number].start()
    cotangent_load = pltpu.make_async_copy(cotangent_hbm, cotangent_ref, load_sems.at[8])
    cotangent_load.start()
    for load in loads:
        load.wait()

    split = proj_ref.shape[2]
    weights_ref[:, z_at, core, :, :split] = proj_ref[...]
    weights_ref[:, z_at, core, :, split:] = out_ref[...]

    length = owner_ref.shape[1]
    owner = owner_ref[...]
    value = offset_ref[...] + 1
    high = (value // 64).astype(f32)
    low = lax.rem(value, 64).astype(f32)
    row_at = lax.broadcasted_iota(jnp.int32, (owners, 256), 0)
    for at in range(0, length, 256):
        member[:, at : at + 256] = (
            (row_at == owner[:, at : at + 256]).astype(f32).astype(bf16)
        )
    slots = []
    for at in range(0, length, 256):
        earlier = jnp.zeros((owners, 256), f32)
        for first in range(0, at + 256, 256):
            before = (
                lax.broadcasted_iota(jnp.int32, (256, 256), 0) + (first - at)
                < lax.broadcasted_iota(jnp.int32, (256, 256), 1)
            )
            earlier += matmul(member[:, first : first + 256], before.astype(f32).astype(bf16))
        slots.append(
            jnp.sum(earlier * member[:, at : at + 256].astype(f32), axis=0, keepdims=True)
        )
    slot = jnp.concatenate(slots, axis=1)
    target_ref[...] = owner * capacity + slot.astype(jnp.int32)
    here = lax.broadcasted_iota(jnp.int32, (128, length), 0).astype(f32) == slot
    request = 64.0 * matmul_nt(member[...], jnp.where(here, high, 0.0).astype(bf16))
    request += matmul_nt(member[...], jnp.where(here, low, 0.0).astype(bf16))
    ask[...] = request.astype(jnp.int32).reshape(ask.shape)

    pl.semaphore_wait(barrier, owners - 1)

    def send_ask(step, carry):
        other = lax.rem(me + step, owners)
        pltpu.make_async_remote_copy(
            src_ref=ask.at[other],
            dst_ref=asked_ref.at[me],
            send_sem=ask_send,
            recv_sem=ask_recv,
            device_id=device_of(other, emb_count),
            device_id_type=MESH,
        ).start()
        return carry

    lax.fori_loop(1, owners, send_ask, 0)
    z_copies = []
    for k in range(3):
        to = lax.rem(z_at + k + 1, 4)
        copy = pltpu.make_async_remote_copy(
            src_ref=weights_ref.at[:, z_at, core],
            dst_ref=weights_ref.at[:, z_at, core],
            send_sem=z_send.at[k],
            recv_sem=z_recv.at[k],
            device_id=(to * 2 + core, emb_at),
            device_id_type=MESH,
        )
        copy.start()
        z_copies.append(copy)
    asked_ref[me] = ask[me]

    table = key_heads.at[1]
    table_rows = table.shape[0]
    for number in range(4):
        table_loads[number].wait()

        def narrow(index, carry):
            at = pl.ds(pl.multiple_of(index * 256, 256), 256)
            to = pl.ds(pl.multiple_of(index * 256 + number * chunk, 256), 256)
            table[to, :] = wide[number][at, :].astype(bf16)
            return carry

        lax.fori_loop(0, chunk // 256, narrow, 0)
        if number == 0:
            table_loads[3].start()

    others = pl.ds(0, owners - 1)
    pltpu.make_async_copy(ask.at[others], ask.at[others], ask_send).wait()
    pltpu.make_async_copy(asked_ref.at[others], asked_ref.at[others], ask_recv).wait()

    group = 256 // capacity
    groups = owners // group

    def find(step, carry):
        index = lax.rem(me // group + step, groups)
        first_user = index * group
        wanted = asked_ref[pl.ds(first_user, group)].astype(f32)
        wanted = jnp.broadcast_to(wanted, (group, capacity, 128))
        same = lax.broadcasted_iota(jnp.int32, wanted.shape, 1) == lax.broadcasted_iota(
            jnp.int32, wanted.shape, 2
        )
        column = jnp.sum(jnp.where(same, wanted, 0.0), axis=2, keepdims=True)
        column = column.reshape(256, 1) - 1.0
        lane = lax.broadcasted_iota(jnp.int32, (256, 256), 1).astype(f32)
        total = jnp.zeros((256, table.shape[1]), f32)
        for first in range(0, table_rows, 256):
            pick = (lane + float(first) == column).astype(f32).astype(bf16)
            total += matmul(pick, table[first : first + 256, :])
        found[pl.ds(pl.multiple_of(index * 256, 256), 256), :] = total.astype(bf16)

        def send_rows(turn, carry):
            user = first_user + lax.rem(me + turn, group)

            @pl.when(user != me)
            def _():
                pltpu.make_async_remote_copy(
                    src_ref=found.at[pl.ds(user * capacity, capacity)],
                    dst_ref=returned_ref.at[pl.ds(me * capacity, capacity)],
                    send_sem=row_send,
                    recv_sem=row_recv,
                    device_id=device_of(user, emb_count),
                    device_id_type=MESH,
                ).start()

            return carry

        lax.fori_loop(0, group, send_rows, 0)
        return carry

    lax.fori_loop(0, groups, find, 0)
    own = pl.ds(pl.multiple_of(me * capacity, capacity), capacity)
    returned_ref[own, :] = found[own, :]

    for copy in z_copies:
        copy.wait()
    pair_copies = []
    for z in range(4):
        copy = pltpu.make_async_remote_copy(
            src_ref=weights_ref.at[:, z, core],
            dst_ref=weights_ref.at[:, z, core],
            send_sem=pair_send.at[z],
            recv_sem=pair_recv.at[z],
            device_id=(z_at * 2 + 1 - core, emb_at),
            device_id_type=MESH,
        )
        copy.start()
        pair_copies.append(copy)
    for copy in pair_copies:
        copy.wait()
    lines = pl.ds(0, (owners - 1) * capacity)
    pltpu.make_async_copy(found.at[lines], found.at[lines], row_send).wait()
    pltpu.make_async_copy(returned_ref.at[lines], returned_ref.at[lines], row_recv).wait()

    block = 256
    width = cotangent_ref.shape[1]
    blocks = length // block
    heads = width // DH
    slots = returned_ref.shape[0]
    layer_count = weights_ref.shape[0]
    head_of = lax.broadcasted_iota(jnp.int32, (heads, width), 1) // DH
    head_mask = (head_of == lax.broadcasted_iota(jnp.int32, (heads, width), 0)).astype(f32)
    head_mask = head_mask.astype(bf16)

    weights = weights_ref.reshape(layer_count, width, 5 * width)

    def rows(index):
        return pl.ds(pl.multiple_of(index * block, block), block)

    def head_rows(index):
        return pl.ds(pl.multiple_of(index * block * heads, block * heads), block * heads)

    def pair_of(query, key):
        return query * (query + 1) // 2 + key

    def fetch(index, carry):
        at = pl.multiple_of(index * 128, 128)
        column = to_column(target_ref[:, pl.ds(at, 128)].astype(f32))
        total = jnp.zeros((128, width), f32)
        for first in range(0, slots, 256):
            lane = lax.broadcasted_iota(jnp.int32, (128, 256), 1).astype(f32) + float(first)
            pick = (lane == column).astype(f32).astype(bf16)
            total += matmul(pick, returned_ref[first : first + 256, :])
        hidden[0, pl.ds(at, 128), :] = total.astype(bf16)
        return carry

    lax.fori_loop(0, length // 128, fetch, 0)

    def forward(layer, carry):
        def project(index, carry):
            at = rows(index)
            value = hidden[layer, at, :].astype(f32)
            center = value - jnp.mean(value, axis=1, keepdims=True)
            inverse = lax.rsqrt(jnp.mean(center * center, axis=1, keepdims=True) + EPSILON)
            norm = (center * inverse).astype(bf16)
            hidden_inv[layer, at, :] = inverse
            normed[layer, at, :] = norm
            for part in range(4):
                columns = slice(part * width, part * width + width)
                pre = matmul(norm, weights[layer, :, columns])
                logistic = 0.5 + 0.5 * jnp.tanh(0.5 * pre)
                act = pre * logistic
                slope[layer, at, columns] = (logistic + act - act * logistic).astype(bf16)
                act = act.astype(bf16)
                if part == 0:
                    gate[layer, at, :] = act
                elif part == 2:
                    queries[layer, at, :] = act * jnp.asarray(0.0625, bf16)
                else:
                    store = value_heads if part == 1 else key_heads
                    for head in range(heads):
                        spot = pl.ds(
                            pl.multiple_of((index * heads + head) * block, block), block
                        )
                        store[layer, spot, :] = act * head_mask[head : head + 1, :]
            return carry

        lax.fori_loop(0, blocks, project, 0)

        def scores(query, key, masked):
            pair = pair_of(query, key)
            query_part = queries[layer, rows(query), :]
            if masked:
                visible = lax.broadcasted_iota(
                    jnp.int32, (block, block), 1
                ) <= lax.broadcasted_iota(jnp.int32, (block, block), 0)
            parts = []
            for head in range(heads):
                spot = pl.ds(pl.multiple_of((key * heads + head) * block, block), block)
                half = matmul_nt(query_part, key_heads[layer, spot, :])
                bend = jnp.tanh(half)
                lift = 1.0 + bend
                if masked:
                    lift = jnp.where(visible, lift, 0.0)
                columns = slice(head * block, head * block + block)
                part = (half * lift).astype(bf16)
                parts.append(part)
                attn[layer, pair, :, columns] = part
                score_slope[layer, pair, :, columns] = (
                    lift * (1.0 + (half - half * bend))
                ).astype(bf16)
            return matmul(
                jnp.concatenate(parts, axis=1), value_heads[layer, head_rows(key), :]
            )

        def attend_rows(query, carry):
            mixture[...] = scores(query, query, True)

            def before(key, carry):
                mixture[...] += scores(query, key, False)
                return carry

            lax.fori_loop(0, query, before, 0)
            at = rows(query)
            value = mixture[...]
            center = value - jnp.mean(value, axis=1, keepdims=True)
            inverse = lax.rsqrt(jnp.mean(center * center, axis=1, keepdims=True) + EPSILON)
            norm = center * inverse
            mix_normed[layer, at, :] = norm
            mix_inv[layer, at, :] = inverse
            gated_part = (norm * gate[layer, at, :].astype(f32)).astype(bf16)
            gated[layer, at, :] = gated_part

            @pl.when(layer < layer_count - 1)
            def _():
                branch = matmul(gated_part, weights[layer, :, 4 * width :])
                hidden[layer + 1, at, :] = (hidden[layer, at, :].astype(f32) + branch).astype(bf16)

            return carry

        lax.fori_loop(0, blocks, attend_rows, 0)
        return carry

    lax.fori_loop(0, layer_count, forward, 0)

    cotangent_load.wait()
    gradient[...] = cotangent_ref[...].astype(f32)

    in_flight = {}

    def send(name, layer, number, source, place, where):
        copy = pltpu.make_async_remote_copy(
            src_ref=source,
            dst_ref=place,
            send_sem=reduce_send.at[layer, number],
            recv_sem=reduce_recv.at[layer, number],
            device_id=where,
            device_id_type=MESH,
        )
        copy.start()
        in_flight.setdefault((name, layer), []).append(copy)

    def receive(name, layer):
        for copy in in_flight[name, layer]:
            copy.wait()

    def reduce_pair(layer):
        where = (z_at * 2 + 1 - core, emb_at)
        send("pair", layer, 0, grads.at[layer, 1 - core], pair_in.at[layer], where)

    def reduce_z(layer):
        receive("pair", layer)
        for z in range(4):
            pair_in[layer, z] = (
                grads[layer, core, z].astype(f32) + pair_in[layer, z].astype(f32)
            ).astype(bf16)
        for k in range(3):
            to = lax.rem(z_at + k + 1, 4)
            where = (to * 2 + core, emb_at)
            send("z", layer, 1 + k, pair_in.at[layer, to], z_in.at[layer, k], where)

    def reduce_x(layer):
        receive("z", layer)
        half = z_sum.shape[3]
        for part in range(4):
            spot = slice(part // 2 * 16, part // 2 * 16 + 16)
            span = slice(part % 2 * half, part % 2 * half + half)
            value = pair_in[layer, z_at, spot, span].astype(f32)
            for k in range(3):
                value += z_in[layer, k, spot, span].astype(f32)
            z_sum[layer, part] = value.astype(bf16)
        for k in range(3):
            to = lax.rem(x_at + k + 1, 4)
            where = (fsdp_at, y_at * 4 + to)
            send("x", layer, 4 + k, z_sum.at[layer, to], x_in.at[layer, k], where)

    def reduce_y(layer):
        receive("x", layer)
        value = z_sum[layer, x_at].astype(f32)
        for k in range(3):
            value += x_in[layer, k].astype(f32)
        y_all[layer, y_at] = value.astype(bf16)
        for k in range(3):
            to = lax.rem(y_at + k + 1, 4)
            where = (fsdp_at, to * 4 + x_at)
            send("y", layer, 7 + k, y_all.at[layer, y_at], y_all.at[layer, y_at], where)

    def reduce_g(layer):
        receive("y", layer)
        value = y_all[layer, 0].astype(f32)
        for y in range(1, 4):
            value += y_all[layer, y].astype(f32)
        total_ref[layer, x_at] = value.astype(bf16)
        for k in range(3):
            to = lax.rem(x_at + k + 1, 4)
            where = (fsdp_at, y_at * 4 + to)
            place = total_ref.at[layer, x_at]
            send("g", layer, 10 + k, place, place, where)

    def reduce_end(layer):
        receive("g", layer)

    def backward(layer, between):

        def through_gate(index, carry):
            at = rows(index)
            grad_round = gradient[at, :].astype(bf16)
            grad_gated = matmul_nt(grad_round, weights[layer, :, 4 * width :])
            norm = mix_normed[layer, at, :]
            first = slope[layer, at, :width].astype(f32)
            grad_pre[at, :width] = (grad_gated * norm * first).astype(bf16)
            inner = grad_gated * gate[layer, at, :].astype(f32)
            grad = mix_inv[layer, at, :] * (
                inner
                - jnp.mean(inner, axis=1, keepdims=True)
                - norm * jnp.mean(inner * norm, axis=1, keepdims=True)
            )
            grad_mix[at, :] = grad.astype(bf16)
            grad_mix_t[:, at] = grad.T.astype(bf16)
            normed_t[:, at] = normed[layer, at, :].T
            queries_t[:, at] = queries[layer, at, :].T
            return carry

        lax.fori_loop(0, blocks, through_gate, 0)
        between[0]()

        gw_out = lax.dot_general(
            gated[layer],
            gradient[...].astype(bf16),
            (((0,), (0,)), ((), ())),
            preferred_element_type=jnp.float32,
        ).astype(bf16)
        depth = grads.shape[3]
        for part in range(8):
            grads[layer, part % 2, part // 2, :, 4 * width :] = gw_out[
                part * depth : part * depth + depth
            ]

        keys_t[...] = jnp.zeros_like(keys_t)
        values_t[...] = jnp.zeros_like(values_t)

        def through_scores(query, carry):
            mixture[...] = jnp.zeros_like(mixture)

            def one(key, carry):
                pair = pair_of(query, key)
                here = rows(query)
                there = rows(key)
                grad_part = grad_mix[here, :]
                parts = []
                for head in range(heads):
                    spot = pl.ds(pl.multiple_of((key * heads + head) * block, block), block)
                    columns = slice(head * block, head * block + block)
                    lines = slice(head * DH, head * DH + DH)
                    grad = matmul_nt(grad_part, value_heads[layer, spot, :])
                    values_t[lines, there] += matmul(
                        grad_mix_t[lines, here], attn[layer, pair, :, columns]
                    )
                    part = (grad * score_slope[layer, pair, :, columns].astype(f32)).astype(bf16)
                    parts.append(part)
                    keys_t[lines, there] += matmul(queries_t[lines, here], part)
                mixture[...] += matmul(
                    jnp.concatenate(parts, axis=1), key_heads[layer, head_rows(key), :]
                )
                return carry

            lax.fori_loop(0, query + 1, one, 0)
            at = rows(query)
            third = slope[layer, at, 2 * width : 3 * width].astype(f32)
            grad_pre[at, 2 * width : 3 * width] = (mixture[...] * 0.0625 * third).astype(bf16)
            return carry

        lax.fori_loop(0, blocks, through_scores, 0)
        between[1]()

        def through_keys(key, carry):
            at = rows(key)
            for part, total in ((1, values_t), (3, keys_t)):
                span = slice(part * width, part * width + width)
                grad_pre[at, span] = (total[:, at].T * slope[layer, at, span].astype(f32)).astype(
                    bf16
                )
            return carry

        lax.fori_loop(0, blocks, through_keys, 0)
        between[2]()

        for part in range(4):
            span = slice(part * width, part * width + width)
            gw_proj = matmul(normed_t[...], grad_pre[:, span]).astype(bf16)
            for piece in range(8):
                grads[layer, piece % 2, piece // 2, :, span] = gw_proj[
                    piece * depth : piece * depth + depth
                ]

        reduce_pair(layer)
        between[3]()

        def through_norm(index, carry):
            at = rows(index)
            grad_normed = matmul_nt(grad_pre[at, :], weights[layer, :, : 4 * width])
            norm = normed[layer, at, :].astype(f32)
            gradient[at, :] = gradient[at, :] + hidden_inv[layer, at, :] * (
                grad_normed
                - jnp.mean(grad_normed, axis=1, keepdims=True)
                - norm * jnp.mean(grad_normed * norm, axis=1, keepdims=True)
            )
            return carry

        lax.fori_loop(0, blocks, through_norm, 0)
    def nothing():
        pass

    backward(1, (nothing, nothing, nothing, nothing))
    backward(
        0,
        (
            lambda: reduce_z(1),
            lambda: reduce_x(1),
            lambda: reduce_y(1),
            lambda: reduce_g(1),
        ),
    )


    reduce_z(0)

    def give_back(step, carry):
        index = lax.rem(me * capacity // 128 + step, slots // 128)
        at = pl.ds(pl.multiple_of(index * 128, 128), 128)
        total = jnp.zeros((128, width), f32)
        for first in range(0, length, 256):
            spot = lax.broadcasted_iota(jnp.int32, (128, 256), 0) + index * 128
            pick = (spot == target_ref[:, first : first + 256]).astype(f32).astype(bf16)
            total += matmul(pick, gradient[first : first + 256, :].astype(bf16))
        found[at, :] = total.astype(bf16)
        return carry

    lax.fori_loop(0, slots // 128, give_back, 0)

    def send_grads(step, carry):
        other = lax.rem(me + step, owners)
        pltpu.make_async_remote_copy(
            src_ref=found.at[pl.ds(other * capacity, capacity)],
            dst_ref=incoming_ref.at[pl.ds(me * capacity, capacity)],
            send_sem=grad_send,
            recv_sem=grad_recv,
            device_id=device_of(other, emb_count),
            device_id_type=MESH,
        ).start()
        return carry

    lax.fori_loop(1, owners, send_grads, 0)
    incoming_ref[own, :] = found[own, :]
    reduce_x(0)
    reduce_end(1)
    reduce_y(0)
    reduce_g(0)
    reduce_end(0)
    pltpu.make_async_copy(found.at[lines], found.at[lines], grad_send).wait()
    pltpu.make_async_copy(incoming_ref.at[lines], incoming_ref.at[lines], grad_recv).wait()


def run_step(owner, offset, w_proj, w_out, table, cotangent, owners, emb_count, capacity):
    f32, bf16, i32 = jnp.float32, jnp.bfloat16, jnp.int32
    layer_count, depth, split = w_proj.shape
    columns = split + w_out.shape[2]
    length, width = cotangent.shape
    slots = owners * capacity
    blocks = length // 256
    pairs = blocks * (blocks + 1) // 2
    heads = width // DH
    two = layer_count
    vmem = pl.BlockSpec(memory_space=pltpu.VMEM)
    sem = pltpu.SemaphoreType.DMA
    scratch = [
        ((1, length), i32),
        ((1, length), i32),
        (w_proj.shape, bf16),
        (w_out.shape, bf16),
        ((length, width), bf16),
        ((slots, width), bf16),
        ((1, length), i32),
        ((two, 4, 2, depth, columns), bf16),
        ((owners, length), bf16),
        ((owners, 1, 128), i32),
        ((slots, width), bf16),
        ((two, length, width), bf16),
        ((two, length, 1), f32),
        ((two, length, width), bf16),
        ((two, length, split), bf16),
        ((two, length, width), bf16),
        ((two, length, width), bf16),
        ((two, length * heads, width), bf16),
        ((two, length * heads, width), bf16),
        ((two, pairs, 256, 256 * heads), bf16),
        ((two, pairs, 256, 256 * heads), bf16),
        ((two, length, width), f32),
        ((two, length, 1), f32),
        ((two, length, width), bf16),
        ((length, width), f32),
        ((256, width), f32),
        ((length, width), bf16),
        ((length, split), bf16),
        ((width, length), bf16),
        ((width, length), bf16),
        ((width, length), bf16),
        ((width, length), f32),
        ((width, length), f32),
        ((two, 2, 4, depth, columns), bf16),
        ((two, 4, depth, columns), bf16),
        ((two, 3, depth, columns), bf16),
        ((two, 4, 16, columns // 2), bf16),
        ((two, 3, 16, columns // 2), bf16),
        ((two, 4, 16, columns // 2), bf16),
    ]
    return pl.pallas_call(
        functools.partial(step_kernel, owners, emb_count, capacity),
        out_shape=(
            jax.ShapeDtypeStruct((slots, width), bf16),
            jax.ShapeDtypeStruct((owners, 1, 128), i32),
            jax.ShapeDtypeStruct((two, 4, 16, columns // 2), bf16),
        ),
        in_specs=[pl.BlockSpec(memory_space=pl.ANY)] * 6,
        out_specs=(vmem,) * 3,
        scratch_shapes=[pltpu.VMEM(*one) for one in scratch]
        + [sem((9,))]
        + [sem] * 6
        + [sem((3,)), sem((3,)), sem((4,)), sem((4,)), sem((two, 13)), sem((two, 13))],
        compiler_params=pltpu.CompilerParams(
            collective_id=1, has_side_effects=True, vmem_limit_bytes=62 << 20
        ),
        name="step",
    )(owner, offset, w_proj, w_out, table, cotangent)


def update_kernel(
    block, scale, table_ref, requested_ref, stale_ref, incoming_ref, total_ref, new_ref, proj_ref, out_ref
):
    @pl.when(pl.program_id(0) == 0)
    def _():
        half = total_ref.shape[3]
        split = proj_ref.shape[2]
        for part in range(4):
            spot = slice(part // 2 * 16, part // 2 * 16 + 16)
            value = total_ref[:, part].astype(jnp.float32) * scale
            if part % 2 == 0:
                proj_ref[:, spot, :half] = value
            else:
                proj_ref[:, spot, half:] = value[:, :, : split - half]
                out_ref[:, spot, :] = value[:, :, split - half :]

    count = requested_ref.shape[1]
    first = pl.program_id(0) * block
    row = first + lax.broadcasted_iota(jnp.int32, (block, count), 0)
    pick = (row == requested_ref[...]).astype(jnp.float32).astype(jnp.bfloat16)
    grad = jnp.dot(pick, incoming_ref[...], preferred_element_type=jnp.float32)
    rate = 0.5 / (1.0 + stale_ref[...].astype(jnp.float32))
    same = lax.broadcasted_iota(jnp.int32, (128, 128), 0) == lax.broadcasted_iota(
        jnp.int32, (128, 128), 1
    )
    for part in range(block // 128):
        rows = slice(part * 128, part * 128 + 128)
        spread = jnp.where(same, rate[0, part : part + 1, :], 0.0)
        column = jnp.sum(spread, axis=1, keepdims=True)
        new_ref[rows, :] = table_ref[rows, :] - column * grad[rows, :]


def update_table(table, requested, staleness, incoming, total, scale):
    rows, width = table.shape
    block = 512
    count = incoming.shape[0]
    parts = block // 128
    layer_count, _, depth, half = total.shape
    depth *= 2
    split = 2 * half - width
    whole = lambda *dims: pl.BlockSpec(dims, lambda i: (0,) * len(dims))
    return pl.pallas_call(
        functools.partial(update_kernel, block, scale),
        out_shape=(
            jax.ShapeDtypeStruct(table.shape, jnp.float32),
            jax.ShapeDtypeStruct((layer_count, depth, split), jnp.float32),
            jax.ShapeDtypeStruct((layer_count, depth, width), jnp.float32),
        ),
        grid=(rows // block,),
        in_specs=[
            pl.BlockSpec((block, width), lambda i: (i, 0)),
            whole(1, count),
            pl.BlockSpec((1, parts, 128), lambda i: (i, 0, 0)),
            whole(count, width),
            whole(*total.shape),
        ],
        out_specs=(
            pl.BlockSpec((block, width), lambda i: (i, 0)),
            whole(layer_count, depth, split),
            whole(layer_count, depth, width),
        ),
        compiler_params=pltpu.CompilerParams(vmem_limit_bytes=58 << 20),
        name="update_table",
    )(
        table,
        requested.reshape(1, count),
        staleness.reshape(rows // block, parts, 128),
        incoming,
        total,
    )


def local(item_table, item_owner, item_row, staleness, w_proj, w_out, out_grad):
    emb_count = lax.axis_size("emb")
    owners = lax.axis_size("fsdp") * emb_count
    length = item_row.shape[1]
    capacity = 2 * length // owners
    incoming, asked, total = run_step(
        item_owner.reshape(1, length),
        item_row,
        w_proj,
        w_out,
        item_table,
        out_grad[0],
        owners,
        emb_count,
        capacity,
    )
    requested = asked[:, 0, :capacity] - 1
    norm_scale = (owners * length) ** (-0.5)
    return update_table(item_table, requested, staleness, incoming, total, norm_scale)


def solution(mesh):
    return jax.shard_map(
        local,
        mesh=mesh,
        in_specs=(
            P(("fsdp", "emb"), None),
            P(("fsdp", "emb"), None, None),
            P(("fsdp", "emb"), None),
            P(("fsdp", "emb")),
            P(None, "fsdp", None),
            P(None, "fsdp", None),
            P(("fsdp", "emb"), None, None),
        ),
        out_specs=(P(("fsdp", "emb"), None), P(None, "fsdp", None), P(None, "fsdp", None)),
        check_vma=False,
    )
```

```python
import functools

import jax
import jax.numpy as jnp
from jax import lax
from jax.experimental import pallas as pl
from jax.experimental.pallas import tpu as pltpu
from jax.sharding import PartitionSpec as P

MESH = pl.DeviceIdType.MESH

DH = 64


EPSILON = 1e-05


NT = (((1,), (1,)), ((), ()))


def matmul(left, right):
    return jnp.dot(left, right, preferred_element_type=jnp.float32)


def matmul_nt(left, right):
    return lax.dot_general(left, right, NT, preferred_element_type=jnp.float32)


def to_column(row):
    same = lax.broadcasted_iota(jnp.int32, (128, 128), 0) == lax.broadcasted_iota(
        jnp.int32, (128, 128), 1
    )
    parts = [
        jnp.sum(jnp.where(same, row[:, at : at + 128], 0.0), axis=1, keepdims=True)
        for at in range(0, row.shape[1], 128)
    ]
    return parts[0] if len(parts) == 1 else jnp.concatenate(parts, axis=0)


def device_of(index, emb_count):
    return (index // emb_count, lax.rem(index, emb_count))


def greet(me, owners, emb_count):
    barrier = pltpu.get_barrier_semaphore()

    def hello(step, carry):
        other = lax.rem(me + step, owners)
        pl.semaphore_signal(
            barrier, inc=1, device_id=device_of(other, emb_count), device_id_type=MESH
        )
        return carry

    lax.fori_loop(1, owners, hello, 0)
    return barrier


def step_kernel(
    owners,
    emb_count,
    capacity,
    owner_hbm,
    offset_hbm,
    proj_hbm,
    out_hbm,
    table_hbm,
    cotangent_hbm,
    incoming_ref,
    requested_ref,
    total_ref,
    owner_ref,
    offset_ref,
    proj_ref,
    out_ref,
    cotangent_ref,
    returned_ref,
    target_ref,
    weights_ref,
    member,
    ask,
    asked_ref,
    found,
    hidden,
    hidden_inv,
    normed,
    slope,
    gate,
    queries,
    key_heads,
    value_heads,
    attn,
    score_slope,
    mix_normed,
    mix_inv,
    gated,
    gradient,
    mixture,
    grad_mix,
    grad_pre,
    grad_mix_t,
    normed_t,
    queries_t,
    keys_t,
    values_t,
    grads,
    pair_in,
    z_in,
    z_sum,
    x_in,
    y_all,
    load_sems,
    ask_send,
    ask_recv,
    row_send,
    row_recv,
    grad_send,
    grad_recv,
    z_send,
    z_recv,
    pair_send,
    pair_recv,
    reduce_send,
    reduce_recv,
):
    f32, bf16 = jnp.float32, jnp.bfloat16
    fsdp_at = lax.axis_index("fsdp")
    emb_at = lax.axis_index("emb")
    me = fsdp_at * emb_count + emb_at
    z_at = fsdp_at // 2
    core = lax.rem(fsdp_at, 2)
    y_at = emb_at // 4
    x_at = lax.rem(emb_at, 4)
    barrier = greet(me, owners, emb_count)
    loads = []
    for number, (source, place) in enumerate(
        ((owner_hbm, owner_ref), (offset_hbm, offset_ref), (proj_hbm, proj_ref), (out_hbm, out_ref))
    ):
        load = pltpu.make_async_copy(source, place, load_sems.at[number])
        load.start()
        loads.append(load)
    chunk = gradient.shape[0]
    wide = (gradient, mix_normed.at[0], mix_normed.at[1], gradient)
    table_loads = [
        pltpu.make_async_copy(
            table_hbm.at[pl.ds(number * chunk, chunk)], wide[number], load_sems.at[4 + number]
        )
        for number in range(4)
    ]
    for number in range(3):
        table_loads[number].start()
    cotangent_load = pltpu.make_async_copy(cotangent_hbm, cotangent_ref, load_sems.at[8])
    cotangent_load.start()
    for load in loads:
        load.wait()

    split = proj_ref.shape[2]
    weights_ref[:, z_at, core, :, :split] = proj_ref[...]
    weights_ref[:, z_at, core, :, split:] = out_ref[...]

    length = owner_ref.shape[1]
    owner = owner_ref[...]
    value = offset_ref[...] + 1
    high = (value // 64).astype(f32)
    low = lax.rem(value, 64).astype(f32)
    row_at = lax.broadcasted_iota(jnp.int32, (owners, 256), 0)
    for at in range(0, length, 256):
        member[:, at : at + 256] = (
            (row_at == owner[:, at : at + 256]).astype(f32).astype(bf16)
        )
    slots = []
    for at in range(0, length, 256):
        earlier = jnp.zeros((owners, 256), f32)
        for first in range(0, at + 256, 256):
            before = (
                lax.broadcasted_iota(jnp.int32, (256, 256), 0) + (first - at)
                < lax.broadcasted_iota(jnp.int32, (256, 256), 1)
            )
            earlier += matmul(member[:, first : first + 256], before.astype(f32).astype(bf16))
        slots.append(
            jnp.sum(earlier * member[:, at : at + 256].astype(f32), axis=0, keepdims=True)
        )
    slot = jnp.concatenate(slots, axis=1)
    target_ref[...] = owner * capacity + slot.astype(jnp.int32)
    here = lax.broadcasted_iota(jnp.int32, (128, length), 0).astype(f32) == slot
    request = 64.0 * matmul_nt(member[...], jnp.where(here, high, 0.0).astype(bf16))
    request += matmul_nt(member[...], jnp.where(here, low, 0.0).astype(bf16))
    ask[...] = request.astype(jnp.int32).reshape(ask.shape)

    pl.semaphore_wait(barrier, owners - 1)

    def send_ask(step, carry):
        other = lax.rem(me + step, owners)
        pltpu.make_async_remote_copy(
            src_ref=ask.at[other],
            dst_ref=asked_ref.at[me],
            send_sem=ask_send,
            recv_sem=ask_recv,
            device_id=device_of(other, emb_count),
            device_id_type=MESH,
        ).start()
        return carry

    lax.fori_loop(1, owners, send_ask, 0)
    z_copies = []
    for k in range(3):
        to = lax.rem(z_at + k + 1, 4)
        copy = pltpu.make_async_remote_copy(
            src_ref=weights_ref.at[:, z_at, core],
            dst_ref=weights_ref.at[:, z_at, core],
            send_sem=z_send.at[k],
            recv_sem=z_recv.at[k],
            device_id=(to * 2 + core, emb_at),
            device_id_type=MESH,
        )
        copy.start()
        z_copies.append(copy)
    asked_ref[me] = ask[me]

    table = key_heads.at[1]
    table_rows = table.shape[0]
    for number in range(4):
        table_loads[number].wait()

        def narrow(index, carry):
            at = pl.ds(pl.multiple_of(index * 256, 256), 256)
            to = pl.ds(pl.multiple_of(index * 256 + number * chunk, 256), 256)
            table[to, :] = wide[number][at, :].astype(bf16)
            return carry

        lax.fori_loop(0, chunk // 256, narrow, 0)
        if number == 0:
            table_loads[3].start()

    others = pl.ds(0, owners - 1)
    pltpu.make_async_copy(ask.at[others], ask.at[others], ask_send).wait()
    pltpu.make_async_copy(asked_ref.at[others], asked_ref.at[others], ask_recv).wait()

    group = 256 // capacity
    groups = owners // group

    def find(step, carry):
        index = lax.rem(me // group + step, groups)
        first_user = index * group
        wanted = asked_ref[pl.ds(first_user, group)].astype(f32)
        wanted = jnp.broadcast_to(wanted, (group, capacity, 128))
        same = lax.broadcasted_iota(jnp.int32, wanted.shape, 1) == lax.broadcasted_iota(
            jnp.int32, wanted.shape, 2
        )
        column = jnp.sum(jnp.where(same, wanted, 0.0), axis=2, keepdims=True)
        column = column.reshape(256, 1) - 1.0
        diagonal = lax.broadcasted_iota(jnp.int32, (256, 256), 0) == lax.broadcasted_iota(
            jnp.int32, (256, 256), 1
        )
        span = pl.ds(pl.multiple_of(index * 256, 256), 256)
        line = jnp.sum(jnp.where(diagonal, column, 0.0), axis=0, keepdims=True)
        requested_ref[:, span] = line.astype(jnp.int32)
        lane = lax.broadcasted_iota(jnp.int32, (256, 256), 1).astype(f32)
        total = jnp.zeros((256, table.shape[1]), f32)
        for first in range(0, table_rows, 256):
            pick = (lane + float(first) == column).astype(f32).astype(bf16)
            total += matmul(pick, table[first : first + 256, :])
        found[pl.ds(pl.multiple_of(index * 256, 256), 256), :] = total.astype(bf16)

        def send_rows(turn, carry):
            user = first_user + lax.rem(me + turn, group)

            @pl.when(user != me)
            def _():
                pltpu.make_async_remote_copy(
                    src_ref=found.at[pl.ds(user * capacity, capacity)],
                    dst_ref=returned_ref.at[pl.ds(me * capacity, capacity)],
                    send_sem=row_send,
                    recv_sem=row_recv,
                    device_id=device_of(user, emb_count),
                    device_id_type=MESH,
                ).start()

            return carry

        lax.fori_loop(0, group, send_rows, 0)
        return carry

    lax.fori_loop(0, groups, find, 0)
    own = pl.ds(pl.multiple_of(me * capacity, capacity), capacity)
    returned_ref[own, :] = found[own, :]

    for copy in z_copies:
        copy.wait()
    pair_copies = []
    for z in range(4):
        copy = pltpu.make_async_remote_copy(
            src_ref=weights_ref.at[:, z, core],
            dst_ref=weights_ref.at[:, z, core],
            send_sem=pair_send.at[z],
            recv_sem=pair_recv.at[z],
            device_id=(z_at * 2 + 1 - core, emb_at),
            device_id_type=MESH,
        )
        copy.start()
        pair_copies.append(copy)
    for copy in pair_copies:
        copy.wait()
    lines = pl.ds(0, (owners - 1) * capacity)
    pltpu.make_async_copy(found.at[lines], found.at[lines], row_send).wait()
    pltpu.make_async_copy(returned_ref.at[lines], returned_ref.at[lines], row_recv).wait()

    block = 256
    width = cotangent_ref.shape[1]
    blocks = length // block
    heads = width // DH
    slots = returned_ref.shape[0]
    layer_count = weights_ref.shape[0]
    head_of = lax.broadcasted_iota(jnp.int32, (heads, width), 1) // DH
    head_mask = (head_of == lax.broadcasted_iota(jnp.int32, (heads, width), 0)).astype(f32)
    head_mask = head_mask.astype(bf16)

    weights = weights_ref.reshape(layer_count, width, 5 * width)

    def rows(index):
        if isinstance(index, int):
            return pl.ds(index * block, block)
        return pl.ds(pl.multiple_of(index * block, block), block)

    def head_rows(index):
        if isinstance(index, int):
            return pl.ds(index * block * heads, block * heads)
        return pl.ds(pl.multiple_of(index * block * heads, block * heads), block * heads)

    def pair_of(query, key):
        return query * (query + 1) // 2 + key

    def fetch(index, carry):
        at = index * 128
        column = to_column(target_ref[:, pl.ds(at, 128)].astype(f32))
        total = jnp.zeros((128, width), f32)
        for first in range(0, slots, 256):
            lane = lax.broadcasted_iota(jnp.int32, (128, 256), 1).astype(f32) + float(first)
            pick = (lane == column).astype(f32).astype(bf16)
            total += matmul(pick, returned_ref[first : first + 256, :])
        hidden[0, pl.ds(at, 128), :] = total.astype(bf16)
        return carry

    for at_index in range(length // 128):
        fetch(at_index, 0)

    def forward(layer, carry):
        def project(index, carry):
            at = rows(index)
            value = hidden[layer, at, :].astype(f32)
            center = value - jnp.mean(value, axis=1, keepdims=True)
            inverse = lax.rsqrt(jnp.mean(center * center, axis=1, keepdims=True) + EPSILON)
            norm = (center * inverse).astype(bf16)
            hidden_inv[layer, at, :] = inverse
            normed[layer, at, :] = norm
            for part in range(4):
                columns = slice(part * width, part * width + width)
                pre = matmul(norm, weights[layer, :, columns])
                logistic = 0.5 + 0.5 * jnp.tanh(0.5 * pre)
                act = pre * logistic
                slope[layer, at, columns] = (logistic + act - act * logistic).astype(bf16)
                act = act.astype(bf16)
                if part == 0:
                    gate[layer, at, :] = act
                elif part == 2:
                    queries[layer, at, :] = act * jnp.asarray(0.0625, bf16)
                else:
                    store = value_heads if part == 1 else key_heads
                    for head in range(heads):
                        spot = rows(index * heads + head)
                        store[layer, spot, :] = act * head_mask[head : head + 1, :]
            return carry

        for at_index in range(0, blocks):
            project(at_index, 0)

        def scores(query, key, masked):
            pair = pair_of(query, key)
            query_part = queries[layer, rows(query), :]
            one = jnp.asarray(1.0, bf16)
            if masked:
                visible = lax.broadcasted_iota(
                    jnp.int32, (block, block), 1
                ) <= lax.broadcasted_iota(jnp.int32, (block, block), 0)
            parts = []
            for head in range(heads):
                spot = rows(key * heads + head)
                half = matmul_nt(query_part, key_heads[layer, spot, :]).astype(bf16)
                bend = jnp.tanh(half)
                lift = one + bend
                if masked:
                    lift = jnp.where(visible, lift, jnp.zeros_like(lift))
                columns = slice(head * block, head * block + block)
                part = half * lift
                parts.append(part)
                attn[layer, pair, :, columns] = part
                score_slope[layer, pair, :, columns] = lift * (one + (half - half * bend))
            return matmul(
                jnp.concatenate(parts, axis=1), value_heads[layer, head_rows(key), :]
            )

        def attend_rows(query, carry):
            mixture[...] = scores(query, query, True)

            def before(key, carry):
                mixture[...] += scores(query, key, False)
                return carry

            for at_index in range(0, query):
                before(at_index, 0)
            at = rows(query)
            value = mixture[...]
            center = value - jnp.mean(value, axis=1, keepdims=True)
            inverse = lax.rsqrt(jnp.mean(center * center, axis=1, keepdims=True) + EPSILON)
            norm = center * inverse
            mix_normed[layer, at, :] = norm
            mix_inv[layer, at, :] = inverse
            gated_part = (norm * gate[layer, at, :].astype(f32)).astype(bf16)
            gated[layer, at, :] = gated_part

            branch = matmul(gated_part, weights[layer, :, 4 * width :])
            following = lax.rem(layer + 1, layer_count)
            hidden[following, at, :] = (hidden[layer, at, :].astype(f32) + branch).astype(bf16)
            return carry

        for at_index in range(0, blocks):
            attend_rows(at_index, 0)
        return carry

    lax.fori_loop(0, layer_count, forward, 0)

    cotangent_load.wait()
    gradient[...] = cotangent_ref[...].astype(f32)

    in_flight = {}

    def send(name, layer, number, source, place, where):
        copy = pltpu.make_async_remote_copy(
            src_ref=source,
            dst_ref=place,
            send_sem=reduce_send.at[layer, number],
            recv_sem=reduce_recv.at[layer, number],
            device_id=where,
            device_id_type=MESH,
        )
        copy.start()
        in_flight.setdefault((name, layer), []).append(copy)

    def receive(name, layer):
        for copy in in_flight[name, layer]:
            copy.wait()

    def reduce_pair(layer):
        where = (z_at * 2 + 1 - core, emb_at)
        send("pair", layer, 0, grads.at[layer, 1 - core], pair_in.at[layer], where)

    def reduce_z(layer):
        receive("pair", layer)
        for z in range(4):
            pair_in[layer, z] = (
                grads[layer, core, z].astype(f32) + pair_in[layer, z].astype(f32)
            ).astype(bf16)
        for k in range(3):
            to = lax.rem(z_at + k + 1, 4)
            where = (to * 2 + core, emb_at)
            send("z", layer, 1 + k, pair_in.at[layer, to], z_in.at[layer, k], where)

    def reduce_x(layer):
        receive("z", layer)
        half = z_sum.shape[3]
        for part in range(4):
            spot = slice(part // 2 * 16, part // 2 * 16 + 16)
            span = slice(part % 2 * half, part % 2 * half + half)
            value = pair_in[layer, z_at, spot, span].astype(f32)
            for k in range(3):
                value += z_in[layer, k, spot, span].astype(f32)
            z_sum[layer, part] = value.astype(bf16)
        for k in range(3):
            to = lax.rem(x_at + k + 1, 4)
            where = (fsdp_at, y_at * 4 + to)
            send("x", layer, 4 + k, z_sum.at[layer, to], x_in.at[layer, k], where)

    def reduce_y(layer):
        receive("x", layer)
        value = z_sum[layer, x_at].astype(f32)
        for k in range(3):
            value += x_in[layer, k].astype(f32)
        y_all[layer, y_at] = value.astype(bf16)
        for k in range(3):
            to = lax.rem(y_at + k + 1, 4)
            where = (fsdp_at, to * 4 + x_at)
            send("y", layer, 7 + k, y_all.at[layer, y_at], y_all.at[layer, y_at], where)

    def reduce_g(layer):
        receive("y", layer)
        value = y_all[layer, 0].astype(f32)
        for y in range(1, 4):
            value += y_all[layer, y].astype(f32)
        total_ref[layer, x_at] = value.astype(bf16)
        for k in range(3):
            to = lax.rem(x_at + k + 1, 4)
            where = (fsdp_at, y_at * 4 + to)
            place = total_ref.at[layer, x_at]
            send("g", layer, 10 + k, place, place, where)

    def reduce_end(layer):
        receive("g", layer)

    def backward(layer, between):

        def through_gate(index, carry):
            at = rows(index)
            grad_round = gradient[at, :].astype(bf16)
            grad_gated = matmul_nt(grad_round, weights[layer, :, 4 * width :])
            norm = mix_normed[layer, at, :]
            first = slope[layer, at, :width].astype(f32)
            grad_pre[at, :width] = (grad_gated * norm * first).astype(bf16)
            inner = grad_gated * gate[layer, at, :].astype(f32)
            grad = mix_inv[layer, at, :] * (
                inner
                - jnp.mean(inner, axis=1, keepdims=True)
                - norm * jnp.mean(inner * norm, axis=1, keepdims=True)
            )
            grad_mix[at, :] = grad.astype(bf16)
            grad_mix_t[:, at] = grad.T.astype(bf16)
            normed_t[:, at] = normed[layer, at, :].T
            queries_t[:, at] = queries[layer, at, :].T
            return carry

        for at_index in range(0, blocks):
            through_gate(at_index, 0)
        between[0]()

        gw_out = lax.dot_general(
            gated[layer],
            gradient[...].astype(bf16),
            (((0,), (0,)), ((), ())),
            preferred_element_type=jnp.float32,
        ).astype(bf16)
        depth = grads.shape[3]
        for part in range(8):
            grads[layer, part % 2, part // 2, :, 4 * width :] = gw_out[
                part * depth : part * depth + depth
            ]

        keys_t[...] = jnp.zeros_like(keys_t)
        values_t[...] = jnp.zeros_like(values_t)

        def through_scores(query, carry):
            mixture[...] = jnp.zeros_like(mixture)

            def one(key, carry):
                pair = pair_of(query, key)
                here = rows(query)
                there = rows(key)
                grad_part = grad_mix[here, :]
                parts = []
                for head in range(heads):
                    spot = rows(key * heads + head)
                    columns = slice(head * block, head * block + block)
                    lines = slice(head * DH, head * DH + DH)
                    grad = matmul_nt(grad_part, value_heads[layer, spot, :]).astype(bf16)
                    values_t[lines, there] += matmul(
                        grad_mix_t[lines, here], attn[layer, pair, :, columns]
                    )
                    part = grad * score_slope[layer, pair, :, columns]
                    parts.append(part)
                    keys_t[lines, there] += matmul(queries_t[lines, here], part)
                mixture[...] += matmul(
                    jnp.concatenate(parts, axis=1), key_heads[layer, head_rows(key), :]
                )
                return carry

            for at_index in range(0, query + 1):
                one(at_index, 0)
            at = rows(query)
            third = slope[layer, at, 2 * width : 3 * width].astype(f32)
            grad_pre[at, 2 * width : 3 * width] = (mixture[...] * 0.0625 * third).astype(bf16)
            return carry

        for at_index in range(0, blocks):
            through_scores(at_index, 0)
        between[1]()

        def through_keys(key, carry):
            at = rows(key)
            for part, total in ((1, values_t), (3, keys_t)):
                span = slice(part * width, part * width + width)
                grad_pre[at, span] = (total[:, at].T * slope[layer, at, span].astype(f32)).astype(
                    bf16
                )
            return carry

        for at_index in range(0, blocks):
            through_keys(at_index, 0)
        between[2]()

        for part in range(4):
            span = slice(part * width, part * width + width)
            gw_proj = matmul(normed_t[...], grad_pre[:, span]).astype(bf16)
            for piece in range(8):
                grads[layer, piece % 2, piece // 2, :, span] = gw_proj[
                    piece * depth : piece * depth + depth
                ]

        reduce_pair(layer)
        between[3]()

        def through_norm(index, carry):
            at = rows(index)
            grad_normed = matmul_nt(grad_pre[at, :], weights[layer, :, : 4 * width])
            norm = normed[layer, at, :].astype(f32)
            gradient[at, :] = gradient[at, :] + hidden_inv[layer, at, :] * (
                grad_normed
                - jnp.mean(grad_normed, axis=1, keepdims=True)
                - norm * jnp.mean(grad_normed * norm, axis=1, keepdims=True)
            )
            return carry

        for at_index in range(0, blocks):
            through_norm(at_index, 0)
    def nothing():
        pass

    backward(1, (nothing, nothing, nothing, nothing))
    backward(
        0,
        (
            lambda: reduce_z(1),
            lambda: reduce_x(1),
            lambda: reduce_y(1),
            lambda: reduce_g(1),
        ),
    )


    reduce_z(0)

    def give_back(index):
        at = pl.ds(index * 128, 128)
        total = jnp.zeros((128, width), f32)
        for first in range(0, length, 256):
            spot = lax.broadcasted_iota(jnp.int32, (128, 256), 0) + index * 128
            pick = (spot == target_ref[:, first : first + 256]).astype(f32).astype(bf16)
            total += matmul(pick, gradient[first : first + 256, :].astype(bf16))
        found[at, :] = total.astype(bf16)

    for at_index in range(slots // 128):
        give_back(at_index)

    def send_grads(step, carry):
        other = lax.rem(me + step, owners)
        pltpu.make_async_remote_copy(
            src_ref=found.at[pl.ds(other * capacity, capacity)],
            dst_ref=incoming_ref.at[pl.ds(me * capacity, capacity)],
            send_sem=grad_send,
            recv_sem=grad_recv,
            device_id=device_of(other, emb_count),
            device_id_type=MESH,
        ).start()
        return carry

    lax.fori_loop(1, 33, send_grads, 0)
    reduce_x(0)
    lax.fori_loop(33, 65, send_grads, 0)
    reduce_y(0)
    lax.fori_loop(65, 97, send_grads, 0)
    reduce_g(0)
    lax.fori_loop(97, owners, send_grads, 0)
    incoming_ref[own, :] = found[own, :]
    reduce_end(1)
    reduce_end(0)
    pltpu.make_async_copy(found.at[lines], found.at[lines], grad_send).wait()
    pltpu.make_async_copy(incoming_ref.at[lines], incoming_ref.at[lines], grad_recv).wait()


def run_step(owner, offset, w_proj, w_out, table, cotangent, owners, emb_count, capacity):
    f32, bf16, i32 = jnp.float32, jnp.bfloat16, jnp.int32
    layer_count, depth, split = w_proj.shape
    columns = split + w_out.shape[2]
    length, width = cotangent.shape
    slots = owners * capacity
    blocks = length // 256
    pairs = blocks * (blocks + 1) // 2
    heads = width // DH
    two = layer_count
    vmem = pl.BlockSpec(memory_space=pltpu.VMEM)
    sem = pltpu.SemaphoreType.DMA
    scratch = [
        ((1, length), i32),
        ((1, length), i32),
        (w_proj.shape, bf16),
        (w_out.shape, bf16),
        ((length, width), bf16),
        ((slots, width), bf16),
        ((1, length), i32),
        ((two, 4, 2, depth, columns), bf16),
        ((owners, length), bf16),
        ((owners, 1, 128), i32),
        ((owners, 1, 128), i32),
        ((slots, width), bf16),
        ((two, length, width), bf16),
        ((two, length, 1), f32),
        ((two, length, width), bf16),
        ((two, length, split), bf16),
        ((two, length, width), bf16),
        ((two, length, width), bf16),
        ((two, length * heads, width), bf16),
        ((two, length * heads, width), bf16),
        ((two, pairs, 256, 256 * heads), bf16),
        ((two, pairs, 256, 256 * heads), bf16),
        ((two, length, width), f32),
        ((two, length, 1), f32),
        ((two, length, width), bf16),
        ((length, width), f32),
        ((256, width), f32),
        ((length, width), bf16),
        ((length, split), bf16),
        ((width, length), bf16),
        ((width, length), bf16),
        ((width, length), bf16),
        ((width, length), f32),
        ((width, length), f32),
        ((two, 2, 4, depth, columns), bf16),
        ((two, 4, depth, columns), bf16),
        ((two, 3, depth, columns), bf16),
        ((two, 4, 16, columns // 2), bf16),
        ((two, 3, 16, columns // 2), bf16),
        ((two, 4, 16, columns // 2), bf16),
    ]
    return pl.pallas_call(
        functools.partial(step_kernel, owners, emb_count, capacity),
        out_shape=(
            jax.ShapeDtypeStruct((slots, width), bf16),
            jax.ShapeDtypeStruct((1, slots), i32),
            jax.ShapeDtypeStruct((two, 4, 16, columns // 2), bf16),
        ),
        in_specs=[pl.BlockSpec(memory_space=pl.ANY)] * 6,
        out_specs=(vmem,) * 3,
        scratch_shapes=[pltpu.VMEM(*one) for one in scratch]
        + [sem((9,))]
        + [sem] * 6
        + [sem((3,)), sem((3,)), sem((4,)), sem((4,)), sem((two, 13)), sem((two, 13))],
        compiler_params=pltpu.CompilerParams(
            collective_id=1, has_side_effects=True, vmem_limit_bytes=62 << 20
        ),
        name="step",
    )(owner, offset, w_proj, w_out, table, cotangent)


def update_kernel(
    block, scale, table_ref, requested_ref, stale_ref, incoming_ref, total_ref, new_ref, proj_ref, out_ref
):
    @pl.when(pl.program_id(0) == 0)
    def _():
        half = total_ref.shape[3]
        split = proj_ref.shape[2]
        for part in range(4):
            spot = slice(part // 2 * 16, part // 2 * 16 + 16)
            value = total_ref[:, part].astype(jnp.float32) * scale
            if part % 2 == 0:
                proj_ref[:, spot, :half] = value
            else:
                proj_ref[:, spot, half:] = value[:, :, : split - half]
                out_ref[:, spot, :] = value[:, :, split - half :]

    count = requested_ref.shape[1]
    first = pl.program_id(0) * block
    row = first + lax.broadcasted_iota(jnp.int32, (block, count), 0)
    pick = (row == requested_ref[...]).astype(jnp.float32).astype(jnp.bfloat16)
    grad = jnp.dot(pick, incoming_ref[...], preferred_element_type=jnp.float32)
    rate = 0.5 / (1.0 + stale_ref[...].astype(jnp.float32))
    same = lax.broadcasted_iota(jnp.int32, (128, 128), 0) == lax.broadcasted_iota(
        jnp.int32, (128, 128), 1
    )
    for part in range(block // 128):
        rows = slice(part * 128, part * 128 + 128)
        spread = jnp.where(same, rate[0, part : part + 1, :], 0.0)
        column = jnp.sum(spread, axis=1, keepdims=True)
        new_ref[rows, :] = table_ref[rows, :] - column * grad[rows, :]


def update_table(table, requested, staleness, incoming, total, scale):
    rows, width = table.shape
    block = 512
    count = incoming.shape[0]
    parts = block // 128
    layer_count, _, depth, half = total.shape
    depth *= 2
    split = 2 * half - width
    whole = lambda *dims: pl.BlockSpec(dims, lambda i: (0,) * len(dims))
    return pl.pallas_call(
        functools.partial(update_kernel, block, scale),
        out_shape=(
            jax.ShapeDtypeStruct(table.shape, jnp.float32),
            jax.ShapeDtypeStruct((layer_count, depth, split), jnp.float32),
            jax.ShapeDtypeStruct((layer_count, depth, width), jnp.float32),
        ),
        grid=(rows // block,),
        in_specs=[
            pl.BlockSpec((block, width), lambda i: (i, 0)),
            whole(1, count),
            pl.BlockSpec((1, parts, 128), lambda i: (i, 0, 0)),
            whole(count, width),
            whole(*total.shape),
        ],
        out_specs=(
            pl.BlockSpec((block, width), lambda i: (i, 0)),
            whole(layer_count, depth, split),
            whole(layer_count, depth, width),
        ),
        compiler_params=pltpu.CompilerParams(vmem_limit_bytes=58 << 20),
        name="update_table",
    )(
        table,
        requested,
        staleness.reshape(rows // block, parts, 128),
        incoming,
        total,
    )


def local(item_table, item_owner, item_row, staleness, w_proj, w_out, out_grad):
    emb_count = lax.axis_size("emb")
    owners = lax.axis_size("fsdp") * emb_count
    length = item_row.shape[1]
    capacity = 2 * length // owners
    incoming, requested, total = run_step(
        item_owner.reshape(1, length),
        item_row,
        w_proj,
        w_out,
        item_table,
        out_grad[0],
        owners,
        emb_count,
        capacity,
    )
    norm_scale = (owners * length) ** (-0.5)
    return update_table(item_table, requested, staleness, incoming, total, norm_scale)


def solution(mesh):
    return jax.shard_map(
        local,
        mesh=mesh,
        in_specs=(
            P(("fsdp", "emb"), None),
            P(("fsdp", "emb"), None, None),
            P(("fsdp", "emb"), None),
            P(("fsdp", "emb")),
            P(None, "fsdp", None),
            P(None, "fsdp", None),
            P(("fsdp", "emb"), None, None),
        ),
        out_specs=(P(("fsdp", "emb"), None), P(None, "fsdp", None), P(None, "fsdp", None)),
        check_vma=False,
    )
```

```python
import functools

import jax
import jax.numpy as jnp
from jax import lax
from jax.experimental import pallas as pl
from jax.experimental.pallas import tpu as pltpu
from jax.sharding import PartitionSpec as P

MESH = pl.DeviceIdType.MESH

DH = 64


EPSILON = 1e-05


NT = (((1,), (1,)), ((), ()))


def matmul(left, right):
    return jnp.dot(left, right, preferred_element_type=jnp.float32)


def matmul_nt(left, right):
    return lax.dot_general(left, right, NT, preferred_element_type=jnp.float32)


def to_column(row):
    same = lax.broadcasted_iota(jnp.int32, (128, 128), 0) == lax.broadcasted_iota(
        jnp.int32, (128, 128), 1
    )
    parts = [
        jnp.sum(jnp.where(same, row[:, at : at + 128], 0.0), axis=1, keepdims=True)
        for at in range(0, row.shape[1], 128)
    ]
    return parts[0] if len(parts) == 1 else jnp.concatenate(parts, axis=0)


def device_of(index, emb_count):
    return (index // emb_count, lax.rem(index, emb_count))


def greet(me, owners, emb_count):
    barrier = pltpu.get_barrier_semaphore()

    def hello(step, carry):
        other = lax.rem(me + step, owners)
        pl.semaphore_signal(
            barrier, inc=1, device_id=device_of(other, emb_count), device_id_type=MESH
        )
        return carry

    lax.fori_loop(1, owners, hello, 0)
    return barrier


def step_kernel(
    owners,
    emb_count,
    capacity,
    owner_hbm,
    offset_hbm,
    proj_hbm,
    out_hbm,
    table_hbm,
    cotangent_hbm,
    incoming_ref,
    requested_ref,
    total_ref,
    owner_ref,
    offset_ref,
    proj_ref,
    out_ref,
    cotangent_ref,
    returned_ref,
    target_ref,
    weights_ref,
    member,
    ask,
    asked_ref,
    found,
    hidden,
    hidden_inv,
    normed,
    slope,
    gate,
    queries,
    key_heads,
    value_heads,
    attn,
    score_slope,
    mix_normed,
    mix_inv,
    gated,
    gradient,
    mixture,
    grad_mix,
    grad_pre,
    grad_mix_t,
    normed_t,
    queries_t,
    keys_t,
    values_t,
    grads,
    pair_in,
    z_in,
    z_sum,
    x_in,
    y_all,
    load_sems,
    ask_send,
    ask_recv,
    row_send,
    row_recv,
    grad_send,
    grad_recv,
    z_send,
    z_recv,
    pair_send,
    pair_recv,
    reduce_send,
    reduce_recv,
):
    f32, bf16 = jnp.float32, jnp.bfloat16
    fsdp_at = lax.axis_index("fsdp")
    emb_at = lax.axis_index("emb")
    me = fsdp_at * emb_count + emb_at
    z_at = fsdp_at // 2
    core = lax.rem(fsdp_at, 2)
    y_at = emb_at // 4
    x_at = lax.rem(emb_at, 4)
    barrier = greet(me, owners, emb_count)
    loads = []
    for number, (source, place) in enumerate(
        ((owner_hbm, owner_ref), (offset_hbm, offset_ref), (proj_hbm, proj_ref), (out_hbm, out_ref))
    ):
        load = pltpu.make_async_copy(source, place, load_sems.at[number])
        load.start()
        loads.append(load)
    chunk = gradient.shape[0]
    wide = (gradient, mix_normed.at[0], mix_normed.at[1], gradient)
    table_loads = [
        pltpu.make_async_copy(
            table_hbm.at[pl.ds(number * chunk, chunk)], wide[number], load_sems.at[4 + number]
        )
        for number in range(4)
    ]
    for number in range(3):
        table_loads[number].start()
    cotangent_load = pltpu.make_async_copy(cotangent_hbm, cotangent_ref, load_sems.at[8])
    cotangent_load.start()
    for load in loads:
        load.wait()

    split = proj_ref.shape[2]
    weights_ref[:, z_at, core, :, :split] = proj_ref[...]
    weights_ref[:, z_at, core, :, split:] = out_ref[...]

    length = owner_ref.shape[1]
    owner = owner_ref[...]
    value = offset_ref[...] + 1
    high = (value // 64).astype(f32)
    low = lax.rem(value, 64).astype(f32)
    row_at = lax.broadcasted_iota(jnp.int32, (owners, 256), 0)
    for at in range(0, length, 256):
        member[:, at : at + 256] = (
            (row_at == owner[:, at : at + 256]).astype(f32).astype(bf16)
        )
    slots = []
    for at in range(0, length, 256):
        earlier = jnp.zeros((owners, 256), f32)
        for first in range(0, at + 256, 256):
            before = (
                lax.broadcasted_iota(jnp.int32, (256, 256), 0) + (first - at)
                < lax.broadcasted_iota(jnp.int32, (256, 256), 1)
            )
            earlier += matmul(member[:, first : first + 256], before.astype(f32).astype(bf16))
        slots.append(
            jnp.sum(earlier * member[:, at : at + 256].astype(f32), axis=0, keepdims=True)
        )
    slot = jnp.concatenate(slots, axis=1)
    target_ref[...] = owner * capacity + slot.astype(jnp.int32)
    here = lax.broadcasted_iota(jnp.int32, (128, length), 0).astype(f32) == slot
    request = 64.0 * matmul_nt(member[...], jnp.where(here, high, 0.0).astype(bf16))
    request += matmul_nt(member[...], jnp.where(here, low, 0.0).astype(bf16))
    ask[...] = request.astype(jnp.int32).reshape(ask.shape)

    pl.semaphore_wait(barrier, owners - 1)

    def send_ask(step, carry):
        other = lax.rem(me + step, owners)
        pltpu.make_async_remote_copy(
            src_ref=ask.at[other],
            dst_ref=asked_ref.at[me],
            send_sem=ask_send,
            recv_sem=ask_recv,
            device_id=device_of(other, emb_count),
            device_id_type=MESH,
        ).start()
        return carry

    lax.fori_loop(1, owners, send_ask, 0)
    z_copies = []
    for k in range(3):
        to = lax.rem(z_at + k + 1, 4)
        copy = pltpu.make_async_remote_copy(
            src_ref=weights_ref.at[:, z_at, core],
            dst_ref=weights_ref.at[:, z_at, core],
            send_sem=z_send.at[k],
            recv_sem=z_recv.at[k],
            device_id=(to * 2 + core, emb_at),
            device_id_type=MESH,
        )
        copy.start()
        z_copies.append(copy)
    asked_ref[me] = ask[me]

    table = key_heads.at[1]
    table_rows = table.shape[0]
    for number in range(4):
        table_loads[number].wait()

        def narrow(index, carry):
            at = pl.ds(pl.multiple_of(index * 256, 256), 256)
            to = pl.ds(pl.multiple_of(index * 256 + number * chunk, 256), 256)
            table[to, :] = wide[number][at, :].astype(bf16)
            return carry

        lax.fori_loop(0, chunk // 256, narrow, 0)
        if number == 0:
            table_loads[3].start()

    others = pl.ds(0, owners - 1)
    pltpu.make_async_copy(ask.at[others], ask.at[others], ask_send).wait()
    pltpu.make_async_copy(asked_ref.at[others], asked_ref.at[others], ask_recv).wait()

    group = 256 // capacity
    groups = owners // group

    def find(step, carry):
        index = lax.rem(me // group + step, groups)
        first_user = index * group
        wanted = asked_ref[pl.ds(first_user, group)].astype(f32)
        wanted = jnp.broadcast_to(wanted, (group, capacity, 128))
        same = lax.broadcasted_iota(jnp.int32, wanted.shape, 1) == lax.broadcasted_iota(
            jnp.int32, wanted.shape, 2
        )
        column = jnp.sum(jnp.where(same, wanted, 0.0), axis=2, keepdims=True)
        column = column.reshape(256, 1) - 1.0
        diagonal = lax.broadcasted_iota(jnp.int32, (256, 256), 0) == lax.broadcasted_iota(
            jnp.int32, (256, 256), 1
        )
        span = pl.ds(pl.multiple_of(index * 256, 256), 256)
        line = jnp.sum(jnp.where(diagonal, column, 0.0), axis=0, keepdims=True)
        requested_ref[:, span] = line.astype(jnp.int32)
        lane = lax.broadcasted_iota(jnp.int32, (256, 256), 1).astype(f32)
        total = jnp.zeros((256, table.shape[1]), f32)
        for first in range(0, table_rows, 256):
            pick = (lane + float(first) == column).astype(f32).astype(bf16)
            total += matmul(pick, table[first : first + 256, :])
        found[pl.ds(pl.multiple_of(index * 256, 256), 256), :] = total.astype(bf16)

        def send_rows(turn, carry):
            user = first_user + lax.rem(me + turn, group)

            @pl.when(user != me)
            def _():
                pltpu.make_async_remote_copy(
                    src_ref=found.at[pl.ds(user * capacity, capacity)],
                    dst_ref=returned_ref.at[pl.ds(me * capacity, capacity)],
                    send_sem=row_send,
                    recv_sem=row_recv,
                    device_id=device_of(user, emb_count),
                    device_id_type=MESH,
                ).start()

            return carry

        lax.fori_loop(0, group, send_rows, 0)
        return carry

    lax.fori_loop(0, groups, find, 0)
    picks = attn.at[0]
    across = picks.shape[2]
    all_slots = owners * capacity
    for part in range(length // 128):
        place = to_column(target_ref[:, part * 128 : part * 128 + 128].astype(f32))
        for first in range(0, all_slots, 256):
            lane = lax.broadcasted_iota(jnp.int32, (128, 256), 1).astype(f32) + float(first)
            line = first // across * 128
            span = slice(first % across, first % across + 256)
            picks[part, line : line + 128, span] = (lane == place).astype(f32).astype(bf16)
    own = pl.ds(pl.multiple_of(me * capacity, capacity), capacity)
    returned_ref[own, :] = found[own, :]

    for copy in z_copies:
        copy.wait()
    pair_copies = []
    for z in range(4):
        copy = pltpu.make_async_remote_copy(
            src_ref=weights_ref.at[:, z, core],
            dst_ref=weights_ref.at[:, z, core],
            send_sem=pair_send.at[z],
            recv_sem=pair_recv.at[z],
            device_id=(z_at * 2 + 1 - core, emb_at),
            device_id_type=MESH,
        )
        copy.start()
        pair_copies.append(copy)
    for copy in pair_copies:
        copy.wait()
    lines = pl.ds(0, (owners - 1) * capacity)
    pltpu.make_async_copy(found.at[lines], found.at[lines], row_send).wait()
    pltpu.make_async_copy(returned_ref.at[lines], returned_ref.at[lines], row_recv).wait()

    block = 256
    width = cotangent_ref.shape[1]
    blocks = length // block
    heads = width // DH
    slots = returned_ref.shape[0]
    layer_count = weights_ref.shape[0]
    head_of = lax.broadcasted_iota(jnp.int32, (heads, width), 1) // DH
    head_mask = (head_of == lax.broadcasted_iota(jnp.int32, (heads, width), 0)).astype(f32)
    head_mask = head_mask.astype(bf16)

    weights = weights_ref.reshape(layer_count, width, 5 * width)

    def rows(index):
        if isinstance(index, int):
            return pl.ds(index * block, block)
        return pl.ds(pl.multiple_of(index * block, block), block)

    def head_rows(index):
        if isinstance(index, int):
            return pl.ds(index * block * heads, block * heads)
        return pl.ds(pl.multiple_of(index * block * heads, block * heads), block * heads)

    def pair_of(query, key):
        return query * (query + 1) // 2 + key

    def fetch(part, carry):
        total = jnp.zeros((128, width), f32)
        for first in range(0, slots, across):
            line = first // across * 128
            total += matmul(picks[part, line : line + 128, :], returned_ref[first : first + across, :])
        hidden[0, pl.ds(pl.multiple_of(part * 128, 128), 128), :] = total.astype(bf16)
        return carry

    lax.fori_loop(0, length // 128, fetch, 0)

    def forward(layer, carry):
        def project(index, carry):
            at = rows(index)
            value = hidden[layer, at, :].astype(f32)
            center = value - jnp.mean(value, axis=1, keepdims=True)
            inverse = lax.rsqrt(jnp.mean(center * center, axis=1, keepdims=True) + EPSILON)
            norm = (center * inverse).astype(bf16)
            hidden_inv[layer, at, :] = inverse
            normed[layer, at, :] = norm
            for part in range(4):
                columns = slice(part * width, part * width + width)
                pre = matmul(norm, weights[layer, :, columns])
                logistic = 0.5 + 0.5 * jnp.tanh(0.5 * pre)
                act = pre * logistic
                slope[layer, at, columns] = (logistic + act - act * logistic).astype(bf16)
                act = act.astype(bf16)
                if part == 0:
                    gate[layer, at, :] = act
                elif part == 2:
                    queries[layer, at, :] = act * jnp.asarray(0.0625, bf16)
                else:
                    store = value_heads if part == 1 else key_heads
                    for head in range(heads):
                        spot = rows(index * heads + head)
                        store[layer, spot, :] = act * head_mask[head : head + 1, :]
            return carry

        for at_index in range(0, blocks):
            project(at_index, 0)

        def scores(query, key, masked):
            pair = pair_of(query, key)
            query_part = queries[layer, rows(query), :]
            one = jnp.asarray(1.0, bf16)
            if masked:
                visible = lax.broadcasted_iota(
                    jnp.int32, (block, block), 1
                ) <= lax.broadcasted_iota(jnp.int32, (block, block), 0)
            parts = []
            for head in range(heads):
                spot = rows(key * heads + head)
                half = matmul_nt(query_part, key_heads[layer, spot, :]).astype(bf16)
                bend = jnp.tanh(half)
                lift = one + bend
                if masked:
                    lift = jnp.where(visible, lift, jnp.zeros_like(lift))
                columns = slice(head * block, head * block + block)
                part = half * lift
                parts.append(part)
                attn[layer, pair, :, columns] = part
                score_slope[layer, pair, :, columns] = lift * (one + (half - half * bend))
            return matmul(
                jnp.concatenate(parts, axis=1), value_heads[layer, head_rows(key), :]
            )

        def attend_rows(query, carry):
            mixture[...] = scores(query, query, True)

            def before(key, carry):
                mixture[...] += scores(query, key, False)
                return carry

            for at_index in range(0, query):
                before(at_index, 0)
            at = rows(query)
            value = mixture[...]
            center = value - jnp.mean(value, axis=1, keepdims=True)
            inverse = lax.rsqrt(jnp.mean(center * center, axis=1, keepdims=True) + EPSILON)
            norm = center * inverse
            mix_normed[layer, at, :] = norm
            mix_inv[layer, at, :] = inverse
            gated_part = (norm * gate[layer, at, :].astype(f32)).astype(bf16)
            gated[layer, at, :] = gated_part

            branch = matmul(gated_part, weights[layer, :, 4 * width :])
            following = lax.rem(layer + 1, layer_count)
            hidden[following, at, :] = (hidden[layer, at, :].astype(f32) + branch).astype(bf16)
            return carry

        for at_index in range(0, blocks):
            attend_rows(at_index, 0)
        return carry

    lax.fori_loop(0, layer_count, forward, 0)

    cotangent_load.wait()
    gradient[...] = cotangent_ref[...].astype(f32)

    in_flight = {}

    def send(name, layer, number, source, place, where):
        copy = pltpu.make_async_remote_copy(
            src_ref=source,
            dst_ref=place,
            send_sem=reduce_send.at[layer, number],
            recv_sem=reduce_recv.at[layer, number],
            device_id=where,
            device_id_type=MESH,
        )
        copy.start()
        in_flight.setdefault((name, layer), []).append(copy)

    def receive(name, layer):
        for copy in in_flight[name, layer]:
            copy.wait()

    def reduce_pair(layer):
        where = (z_at * 2 + 1 - core, emb_at)
        send("pair", layer, 0, grads.at[layer, 1 - core], pair_in.at[layer], where)

    def reduce_z(layer):
        receive("pair", layer)
        for z in range(4):
            pair_in[layer, z] = (
                grads[layer, core, z].astype(f32) + pair_in[layer, z].astype(f32)
            ).astype(bf16)
        for k in range(3):
            to = lax.rem(z_at + k + 1, 4)
            where = (to * 2 + core, emb_at)
            send("z", layer, 1 + k, pair_in.at[layer, to], z_in.at[layer, k], where)

    def reduce_x():
        for layer in range(layer_count):
            receive("z", layer)
        half = z_sum.shape[3]
        for layer in range(layer_count):
            for part in range(4):
                spot = slice(part // 2 * 16, part // 2 * 16 + 16)
                span = slice(part % 2 * half, part % 2 * half + half)
                value = pair_in[layer, z_at, spot, span].astype(f32)
                for k in range(3):
                    value += z_in[layer, k, spot, span].astype(f32)
                z_sum[layer, part] = value.astype(bf16)
        for k in range(3):
            to = lax.rem(x_at + k + 1, 4)
            where = (fsdp_at, y_at * 4 + to)
            send("x", 0, 4 + k, z_sum.at[:, to], x_in.at[:, k], where)

    def reduce_y():
        receive("x", 0)
        for layer in range(layer_count):
            value = z_sum[layer, x_at].astype(f32)
            for k in range(3):
                value += x_in[layer, k].astype(f32)
            y_all[layer, y_at] = value.astype(bf16)
        for k in range(3):
            to = lax.rem(y_at + k + 1, 4)
            where = (fsdp_at, to * 4 + x_at)
            send("y", 0, 7 + k, y_all.at[:, y_at], y_all.at[:, y_at], where)

    def reduce_g():
        receive("y", 0)
        for layer in range(layer_count):
            value = y_all[layer, 0].astype(f32)
            for y in range(1, 4):
                value += y_all[layer, y].astype(f32)
            total_ref[layer, x_at] = value.astype(bf16)
        for k in range(3):
            to = lax.rem(x_at + k + 1, 4)
            where = (fsdp_at, y_at * 4 + to)
            place = total_ref.at[:, x_at]
            send("g", 0, 10 + k, place, place, where)

    def backward(layer, between):

        def through_gate(index, carry):
            at = rows(index)
            grad_round = gradient[at, :].astype(bf16)
            grad_gated = matmul_nt(grad_round, weights[layer, :, 4 * width :])
            norm = mix_normed[layer, at, :]
            first = slope[layer, at, :width].astype(f32)
            grad_pre[at, :width] = (grad_gated * norm * first).astype(bf16)
            inner = grad_gated * gate[layer, at, :].astype(f32)
            grad = mix_inv[layer, at, :] * (
                inner
                - jnp.mean(inner, axis=1, keepdims=True)
                - norm * jnp.mean(inner * norm, axis=1, keepdims=True)
            )
            grad_mix[at, :] = grad.astype(bf16)
            grad_mix_t[:, at] = grad.T.astype(bf16)
            normed_t[:, at] = normed[layer, at, :].T
            queries_t[:, at] = queries[layer, at, :].T
            return carry

        for at_index in range(0, blocks):
            through_gate(at_index, 0)
        between[0]()

        gw_out = lax.dot_general(
            gated[layer],
            gradient[...].astype(bf16),
            (((0,), (0,)), ((), ())),
            preferred_element_type=jnp.float32,
        ).astype(bf16)
        depth = grads.shape[3]
        for part in range(8):
            grads[layer, part % 2, part // 2, :, 4 * width :] = gw_out[
                part * depth : part * depth + depth
            ]

        keys_t[...] = jnp.zeros_like(keys_t)
        values_t[...] = jnp.zeros_like(values_t)

        def through_scores(query, carry):
            mixture[...] = jnp.zeros_like(mixture)

            def one(key, carry):
                pair = pair_of(query, key)
                here = rows(query)
                there = rows(key)
                grad_part = grad_mix[here, :]
                parts = []
                for head in range(heads):
                    spot = rows(key * heads + head)
                    columns = slice(head * block, head * block + block)
                    lines = slice(head * DH, head * DH + DH)
                    grad = matmul_nt(grad_part, value_heads[layer, spot, :]).astype(bf16)
                    values_t[lines, there] += matmul(
                        grad_mix_t[lines, here], attn[layer, pair, :, columns]
                    )
                    part = grad * score_slope[layer, pair, :, columns]
                    parts.append(part)
                    keys_t[lines, there] += matmul(queries_t[lines, here], part)
                mixture[...] += matmul(
                    jnp.concatenate(parts, axis=1), key_heads[layer, head_rows(key), :]
                )
                return carry

            for at_index in range(0, query + 1):
                one(at_index, 0)
            at = rows(query)
            third = slope[layer, at, 2 * width : 3 * width].astype(f32)
            grad_pre[at, 2 * width : 3 * width] = (mixture[...] * 0.0625 * third).astype(bf16)
            return carry

        for at_index in range(0, blocks):
            through_scores(at_index, 0)
        between[1]()

        def through_keys(key, carry):
            at = rows(key)
            for part, total in ((1, values_t), (3, keys_t)):
                span = slice(part * width, part * width + width)
                grad_pre[at, span] = (total[:, at].T * slope[layer, at, span].astype(f32)).astype(
                    bf16
                )
            return carry

        for at_index in range(0, blocks):
            through_keys(at_index, 0)
        between[2]()

        for part in range(4):
            span = slice(part * width, part * width + width)
            gw_proj = matmul(normed_t[...], grad_pre[:, span]).astype(bf16)
            for piece in range(8):
                grads[layer, piece % 2, piece // 2, :, span] = gw_proj[
                    piece * depth : piece * depth + depth
                ]

        reduce_pair(layer)
        between[3]()

        def through_norm(index, carry):
            at = rows(index)
            grad_normed = matmul_nt(grad_pre[at, :], weights[layer, :, : 4 * width])
            norm = normed[layer, at, :].astype(f32)
            gradient[at, :] = gradient[at, :] + hidden_inv[layer, at, :] * (
                grad_normed
                - jnp.mean(grad_normed, axis=1, keepdims=True)
                - norm * jnp.mean(grad_normed * norm, axis=1, keepdims=True)
            )
            return carry

        for at_index in range(0, blocks):
            through_norm(at_index, 0)
    def nothing():
        pass

    backward(1, (nothing, nothing, nothing, nothing))
    backward(0, (lambda: reduce_z(1), nothing, nothing, nothing))


    reduce_z(0)

    def give_back(index):
        at = pl.ds(index * 128, 128)
        total = jnp.zeros((128, width), f32)
        for first in range(0, length, 256):
            spot = lax.broadcasted_iota(jnp.int32, (128, 256), 0) + index * 128
            pick = (spot == target_ref[:, first : first + 256]).astype(f32).astype(bf16)
            total += matmul(pick, gradient[first : first + 256, :].astype(bf16))
        found[at, :] = total.astype(bf16)

    for at_index in range(slots // 128):
        give_back(at_index)

    def send_grads(step, carry):
        other = lax.rem(me + step, owners)
        pltpu.make_async_remote_copy(
            src_ref=found.at[pl.ds(other * capacity, capacity)],
            dst_ref=incoming_ref.at[pl.ds(me * capacity, capacity)],
            send_sem=grad_send,
            recv_sem=grad_recv,
            device_id=device_of(other, emb_count),
            device_id_type=MESH,
        ).start()
        return carry

    lax.fori_loop(1, 17, send_grads, 0)
    reduce_x()
    lax.fori_loop(17, 49, send_grads, 0)
    reduce_y()
    lax.fori_loop(49, 89, send_grads, 0)
    reduce_g()
    lax.fori_loop(89, owners, send_grads, 0)
    incoming_ref[own, :] = found[own, :]
    receive("g", 0)
    pltpu.make_async_copy(found.at[lines], found.at[lines], grad_send).wait()
    pltpu.make_async_copy(incoming_ref.at[lines], incoming_ref.at[lines], grad_recv).wait()


def run_step(owner, offset, w_proj, w_out, table, cotangent, owners, emb_count, capacity):
    f32, bf16, i32 = jnp.float32, jnp.bfloat16, jnp.int32
    layer_count, depth, split = w_proj.shape
    columns = split + w_out.shape[2]
    length, width = cotangent.shape
    slots = owners * capacity
    blocks = length // 256
    pairs = blocks * (blocks + 1) // 2
    heads = width // DH
    two = layer_count
    vmem = pl.BlockSpec(memory_space=pltpu.VMEM)
    sem = pltpu.SemaphoreType.DMA
    scratch = [
        ((1, length), i32),
        ((1, length), i32),
        (w_proj.shape, bf16),
        (w_out.shape, bf16),
        ((length, width), bf16),
        ((slots, width), bf16),
        ((1, length), i32),
        ((two, 4, 2, depth, columns), bf16),
        ((owners, length), bf16),
        ((owners, 1, 128), i32),
        ((owners, 1, 128), i32),
        ((slots, width), bf16),
        ((two, length, width), bf16),
        ((two, length, 1), f32),
        ((two, length, width), bf16),
        ((two, length, split), bf16),
        ((two, length, width), bf16),
        ((two, length, width), bf16),
        ((two, length * heads, width), bf16),
        ((two, length * heads, width), bf16),
        ((two, pairs, 256, 256 * heads), bf16),
        ((two, pairs, 256, 256 * heads), bf16),
        ((two, length, width), f32),
        ((two, length, 1), f32),
        ((two, length, width), bf16),
        ((length, width), f32),
        ((256, width), f32),
        ((length, width), bf16),
        ((length, split), bf16),
        ((width, length), bf16),
        ((width, length), bf16),
        ((width, length), bf16),
        ((width, length), f32),
        ((width, length), f32),
        ((two, 2, 4, depth, columns), bf16),
        ((two, 4, depth, columns), bf16),
        ((two, 3, depth, columns), bf16),
        ((two, 4, 16, columns // 2), bf16),
        ((two, 3, 16, columns // 2), bf16),
        ((two, 4, 16, columns // 2), bf16),
    ]
    return pl.pallas_call(
        functools.partial(step_kernel, owners, emb_count, capacity),
        out_shape=(
            jax.ShapeDtypeStruct((slots, width), bf16),
            jax.ShapeDtypeStruct((1, slots), i32),
            jax.ShapeDtypeStruct((two, 4, 16, columns // 2), bf16),
        ),
        in_specs=[pl.BlockSpec(memory_space=pl.ANY)] * 6,
        out_specs=(vmem,) * 3,
        scratch_shapes=[pltpu.VMEM(*one) for one in scratch]
        + [sem((9,))]
        + [sem] * 6
        + [sem((3,)), sem((3,)), sem((4,)), sem((4,)), sem((two, 13)), sem((two, 13))],
        compiler_params=pltpu.CompilerParams(
            collective_id=1, has_side_effects=True, vmem_limit_bytes=62 << 20
        ),
        name="step",
    )(owner, offset, w_proj, w_out, table, cotangent)


def update_kernel(
    block, scale, table_ref, requested_ref, stale_ref, incoming_ref, total_ref, new_ref, proj_ref, out_ref
):
    @pl.when(pl.program_id(0) == 0)
    def _():
        half = total_ref.shape[3]
        split = proj_ref.shape[2]
        for part in range(4):
            spot = slice(part // 2 * 16, part // 2 * 16 + 16)
            value = total_ref[:, part].astype(jnp.float32) * scale
            if part % 2 == 0:
                proj_ref[:, spot, :half] = value
            else:
                proj_ref[:, spot, half:] = value[:, :, : split - half]
                out_ref[:, spot, :] = value[:, :, split - half :]

    count = requested_ref.shape[1]
    first = pl.program_id(0) * block
    row = first + lax.broadcasted_iota(jnp.int32, (block, count), 0)
    pick = (row == requested_ref[...]).astype(jnp.float32).astype(jnp.bfloat16)
    grad = jnp.dot(pick, incoming_ref[...], preferred_element_type=jnp.float32)
    rate = 0.5 / (1.0 + stale_ref[...].astype(jnp.float32))
    same = lax.broadcasted_iota(jnp.int32, (128, 128), 0) == lax.broadcasted_iota(
        jnp.int32, (128, 128), 1
    )
    for part in range(block // 128):
        rows = slice(part * 128, part * 128 + 128)
        spread = jnp.where(same, rate[0, part : part + 1, :], 0.0)
        column = jnp.sum(spread, axis=1, keepdims=True)
        new_ref[rows, :] = table_ref[rows, :] - column * grad[rows, :]


def update_table(table, requested, staleness, incoming, total, scale):
    rows, width = table.shape
    block = 1024
    count = incoming.shape[0]
    parts = block // 128
    layer_count, _, depth, half = total.shape
    depth *= 2
    split = 2 * half - width
    whole = lambda *dims: pl.BlockSpec(dims, lambda i: (0,) * len(dims))
    return pl.pallas_call(
        functools.partial(update_kernel, block, scale),
        out_shape=(
            jax.ShapeDtypeStruct(table.shape, jnp.float32),
            jax.ShapeDtypeStruct((layer_count, depth, split), jnp.float32),
            jax.ShapeDtypeStruct((layer_count, depth, width), jnp.float32),
        ),
        grid=(rows // block,),
        in_specs=[
            pl.BlockSpec((block, width), lambda i: (i, 0)),
            whole(1, count),
            pl.BlockSpec((1, parts, 128), lambda i: (i, 0, 0)),
            whole(count, width),
            whole(*total.shape),
        ],
        out_specs=(
            pl.BlockSpec((block, width), lambda i: (i, 0)),
            whole(layer_count, depth, split),
            whole(layer_count, depth, width),
        ),
        compiler_params=pltpu.CompilerParams(vmem_limit_bytes=58 << 20),
        name="update_table",
    )(
        table,
        requested,
        staleness.reshape(rows // block, parts, 128),
        incoming,
        total,
    )


def local(item_table, item_owner, item_row, staleness, w_proj, w_out, out_grad):
    emb_count = lax.axis_size("emb")
    owners = lax.axis_size("fsdp") * emb_count
    length = item_row.shape[1]
    capacity = 2 * length // owners
    incoming, requested, total = run_step(
        item_owner.reshape(1, length),
        item_row,
        w_proj,
        w_out,
        item_table,
        out_grad[0],
        owners,
        emb_count,
        capacity,
    )
    norm_scale = (owners * length) ** (-0.5)
    return update_table(item_table, requested, staleness, incoming, total, norm_scale)


def solution(mesh):
    return jax.shard_map(
        local,
        mesh=mesh,
        in_specs=(
            P(("fsdp", "emb"), None),
            P(("fsdp", "emb"), None, None),
            P(("fsdp", "emb"), None),
            P(("fsdp", "emb")),
            P(None, "fsdp", None),
            P(None, "fsdp", None),
            P(("fsdp", "emb"), None, None),
        ),
        out_specs=(P(("fsdp", "emb"), None), P(None, "fsdp", None), P(None, "fsdp", None)),
        check_vma=False,
    )
```

```python
import functools

import jax
import jax.numpy as jnp
from jax import lax
from jax.experimental import pallas as pl
from jax.experimental.pallas import tpu as pltpu
from jax.sharding import PartitionSpec as P

MESH = pl.DeviceIdType.MESH

DH = 64


EPSILON = 1e-05


NT = (((1,), (1,)), ((), ()))


def matmul(left, right):
    return jnp.dot(left, right, preferred_element_type=jnp.float32)


def matmul_nt(left, right):
    return lax.dot_general(left, right, NT, preferred_element_type=jnp.float32)


def to_column(row):
    same = lax.broadcasted_iota(jnp.int32, (128, 128), 0) == lax.broadcasted_iota(
        jnp.int32, (128, 128), 1
    )
    parts = [
        jnp.sum(jnp.where(same, row[:, at : at + 128], 0.0), axis=1, keepdims=True)
        for at in range(0, row.shape[1], 128)
    ]
    return parts[0] if len(parts) == 1 else jnp.concatenate(parts, axis=0)


def device_of(index, emb_count):
    return (index // emb_count, lax.rem(index, emb_count))


def greet(me, owners, emb_count):
    barrier = pltpu.get_barrier_semaphore()

    def hello(step, carry):
        other = lax.rem(me + step, owners)
        pl.semaphore_signal(
            barrier, inc=1, device_id=device_of(other, emb_count), device_id_type=MESH
        )
        return carry

    lax.fori_loop(1, owners, hello, 0)
    return barrier


def step_kernel(
    owners,
    emb_count,
    capacity,
    owner_hbm,
    offset_hbm,
    proj_hbm,
    out_hbm,
    table_hbm,
    cotangent_hbm,
    incoming_ref,
    requested_ref,
    total_ref,
    owner_ref,
    offset_ref,
    proj_ref,
    out_ref,
    cotangent_ref,
    returned_ref,
    target_ref,
    weights_ref,
    member,
    ask,
    asked_ref,
    found,
    hidden,
    hidden_inv,
    normed,
    slope,
    gate,
    queries,
    key_heads,
    value_heads,
    attn,
    score_slope,
    mix_normed,
    mix_inv,
    gated,
    gradient,
    mixture,
    grad_mix,
    grad_pre,
    grad_mix_t,
    normed_t,
    queries_t,
    keys_t,
    values_t,
    grads,
    pair_in,
    z_in,
    z_sum,
    x_in,
    y_all,
    load_sems,
    ask_send,
    ask_recv,
    row_send,
    row_recv,
    grad_send,
    grad_recv,
    z_send,
    z_recv,
    pair_send,
    pair_recv,
    reduce_send,
    reduce_recv,
):
    f32, bf16 = jnp.float32, jnp.bfloat16
    fsdp_at = lax.axis_index("fsdp")
    emb_at = lax.axis_index("emb")
    me = fsdp_at * emb_count + emb_at
    z_at = fsdp_at // 2
    core = lax.rem(fsdp_at, 2)
    y_at = emb_at // 4
    x_at = lax.rem(emb_at, 4)
    barrier = greet(me, owners, emb_count)
    loads = []
    for number, (source, place) in enumerate(
        ((owner_hbm, owner_ref), (offset_hbm, offset_ref), (proj_hbm, proj_ref), (out_hbm, out_ref))
    ):
        load = pltpu.make_async_copy(source, place, load_sems.at[number])
        load.start()
        loads.append(load)
    chunk = gradient.shape[0]
    wide = (gradient, mix_normed.at[0], mix_normed.at[1], gradient)
    table_loads = [
        pltpu.make_async_copy(
            table_hbm.at[pl.ds(number * chunk, chunk)], wide[number], load_sems.at[4 + number]
        )
        for number in range(4)
    ]
    for number in range(3):
        table_loads[number].start()
    cotangent_load = pltpu.make_async_copy(cotangent_hbm, cotangent_ref, load_sems.at[8])
    cotangent_load.start()
    for load in loads:
        load.wait()

    split = proj_ref.shape[2]
    weights_ref[:, z_at, core, :, :split] = proj_ref[...]
    weights_ref[:, z_at, core, :, split:] = out_ref[...]

    length = owner_ref.shape[1]
    owner = owner_ref[...]
    value = offset_ref[...] + 1
    high = (value // 64).astype(f32)
    low = lax.rem(value, 64).astype(f32)
    row_at = lax.broadcasted_iota(jnp.int32, (owners, 256), 0)
    for at in range(0, length, 256):
        member[:, at : at + 256] = (
            (row_at == owner[:, at : at + 256]).astype(f32).astype(bf16)
        )
    slots = []
    for at in range(0, length, 256):
        earlier = jnp.zeros((owners, 256), f32)
        for first in range(0, at + 256, 256):
            before = (
                lax.broadcasted_iota(jnp.int32, (256, 256), 0) + (first - at)
                < lax.broadcasted_iota(jnp.int32, (256, 256), 1)
            )
            earlier += matmul(member[:, first : first + 256], before.astype(f32).astype(bf16))
        slots.append(
            jnp.sum(earlier * member[:, at : at + 256].astype(f32), axis=0, keepdims=True)
        )
    slot = jnp.concatenate(slots, axis=1)
    target_ref[...] = owner * capacity + slot.astype(jnp.int32)
    here = lax.broadcasted_iota(jnp.int32, (128, length), 0).astype(f32) == slot
    request = 64.0 * matmul_nt(member[...], jnp.where(here, high, 0.0).astype(bf16))
    request += matmul_nt(member[...], jnp.where(here, low, 0.0).astype(bf16))
    ask[...] = request.astype(jnp.int32).reshape(ask.shape)

    pl.semaphore_wait(barrier, owners - 1)

    def send_ask(step, carry):
        other = lax.rem(me + step, owners)
        pltpu.make_async_remote_copy(
            src_ref=ask.at[other],
            dst_ref=asked_ref.at[me],
            send_sem=ask_send,
            recv_sem=ask_recv,
            device_id=device_of(other, emb_count),
            device_id_type=MESH,
        ).start()
        return carry

    lax.fori_loop(1, owners, send_ask, 0)
    z_copies = []
    for k in range(3):
        to = lax.rem(z_at + k + 1, 4)
        copy = pltpu.make_async_remote_copy(
            src_ref=weights_ref.at[:, z_at, core],
            dst_ref=weights_ref.at[:, z_at, core],
            send_sem=z_send.at[k],
            recv_sem=z_recv.at[k],
            device_id=(to * 2 + core, emb_at),
            device_id_type=MESH,
        )
        copy.start()
        z_copies.append(copy)
    asked_ref[me] = ask[me]

    table = key_heads.at[1]
    table_rows = table.shape[0]
    for number in range(4):
        table_loads[number].wait()

        def narrow(index, carry):
            at = pl.ds(pl.multiple_of(index * 256, 256), 256)
            to = pl.ds(pl.multiple_of(index * 256 + number * chunk, 256), 256)
            table[to, :] = wide[number][at, :].astype(bf16)
            return carry

        lax.fori_loop(0, chunk // 256, narrow, 0)
        if number == 0:
            table_loads[3].start()

    others = pl.ds(0, owners - 1)
    pltpu.make_async_copy(ask.at[others], ask.at[others], ask_send).wait()
    pltpu.make_async_copy(asked_ref.at[others], asked_ref.at[others], ask_recv).wait()

    group = 256 // capacity
    groups = owners // group

    def find(step, carry):
        index = lax.rem(me // group + step, groups)
        first_user = index * group
        wanted = asked_ref[pl.ds(first_user, group)].astype(f32)
        wanted = jnp.broadcast_to(wanted, (group, capacity, 128))
        same = lax.broadcasted_iota(jnp.int32, wanted.shape, 1) == lax.broadcasted_iota(
            jnp.int32, wanted.shape, 2
        )
        column = jnp.sum(jnp.where(same, wanted, 0.0), axis=2, keepdims=True)
        column = column.reshape(256, 1) - 1.0
        diagonal = lax.broadcasted_iota(jnp.int32, (256, 256), 0) == lax.broadcasted_iota(
            jnp.int32, (256, 256), 1
        )
        span = pl.ds(pl.multiple_of(index * 256, 256), 256)
        line = jnp.sum(jnp.where(diagonal, column, 0.0), axis=0, keepdims=True)
        requested_ref[:, span] = line.astype(jnp.int32)
        lane = lax.broadcasted_iota(jnp.int32, (256, 256), 1).astype(f32)
        total = jnp.zeros((256, table.shape[1]), f32)
        for first in range(0, table_rows, 256):
            pick = (lane + float(first) == column).astype(f32).astype(bf16)
            total += matmul(pick, table[first : first + 256, :])
        found[pl.ds(pl.multiple_of(index * 256, 256), 256), :] = total.astype(bf16)

        def send_rows(turn, carry):
            user = first_user + lax.rem(me + turn, group)

            @pl.when(user != me)
            def _():
                pltpu.make_async_remote_copy(
                    src_ref=found.at[pl.ds(user * capacity, capacity)],
                    dst_ref=returned_ref.at[pl.ds(me * capacity, capacity)],
                    send_sem=row_send,
                    recv_sem=row_recv,
                    device_id=device_of(user, emb_count),
                    device_id_type=MESH,
                ).start()

            return carry

        lax.fori_loop(0, group, send_rows, 0)
        return carry

    lax.fori_loop(0, groups, find, 0)
    picks = attn.at[0]
    across = picks.shape[2]
    all_slots = owners * capacity
    halves = all_slots // across
    for part in range(length // 256):
        place = to_column(target_ref[:, part * 256 : part * 256 + 256].astype(f32))
        for first in range(0, all_slots, 256):
            lane = lax.broadcasted_iota(jnp.int32, (256, 256), 1).astype(f32) + float(first)
            span = slice(first % across, first % across + 256)
            picks[part * halves + first // across, :, span] = (
                (lane == place).astype(f32).astype(bf16)
            )
    own = pl.ds(pl.multiple_of(me * capacity, capacity), capacity)
    returned_ref[own, :] = found[own, :]

    for copy in z_copies:
        copy.wait()
    pair_copies = []
    for z in range(4):
        copy = pltpu.make_async_remote_copy(
            src_ref=weights_ref.at[:, z, core],
            dst_ref=weights_ref.at[:, z, core],
            send_sem=pair_send.at[z],
            recv_sem=pair_recv.at[z],
            device_id=(z_at * 2 + 1 - core, emb_at),
            device_id_type=MESH,
        )
        copy.start()
        pair_copies.append(copy)
    for copy in pair_copies:
        copy.wait()
    lines = pl.ds(0, (owners - 1) * capacity)
    pltpu.make_async_copy(found.at[lines], found.at[lines], row_send).wait()
    pltpu.make_async_copy(returned_ref.at[lines], returned_ref.at[lines], row_recv).wait()

    block = 256
    width = cotangent_ref.shape[1]
    blocks = length // block
    heads = width // DH
    slots = returned_ref.shape[0]
    layer_count = weights_ref.shape[0]
    head_of = lax.broadcasted_iota(jnp.int32, (heads, width), 1) // DH
    head_mask = (head_of == lax.broadcasted_iota(jnp.int32, (heads, width), 0)).astype(f32)
    head_mask = head_mask.astype(bf16)

    weights = weights_ref.reshape(layer_count, width, 5 * width)

    def rows(index):
        if isinstance(index, int):
            return pl.ds(index * block, block)
        return pl.ds(pl.multiple_of(index * block, block), block)

    def head_rows(index):
        if isinstance(index, int):
            return pl.ds(index * block * heads, block * heads)
        return pl.ds(pl.multiple_of(index * block * heads, block * heads), block * heads)

    def pair_of(query, key):
        return query * (query + 1) // 2 + key

    def fetch(part, carry):
        total = jnp.zeros((256, width), f32)
        for half in range(halves):
            total += matmul(
                picks[part * halves + half], returned_ref[half * across : half * across + across, :]
            )
        hidden[0, rows(part), :] = total.astype(bf16)
        return carry

    lax.fori_loop(0, length // 256, fetch, 0)

    def forward(layer, carry):
        def project(index, carry):
            at = rows(index)
            value = hidden[layer, at, :].astype(f32)
            center = value - jnp.mean(value, axis=1, keepdims=True)
            inverse = lax.rsqrt(jnp.mean(center * center, axis=1, keepdims=True) + EPSILON)
            norm = (center * inverse).astype(bf16)
            hidden_inv[layer, at, :] = inverse
            normed[layer, at, :] = norm
            for part in range(4):
                columns = slice(part * width, part * width + width)
                pre = matmul(norm, weights[layer, :, columns])
                logistic = 0.5 + 0.5 * jnp.tanh(0.5 * pre)
                act = (pre * logistic).astype(bf16)
                logistic = logistic.astype(bf16)
                slope[layer, at, columns] = logistic + (act - act * logistic)
                if part == 0:
                    gate[layer, at, :] = act
                elif part == 2:
                    queries[layer, at, :] = act * jnp.asarray(0.0625, bf16)
                else:
                    store = value_heads if part == 1 else key_heads
                    for head in range(heads):
                        spot = rows(index * heads + head)
                        store[layer, spot, :] = act * head_mask[head : head + 1, :]
            return carry

        for at_index in range(0, blocks):
            project(at_index, 0)

        def scores(query, key, masked):
            pair = pair_of(query, key)
            query_part = queries[layer, rows(query), :]
            one = jnp.asarray(1.0, bf16)
            if masked:
                visible = lax.broadcasted_iota(
                    jnp.int32, (block, block), 1
                ) <= lax.broadcasted_iota(jnp.int32, (block, block), 0)
            parts = []
            for head in range(heads):
                spot = rows(key * heads + head)
                half = matmul_nt(query_part, key_heads[layer, spot, :]).astype(bf16)
                bend = jnp.tanh(half)
                lift = one + bend
                if masked:
                    lift = jnp.where(visible, lift, jnp.zeros_like(lift))
                columns = slice(head * block, head * block + block)
                part = half * lift
                parts.append(part)
                attn[layer, pair, :, columns] = part
                score_slope[layer, pair, :, columns] = lift * (one + (half - half * bend))
            return matmul(
                jnp.concatenate(parts, axis=1), value_heads[layer, head_rows(key), :]
            )

        def attend_rows(query, carry):
            mixture[...] = scores(query, query, True)

            def before(key, carry):
                mixture[...] += scores(query, key, False)
                return carry

            for at_index in range(0, query):
                before(at_index, 0)
            at = rows(query)
            value = mixture[...]
            center = value - jnp.mean(value, axis=1, keepdims=True)
            inverse = lax.rsqrt(jnp.mean(center * center, axis=1, keepdims=True) + EPSILON)
            norm = center * inverse
            mix_normed[layer, at, :] = norm
            mix_inv[layer, at, :] = inverse
            gated_part = (norm * gate[layer, at, :].astype(f32)).astype(bf16)
            gated[layer, at, :] = gated_part

            branch = matmul(gated_part, weights[layer, :, 4 * width :])
            following = lax.rem(layer + 1, layer_count)
            hidden[following, at, :] = (hidden[layer, at, :].astype(f32) + branch).astype(bf16)
            return carry

        for at_index in range(0, blocks):
            attend_rows(at_index, 0)
        return carry

    lax.fori_loop(0, layer_count, forward, 0)

    cotangent_load.wait()
    gradient[...] = cotangent_ref[...].astype(f32)

    in_flight = {}

    def send(name, layer, number, source, place, where):
        copy = pltpu.make_async_remote_copy(
            src_ref=source,
            dst_ref=place,
            send_sem=reduce_send.at[layer, number],
            recv_sem=reduce_recv.at[layer, number],
            device_id=where,
            device_id_type=MESH,
        )
        copy.start()
        in_flight.setdefault((name, layer), []).append(copy)

    def receive(name, layer):
        for copy in in_flight[name, layer]:
            copy.wait()

    def reduce_pair(layer):
        where = (z_at * 2 + 1 - core, emb_at)
        send("pair", layer, 0, grads.at[layer, 1 - core], pair_in.at[layer], where)

    def reduce_z(layer):
        receive("pair", layer)
        for z in range(4):
            pair_in[layer, z] = (
                grads[layer, core, z].astype(f32) + pair_in[layer, z].astype(f32)
            ).astype(bf16)
        for k in range(3):
            to = lax.rem(z_at + k + 1, 4)
            where = (to * 2 + core, emb_at)
            send("z", layer, 1 + k, pair_in.at[layer, to], z_in.at[layer, k], where)

    def reduce_x():
        for layer in range(layer_count):
            receive("z", layer)
        half = z_sum.shape[3]
        for layer in range(layer_count):
            for part in range(4):
                spot = slice(part // 2 * 16, part // 2 * 16 + 16)
                span = slice(part % 2 * half, part % 2 * half + half)
                value = pair_in[layer, z_at, spot, span].astype(f32)
                for k in range(3):
                    value += z_in[layer, k, spot, span].astype(f32)
                z_sum[layer, part] = value.astype(bf16)
        for k in range(3):
            to = lax.rem(x_at + k + 1, 4)
            where = (fsdp_at, y_at * 4 + to)
            send("x", 0, 4 + k, z_sum.at[:, to], x_in.at[:, k], where)

    def reduce_y():
        receive("x", 0)
        for layer in range(layer_count):
            value = z_sum[layer, x_at].astype(f32)
            for k in range(3):
                value += x_in[layer, k].astype(f32)
            y_all[layer, y_at] = value.astype(bf16)
        for k in range(3):
            to = lax.rem(y_at + k + 1, 4)
            where = (fsdp_at, to * 4 + x_at)
            send("y", 0, 7 + k, y_all.at[:, y_at], y_all.at[:, y_at], where)

    def reduce_g():
        receive("y", 0)
        for layer in range(layer_count):
            value = y_all[layer, 0].astype(f32)
            for y in range(1, 4):
                value += y_all[layer, y].astype(f32)
            total_ref[layer, x_at] = value.astype(bf16)
        for k in range(3):
            to = lax.rem(x_at + k + 1, 4)
            where = (fsdp_at, y_at * 4 + to)
            place = total_ref.at[:, x_at]
            send("g", 0, 10 + k, place, place, where)

    def backward(layer, between):

        def through_gate(index, carry):
            at = rows(index)
            grad_round = gradient[at, :].astype(bf16)
            grad_gated = matmul_nt(grad_round, weights[layer, :, 4 * width :])
            norm = mix_normed[layer, at, :]
            first = slope[layer, at, :width].astype(f32)
            grad_pre[at, :width] = (grad_gated * norm * first).astype(bf16)
            inner = grad_gated * gate[layer, at, :].astype(f32)
            grad = mix_inv[layer, at, :] * (
                inner
                - jnp.mean(inner, axis=1, keepdims=True)
                - norm * jnp.mean(inner * norm, axis=1, keepdims=True)
            )
            grad_mix[at, :] = grad.astype(bf16)
            grad_mix_t[:, at] = grad.T.astype(bf16)
            normed_t[:, at] = normed[layer, at, :].T
            queries_t[:, at] = queries[layer, at, :].T
            return carry

        for at_index in range(0, blocks):
            through_gate(at_index, 0)
        between[0]()

        gw_out = lax.dot_general(
            gated[layer],
            gradient[...].astype(bf16),
            (((0,), (0,)), ((), ())),
            preferred_element_type=jnp.float32,
        ).astype(bf16)
        depth = grads.shape[3]
        for part in range(8):
            grads[layer, part % 2, part // 2, :, 4 * width :] = gw_out[
                part * depth : part * depth + depth
            ]

        keys_t[...] = jnp.zeros_like(keys_t)
        values_t[...] = jnp.zeros_like(values_t)

        def through_scores(query, carry):
            mixture[...] = jnp.zeros_like(mixture)

            def one(key, carry):
                pair = pair_of(query, key)
                here = rows(query)
                there = rows(key)
                grad_part = grad_mix[here, :]
                parts = []
                for head in range(heads):
                    spot = rows(key * heads + head)
                    columns = slice(head * block, head * block + block)
                    lines = slice(head * DH, head * DH + DH)
                    grad = matmul_nt(grad_part, value_heads[layer, spot, :]).astype(bf16)
                    values_t[lines, there] += matmul(
                        grad_mix_t[lines, here], attn[layer, pair, :, columns]
                    )
                    part = grad * score_slope[layer, pair, :, columns]
                    parts.append(part)
                    keys_t[lines, there] += matmul(queries_t[lines, here], part)
                mixture[...] += matmul(
                    jnp.concatenate(parts, axis=1), key_heads[layer, head_rows(key), :]
                )
                return carry

            for at_index in range(0, query + 1):
                one(at_index, 0)
            at = rows(query)
            third = slope[layer, at, 2 * width : 3 * width].astype(f32)
            grad_pre[at, 2 * width : 3 * width] = (mixture[...] * 0.0625 * third).astype(bf16)
            return carry

        for at_index in range(0, blocks):
            through_scores(at_index, 0)
        between[1]()

        def through_keys(key, carry):
            at = rows(key)
            for part, total in ((1, values_t), (3, keys_t)):
                span = slice(part * width, part * width + width)
                grad_pre[at, span] = (total[:, at].T * slope[layer, at, span].astype(f32)).astype(
                    bf16
                )
            return carry

        for at_index in range(0, blocks):
            through_keys(at_index, 0)
        between[2]()

        for part in range(4):
            span = slice(part * width, part * width + width)
            gw_proj = matmul(normed_t[...], grad_pre[:, span]).astype(bf16)
            for piece in range(8):
                grads[layer, piece % 2, piece // 2, :, span] = gw_proj[
                    piece * depth : piece * depth + depth
                ]

        reduce_pair(layer)
        between[3]()

        def through_norm(index, carry):
            at = rows(index)
            grad_normed = matmul_nt(grad_pre[at, :], weights[layer, :, : 4 * width])
            norm = normed[layer, at, :].astype(f32)
            gradient[at, :] = gradient[at, :] + hidden_inv[layer, at, :] * (
                grad_normed
                - jnp.mean(grad_normed, axis=1, keepdims=True)
                - norm * jnp.mean(grad_normed * norm, axis=1, keepdims=True)
            )
            return carry

        for at_index in range(0, blocks):
            through_norm(at_index, 0)
    def nothing():
        pass

    backward(1, (nothing, nothing, nothing, nothing))
    backward(0, (lambda: reduce_z(1), nothing, nothing, nothing))


    reduce_z(0)

    def give_back(index):
        at = pl.ds(index * 256, 256)
        spot = lax.broadcasted_iota(jnp.int32, (256, 256), 0) + index * 256
        parts = [
            (spot == target_ref[:, first : first + 256]).astype(f32).astype(bf16)
            for first in range(0, length, 256)
        ]
        found[at, :] = matmul(
            jnp.concatenate(parts, axis=1), gradient[...].astype(bf16)
        ).astype(bf16)

    for at_index in range(slots // 256):
        give_back(at_index)

    def send_grads(step, carry):
        other = lax.rem(me + step, owners)
        pltpu.make_async_remote_copy(
            src_ref=found.at[pl.ds(other * capacity, capacity)],
            dst_ref=incoming_ref.at[pl.ds(me * capacity, capacity)],
            send_sem=grad_send,
            recv_sem=grad_recv,
            device_id=device_of(other, emb_count),
            device_id_type=MESH,
        ).start()
        return carry

    lax.fori_loop(1, 17, send_grads, 0)
    reduce_x()
    lax.fori_loop(17, 49, send_grads, 0)
    reduce_y()
    lax.fori_loop(49, 89, send_grads, 0)
    reduce_g()
    lax.fori_loop(89, owners, send_grads, 0)
    incoming_ref[own, :] = found[own, :]
    receive("g", 0)
    pltpu.make_async_copy(found.at[lines], found.at[lines], grad_send).wait()
    pltpu.make_async_copy(incoming_ref.at[lines], incoming_ref.at[lines], grad_recv).wait()


def run_step(owner, offset, w_proj, w_out, table, cotangent, owners, emb_count, capacity):
    f32, bf16, i32 = jnp.float32, jnp.bfloat16, jnp.int32
    layer_count, depth, split = w_proj.shape
    columns = split + w_out.shape[2]
    length, width = cotangent.shape
    slots = owners * capacity
    blocks = length // 256
    pairs = blocks * (blocks + 1) // 2
    heads = width // DH
    two = layer_count
    vmem = pl.BlockSpec(memory_space=pltpu.VMEM)
    sem = pltpu.SemaphoreType.DMA
    scratch = [
        ((1, length), i32),
        ((1, length), i32),
        (w_proj.shape, bf16),
        (w_out.shape, bf16),
        ((length, width), bf16),
        ((slots, width), bf16),
        ((1, length), i32),
        ((two, 4, 2, depth, columns), bf16),
        ((owners, length), bf16),
        ((owners, 1, 128), i32),
        ((owners, 1, 128), i32),
        ((slots, width), bf16),
        ((two, length, width), bf16),
        ((two, length, 1), f32),
        ((two, length, width), bf16),
        ((two, length, split), bf16),
        ((two, length, width), bf16),
        ((two, length, width), bf16),
        ((two, length * heads, width), bf16),
        ((two, length * heads, width), bf16),
        ((two, pairs, 256, 256 * heads), bf16),
        ((two, pairs, 256, 256 * heads), bf16),
        ((two, length, width), f32),
        ((two, length, 1), f32),
        ((two, length, width), bf16),
        ((length, width), f32),
        ((256, width), f32),
        ((length, width), bf16),
        ((length, split), bf16),
        ((width, length), bf16),
        ((width, length), bf16),
        ((width, length), bf16),
        ((width, length), f32),
        ((width, length), f32),
        ((two, 2, 4, depth, columns), bf16),
        ((two, 4, depth, columns), bf16),
        ((two, 3, depth, columns), bf16),
        ((two, 4, 16, columns // 2), bf16),
        ((two, 3, 16, columns // 2), bf16),
        ((two, 4, 16, columns // 2), bf16),
    ]
    return pl.pallas_call(
        functools.partial(step_kernel, owners, emb_count, capacity),
        out_shape=(
            jax.ShapeDtypeStruct((slots, width), bf16),
            jax.ShapeDtypeStruct((1, slots), i32),
            jax.ShapeDtypeStruct((two, 4, 16, columns // 2), bf16),
        ),
        in_specs=[pl.BlockSpec(memory_space=pl.ANY)] * 6,
        out_specs=(vmem,) * 3,
        scratch_shapes=[pltpu.VMEM(*one) for one in scratch]
        + [sem((9,))]
        + [sem] * 6
        + [sem((3,)), sem((3,)), sem((4,)), sem((4,)), sem((two, 13)), sem((two, 13))],
        compiler_params=pltpu.CompilerParams(
            collective_id=1, has_side_effects=True, vmem_limit_bytes=62 << 20
        ),
        name="step",
    )(owner, offset, w_proj, w_out, table, cotangent)


def update_kernel(
    block, scale, table_ref, requested_ref, stale_ref, incoming_ref, total_ref, new_ref, proj_ref, out_ref
):
    @pl.when(pl.program_id(0) == 0)
    def _():
        half = total_ref.shape[3]
        split = proj_ref.shape[2]
        for part in range(4):
            spot = slice(part // 2 * 16, part // 2 * 16 + 16)
            value = total_ref[:, part].astype(jnp.float32) * scale
            if part % 2 == 0:
                proj_ref[:, spot, :half] = value
            else:
                proj_ref[:, spot, half:] = value[:, :, : split - half]
                out_ref[:, spot, :] = value[:, :, split - half :]

    count = requested_ref.shape[1]
    first = pl.program_id(0) * block
    row = first + lax.broadcasted_iota(jnp.int32, (block, count), 0)
    pick = (row == requested_ref[...]).astype(jnp.float32).astype(jnp.bfloat16)
    grad = jnp.dot(pick, incoming_ref[...], preferred_element_type=jnp.float32)
    rate = 0.5 / (1.0 + stale_ref[...].astype(jnp.float32))
    same = lax.broadcasted_iota(jnp.int32, (128, 128), 0) == lax.broadcasted_iota(
        jnp.int32, (128, 128), 1
    )
    for part in range(block // 128):
        rows = slice(part * 128, part * 128 + 128)
        spread = jnp.where(same, rate[0, part : part + 1, :], 0.0)
        column = jnp.sum(spread, axis=1, keepdims=True)
        new_ref[rows, :] = table_ref[rows, :] - column * grad[rows, :]


def update_table(table, requested, staleness, incoming, total, scale):
    rows, width = table.shape
    block = 1024
    count = incoming.shape[0]
    parts = block // 128
    layer_count, _, depth, half = total.shape
    depth *= 2
    split = 2 * half - width
    whole = lambda *dims: pl.BlockSpec(dims, lambda i: (0,) * len(dims))
    return pl.pallas_call(
        functools.partial(update_kernel, block, scale),
        out_shape=(
            jax.ShapeDtypeStruct(table.shape, jnp.float32),
            jax.ShapeDtypeStruct((layer_count, depth, split), jnp.float32),
            jax.ShapeDtypeStruct((layer_count, depth, width), jnp.float32),
        ),
        grid=(rows // block,),
        in_specs=[
            pl.BlockSpec((block, width), lambda i: (i, 0)),
            whole(1, count),
            pl.BlockSpec((1, parts, 128), lambda i: (i, 0, 0)),
            whole(count, width),
            whole(*total.shape),
        ],
        out_specs=(
            pl.BlockSpec((block, width), lambda i: (i, 0)),
            whole(layer_count, depth, split),
            whole(layer_count, depth, width),
        ),
        compiler_params=pltpu.CompilerParams(vmem_limit_bytes=58 << 20),
        name="update_table",
    )(
        table,
        requested,
        staleness.reshape(rows // block, parts, 128),
        incoming,
        total,
    )


def local(item_table, item_owner, item_row, staleness, w_proj, w_out, out_grad):
    emb_count = lax.axis_size("emb")
    owners = lax.axis_size("fsdp") * emb_count
    length = item_row.shape[1]
    capacity = 2 * length // owners
    incoming, requested, total = run_step(
        item_owner.reshape(1, length),
        item_row,
        w_proj,
        w_out,
        item_table,
        out_grad[0],
        owners,
        emb_count,
        capacity,
    )
    norm_scale = (owners * length) ** (-0.5)
    return update_table(item_table, requested, staleness, incoming, total, norm_scale)


def solution(mesh):
    return jax.shard_map(
        local,
        mesh=mesh,
        in_specs=(
            P(("fsdp", "emb"), None),
            P(("fsdp", "emb"), None, None),
            P(("fsdp", "emb"), None),
            P(("fsdp", "emb")),
            P(None, "fsdp", None),
            P(None, "fsdp", None),
            P(("fsdp", "emb"), None, None),
        ),
        out_specs=(P(("fsdp", "emb"), None), P(None, "fsdp", None), P(None, "fsdp", None)),
        check_vma=False,
    )
```

```python
import functools

import jax
import jax.numpy as jnp
from jax import lax
from jax.experimental import pallas as pl
from jax.experimental.pallas import tpu as pltpu
from jax.sharding import PartitionSpec as P

MESH = pl.DeviceIdType.MESH

DH = 64


EPSILON = 1e-05


NT = (((1,), (1,)), ((), ()))


def matmul(left, right):
    return jnp.dot(left, right, preferred_element_type=jnp.float32)


def matmul_nt(left, right):
    return lax.dot_general(left, right, NT, preferred_element_type=jnp.float32)


def to_column(row):
    same = lax.broadcasted_iota(jnp.int32, (128, 128), 0) == lax.broadcasted_iota(
        jnp.int32, (128, 128), 1
    )
    parts = [
        jnp.sum(jnp.where(same, row[:, at : at + 128], 0.0), axis=1, keepdims=True)
        for at in range(0, row.shape[1], 128)
    ]
    return parts[0] if len(parts) == 1 else jnp.concatenate(parts, axis=0)


def device_of(index, emb_count):
    return (index // emb_count, lax.rem(index, emb_count))


def greet(me, owners, emb_count):
    barrier = pltpu.get_barrier_semaphore()

    def hello(step, carry):
        other = lax.rem(me + step, owners)
        pl.semaphore_signal(
            barrier, inc=1, device_id=device_of(other, emb_count), device_id_type=MESH
        )
        return carry

    lax.fori_loop(1, owners, hello, 0)
    return barrier


def step_kernel(
    owners,
    emb_count,
    capacity,
    owner_hbm,
    offset_hbm,
    proj_hbm,
    out_hbm,
    table_hbm,
    cotangent_hbm,
    incoming_ref,
    requested_ref,
    total_ref,
    owner_ref,
    offset_ref,
    proj_ref,
    out_ref,
    cotangent_ref,
    returned_ref,
    target_ref,
    weights_ref,
    member,
    ask,
    asked_ref,
    found,
    hidden,
    hidden_inv,
    normed,
    slope,
    gate,
    queries,
    key_heads,
    value_heads,
    attn,
    score_slope,
    mix_normed,
    mix_inv,
    gated,
    gradient,
    mixture,
    grad_mix,
    grad_pre,
    grad_mix_t,
    normed_t,
    queries_t,
    keys_t,
    values_t,
    grads,
    pair_in,
    z_in,
    z_sum,
    x_in,
    y_all,
    load_sems,
    ask_send,
    ask_recv,
    row_send,
    row_recv,
    grad_send,
    grad_recv,
    z_send,
    z_recv,
    pair_send,
    pair_recv,
    reduce_send,
    reduce_recv,
):
    f32, bf16 = jnp.float32, jnp.bfloat16
    fsdp_at = lax.axis_index("fsdp")
    emb_at = lax.axis_index("emb")
    me = fsdp_at * emb_count + emb_at
    z_at = fsdp_at // 2
    core = lax.rem(fsdp_at, 2)
    y_at = emb_at // 4
    x_at = lax.rem(emb_at, 4)
    barrier = greet(me, owners, emb_count)
    loads = []
    for number, (source, place) in enumerate(
        ((owner_hbm, owner_ref), (offset_hbm, offset_ref), (proj_hbm, proj_ref), (out_hbm, out_ref))
    ):
        load = pltpu.make_async_copy(source, place, load_sems.at[number])
        load.start()
        loads.append(load)
    chunk = gradient.shape[0]
    wide = (gradient, mix_normed.at[0], mix_normed.at[1], gradient)
    table_loads = [
        pltpu.make_async_copy(
            table_hbm.at[pl.ds(number * chunk, chunk)], wide[number], load_sems.at[4 + number]
        )
        for number in range(4)
    ]
    for number in range(3):
        table_loads[number].start()
    cotangent_load = pltpu.make_async_copy(cotangent_hbm, cotangent_ref, load_sems.at[8])
    cotangent_load.start()
    for load in loads:
        load.wait()

    split = proj_ref.shape[2]
    weights_ref[:, z_at, core, :, :split] = proj_ref[...]
    weights_ref[:, z_at, core, :, split:] = out_ref[...]

    length = owner_ref.shape[1]
    owner = owner_ref[...]
    value = offset_ref[...] + 1
    high = (value // 64).astype(f32)
    low = lax.rem(value, 64).astype(f32)
    row_at = lax.broadcasted_iota(jnp.int32, (owners, 256), 0)
    for at in range(0, length, 256):
        member[:, at : at + 256] = (
            (row_at == owner[:, at : at + 256]).astype(f32).astype(bf16)
        )
    slots = []
    for at in range(0, length, 256):
        earlier = jnp.zeros((owners, 256), f32)
        for first in range(0, at + 256, 256):
            before = (
                lax.broadcasted_iota(jnp.int32, (256, 256), 0) + (first - at)
                < lax.broadcasted_iota(jnp.int32, (256, 256), 1)
            )
            earlier += matmul(member[:, first : first + 256], before.astype(f32).astype(bf16))
        slots.append(
            jnp.sum(earlier * member[:, at : at + 256].astype(f32), axis=0, keepdims=True)
        )
    slot = jnp.concatenate(slots, axis=1)
    target_ref[...] = owner * capacity + slot.astype(jnp.int32)
    here = lax.broadcasted_iota(jnp.int32, (128, length), 0).astype(f32) == slot
    request = 64.0 * matmul_nt(member[...], jnp.where(here, high, 0.0).astype(bf16))
    request += matmul_nt(member[...], jnp.where(here, low, 0.0).astype(bf16))
    ask[...] = request.astype(jnp.int32).reshape(ask.shape)

    pl.semaphore_wait(barrier, owners - 1)

    def send_ask(step, carry):
        other = lax.rem(me + step, owners)
        pltpu.make_async_remote_copy(
            src_ref=ask.at[other],
            dst_ref=asked_ref.at[me],
            send_sem=ask_send,
            recv_sem=ask_recv,
            device_id=device_of(other, emb_count),
            device_id_type=MESH,
        ).start()
        return carry

    lax.fori_loop(1, owners, send_ask, 0)
    z_copies = []
    for k in range(3):
        to = lax.rem(z_at + k + 1, 4)
        copy = pltpu.make_async_remote_copy(
            src_ref=weights_ref.at[:, z_at, core],
            dst_ref=weights_ref.at[:, z_at, core],
            send_sem=z_send.at[k],
            recv_sem=z_recv.at[k],
            device_id=(to * 2 + core, emb_at),
            device_id_type=MESH,
        )
        copy.start()
        z_copies.append(copy)
    asked_ref[me] = ask[me]

    table = key_heads.at[1]
    table_rows = table.shape[0]
    for number in range(4):
        table_loads[number].wait()

        def narrow(index, carry):
            at = pl.ds(pl.multiple_of(index * 256, 256), 256)
            to = pl.ds(pl.multiple_of(index * 256 + number * chunk, 256), 256)
            table[to, :] = wide[number][at, :].astype(bf16)
            return carry

        lax.fori_loop(0, chunk // 256, narrow, 0)
        if number == 0:
            table_loads[3].start()

    others = pl.ds(0, owners - 1)
    pltpu.make_async_copy(ask.at[others], ask.at[others], ask_send).wait()
    pltpu.make_async_copy(asked_ref.at[others], asked_ref.at[others], ask_recv).wait()

    group = 256 // capacity
    groups = owners // group

    def find(step, carry):
        index = lax.rem(me // group + step, groups)
        first_user = index * group
        wanted = asked_ref[pl.ds(first_user, group)].astype(f32)
        wanted = jnp.broadcast_to(wanted, (group, capacity, 128))
        same = lax.broadcasted_iota(jnp.int32, wanted.shape, 1) == lax.broadcasted_iota(
            jnp.int32, wanted.shape, 2
        )
        column = jnp.sum(jnp.where(same, wanted, 0.0), axis=2, keepdims=True)
        column = column.reshape(256, 1) - 1.0
        diagonal = lax.broadcasted_iota(jnp.int32, (256, 256), 0) == lax.broadcasted_iota(
            jnp.int32, (256, 256), 1
        )
        span = pl.ds(pl.multiple_of(index * 256, 256), 256)
        line = jnp.sum(jnp.where(diagonal, column, 0.0), axis=0, keepdims=True)
        requested_ref[:, span] = line.astype(jnp.int32)
        lane = lax.broadcasted_iota(jnp.int32, (256, 256), 1).astype(f32)
        total = jnp.zeros((256, table.shape[1]), f32)
        for first in range(0, table_rows, 256):
            pick = (lane + float(first) == column).astype(f32).astype(bf16)
            total += matmul(pick, table[first : first + 256, :])
        found[pl.ds(pl.multiple_of(index * 256, 256), 256), :] = total.astype(bf16)

        def send_rows(turn, carry):
            user = first_user + lax.rem(me + turn, group)

            @pl.when(user != me)
            def _():
                pltpu.make_async_remote_copy(
                    src_ref=found.at[pl.ds(user * capacity, capacity)],
                    dst_ref=returned_ref.at[pl.ds(me * capacity, capacity)],
                    send_sem=row_send,
                    recv_sem=row_recv,
                    device_id=device_of(user, emb_count),
                    device_id_type=MESH,
                ).start()

            return carry

        lax.fori_loop(0, group, send_rows, 0)
        return carry

    lax.fori_loop(0, groups, find, 0)
    picks = attn.at[0]
    across = picks.shape[2]
    all_slots = owners * capacity
    halves = all_slots // across
    for part in range(length // 256):
        place = to_column(target_ref[:, part * 256 : part * 256 + 256].astype(f32))
        for first in range(0, all_slots, 256):
            lane = lax.broadcasted_iota(jnp.int32, (256, 256), 1).astype(f32) + float(first)
            span = slice(first % across, first % across + 256)
            picks[part * halves + first // across, :, span] = (
                (lane == place).astype(f32).astype(bf16)
            )
    own = pl.ds(pl.multiple_of(me * capacity, capacity), capacity)
    returned_ref[own, :] = found[own, :]

    for copy in z_copies:
        copy.wait()
    pair_copies = []
    for z in range(4):
        copy = pltpu.make_async_remote_copy(
            src_ref=weights_ref.at[:, z, core],
            dst_ref=weights_ref.at[:, z, core],
            send_sem=pair_send.at[z],
            recv_sem=pair_recv.at[z],
            device_id=(z_at * 2 + 1 - core, emb_at),
            device_id_type=MESH,
        )
        copy.start()
        pair_copies.append(copy)
    for copy in pair_copies:
        copy.wait()
    lines = pl.ds(0, (owners - 1) * capacity)
    pltpu.make_async_copy(found.at[lines], found.at[lines], row_send).wait()
    pltpu.make_async_copy(returned_ref.at[lines], returned_ref.at[lines], row_recv).wait()

    block = 256
    width = cotangent_ref.shape[1]
    blocks = length // block
    heads = width // DH
    slots = returned_ref.shape[0]
    layer_count = weights_ref.shape[0]
    head_of = lax.broadcasted_iota(jnp.int32, (heads, width), 1) // DH
    head_mask = (head_of == lax.broadcasted_iota(jnp.int32, (heads, width), 0)).astype(f32)
    head_mask = head_mask.astype(bf16)

    weights = weights_ref.reshape(layer_count, width, 5 * width)

    def rows(index):
        if isinstance(index, int):
            return pl.ds(index * block, block)
        return pl.ds(pl.multiple_of(index * block, block), block)

    def head_rows(index):
        if isinstance(index, int):
            return pl.ds(index * block * heads, block * heads)
        return pl.ds(pl.multiple_of(index * block * heads, block * heads), block * heads)

    def pair_of(query, key):
        return query * (query + 1) // 2 + key

    def fetch(part, carry):
        total = jnp.zeros((256, width), f32)
        for half in range(halves):
            total += matmul(
                picks[part * halves + half], returned_ref[half * across : half * across + across, :]
            )
        hidden[0, rows(part), :] = total.astype(bf16)
        return carry

    lax.fori_loop(0, length // 256, fetch, 0)

    def forward(layer, carry):
        def project(index, carry):
            at = rows(index)
            value = hidden[layer, at, :].astype(f32)
            center = value - jnp.mean(value, axis=1, keepdims=True)
            inverse = lax.rsqrt(jnp.mean(center * center, axis=1, keepdims=True) + EPSILON)
            norm = (center * inverse).astype(bf16)
            hidden_inv[layer, at, :] = inverse
            normed[layer, at, :] = norm
            for part in range(4):
                columns = slice(part * width, part * width + width)
                pre = matmul(norm, weights[layer, :, columns])
                logistic = 0.5 + 0.5 * jnp.tanh(0.5 * pre)
                act = (pre * logistic).astype(bf16)
                logistic = logistic.astype(bf16)
                slope[layer, at, columns] = logistic + (act - act * logistic)
                if part == 0:
                    gate[layer, at, :] = act
                elif part == 2:
                    queries[layer, at, :] = act * jnp.asarray(0.0625, bf16)
                else:
                    store = value_heads if part == 1 else key_heads
                    for head in range(heads):
                        spot = rows(index * heads + head)
                        store[layer, spot, :] = act * head_mask[head : head + 1, :]
            return carry

        for at_index in range(0, blocks):
            project(at_index, 0)

        def scores(query, key, masked):
            pair = pair_of(query, key)
            query_part = queries[layer, rows(query), :]
            one = jnp.asarray(1.0, bf16)
            if masked:
                visible = lax.broadcasted_iota(
                    jnp.int32, (block, block), 1
                ) <= lax.broadcasted_iota(jnp.int32, (block, block), 0)
            parts = []
            for head in range(heads):
                spot = rows(key * heads + head)
                half = matmul_nt(query_part, key_heads[layer, spot, :]).astype(bf16)
                bend = jnp.tanh(half)
                lift = one + bend
                if masked:
                    lift = jnp.where(visible, lift, jnp.zeros_like(lift))
                columns = slice(head * block, head * block + block)
                part = half * lift
                parts.append(part)
                attn[layer, pair, :, columns] = part
                score_slope[layer, pair, :, columns] = lift * (one + (half - half * bend))
            return matmul(
                jnp.concatenate(parts, axis=1), value_heads[layer, head_rows(key), :]
            )

        def attend_rows(query, carry):
            mixture[...] = scores(query, query, True)

            def before(key, carry):
                mixture[...] += scores(query, key, False)
                return carry

            for at_index in range(0, query):
                before(at_index, 0)
            at = rows(query)
            value = mixture[...]
            center = value - jnp.mean(value, axis=1, keepdims=True)
            inverse = lax.rsqrt(jnp.mean(center * center, axis=1, keepdims=True) + EPSILON)
            norm = center * inverse
            mix_normed[layer, at, :] = norm
            mix_inv[layer, at, :] = inverse
            gated_part = (norm * gate[layer, at, :].astype(f32)).astype(bf16)
            gated[layer, at, :] = gated_part

            branch = matmul(gated_part, weights[layer, :, 4 * width :])
            following = lax.rem(layer + 1, layer_count)
            hidden[following, at, :] = (hidden[layer, at, :].astype(f32) + branch).astype(bf16)
            return carry

        for at_index in range(0, blocks):
            attend_rows(at_index, 0)
        return carry

    lax.fori_loop(0, layer_count, forward, 0)

    cotangent_load.wait()
    gradient[...] = cotangent_ref[...].astype(f32)

    in_flight = {}

    def send(name, layer, number, source, place, where):
        copy = pltpu.make_async_remote_copy(
            src_ref=source,
            dst_ref=place,
            send_sem=reduce_send.at[layer, number],
            recv_sem=reduce_recv.at[layer, number],
            device_id=where,
            device_id_type=MESH,
        )
        copy.start()
        in_flight.setdefault((name, layer), []).append(copy)

    def receive(name, layer):
        for copy in in_flight[name, layer]:
            copy.wait()

    def reduce_pair(layer):
        where = (z_at * 2 + 1 - core, emb_at)
        send("pair", layer, 0, grads.at[layer, 1 - core], pair_in.at[layer], where)

    def reduce_z(layer):
        receive("pair", layer)
        for z in range(4):
            pair_in[layer, z] = (
                grads[layer, core, z].astype(f32) + pair_in[layer, z].astype(f32)
            ).astype(bf16)
        for k in range(3):
            to = lax.rem(z_at + k + 1, 4)
            where = (to * 2 + core, emb_at)
            send("z", layer, 1 + k, pair_in.at[layer, to], z_in.at[layer, k], where)

    def reduce_x():
        for layer in range(layer_count):
            receive("z", layer)
        half = z_sum.shape[3]
        for layer in range(layer_count):
            for part in range(4):
                spot = slice(part // 2 * 16, part // 2 * 16 + 16)
                span = slice(part % 2 * half, part % 2 * half + half)
                value = pair_in[layer, z_at, spot, span].astype(f32)
                for k in range(3):
                    value += z_in[layer, k, spot, span].astype(f32)
                z_sum[layer, part] = value.astype(bf16)
        for k in range(3):
            to = lax.rem(x_at + k + 1, 4)
            where = (fsdp_at, y_at * 4 + to)
            send("x", 0, 4 + k, z_sum.at[:, to], x_in.at[:, k], where)

    def reduce_y():
        receive("x", 0)
        for layer in range(layer_count):
            value = z_sum[layer, x_at].astype(f32)
            for k in range(3):
                value += x_in[layer, k].astype(f32)
            y_all[layer, y_at] = value.astype(bf16)
        for k in range(3):
            to = lax.rem(y_at + k + 1, 4)
            where = (fsdp_at, to * 4 + x_at)
            send("y", 0, 7 + k, y_all.at[:, y_at], y_all.at[:, y_at], where)

    def reduce_g():
        receive("y", 0)
        for layer in range(layer_count):
            value = y_all[layer, 0].astype(f32)
            for y in range(1, 4):
                value += y_all[layer, y].astype(f32)
            total_ref[layer, x_at] = value.astype(bf16)
        for k in range(3):
            to = lax.rem(x_at + k + 1, 4)
            where = (fsdp_at, y_at * 4 + to)
            place = total_ref.at[:, x_at]
            send("g", 0, 10 + k, place, place, where)

    def backward(layer, between):

        def through_gate(index, carry):
            at = rows(index)
            grad_round = gradient[at, :].astype(bf16)
            grad_gated = matmul_nt(grad_round, weights[layer, :, 4 * width :])
            norm = mix_normed[layer, at, :]
            first = slope[layer, at, :width].astype(f32)
            grad_pre[at, :width] = (grad_gated * norm * first).astype(bf16)
            inner = grad_gated * gate[layer, at, :].astype(f32)
            grad = mix_inv[layer, at, :] * (
                inner
                - jnp.mean(inner, axis=1, keepdims=True)
                - norm * jnp.mean(inner * norm, axis=1, keepdims=True)
            )
            grad_mix[at, :] = grad.astype(bf16)
            grad_mix_t[:, at] = grad.T.astype(bf16)
            normed_t[:, at] = normed[layer, at, :].T
            queries_t[:, at] = queries[layer, at, :].T
            return carry

        for at_index in range(0, blocks):
            through_gate(at_index, 0)
        between[0]()

        gw_out = lax.dot_general(
            gated[layer],
            gradient[...].astype(bf16),
            (((0,), (0,)), ((), ())),
            preferred_element_type=jnp.float32,
        ).astype(bf16)
        depth = grads.shape[3]
        for part in range(8):
            grads[layer, part % 2, part // 2, :, 4 * width :] = gw_out[
                part * depth : part * depth + depth
            ]

        keys_t[...] = jnp.zeros_like(keys_t)
        values_t[...] = jnp.zeros_like(values_t)

        def through_scores(query, carry):
            mixture[...] = jnp.zeros_like(mixture)

            def one(key, carry):
                pair = pair_of(query, key)
                here = rows(query)
                there = rows(key)
                grad_part = grad_mix[here, :]
                parts = []
                for head in range(heads):
                    spot = rows(key * heads + head)
                    columns = slice(head * block, head * block + block)
                    lines = slice(head * DH, head * DH + DH)
                    grad = matmul_nt(grad_part, value_heads[layer, spot, :]).astype(bf16)
                    values_t[lines, there] += matmul(
                        grad_mix_t[lines, here], attn[layer, pair, :, columns]
                    )
                    part = grad * score_slope[layer, pair, :, columns]
                    parts.append(part)
                    keys_t[lines, there] += matmul(queries_t[lines, here], part)
                mixture[...] += matmul(
                    jnp.concatenate(parts, axis=1), key_heads[layer, head_rows(key), :]
                )
                return carry

            for at_index in range(0, query + 1):
                one(at_index, 0)
            at = rows(query)
            third = slope[layer, at, 2 * width : 3 * width].astype(f32)
            grad_pre[at, 2 * width : 3 * width] = (mixture[...] * 0.0625 * third).astype(bf16)
            return carry

        for at_index in range(0, blocks):
            through_scores(at_index, 0)
        between[1]()

        def through_keys(key, carry):
            at = rows(key)
            for part, total in ((1, values_t), (3, keys_t)):
                span = slice(part * width, part * width + width)
                grad_pre[at, span] = (total[:, at].T * slope[layer, at, span].astype(f32)).astype(
                    bf16
                )
            return carry

        for at_index in range(0, blocks):
            through_keys(at_index, 0)
        between[2]()

        def weigh():
            for part in range(4):
                span = slice(part * width, part * width + width)
                gw_proj = matmul(normed_t[...], grad_pre[:, span]).astype(bf16)
                for piece in range(8):
                    grads[layer, piece % 2, piece // 2, :, span] = gw_proj[
                        piece * depth : piece * depth + depth
                    ]
            reduce_pair(layer)

        if layer > 0:
            weigh()
        between[3]()

        def through_norm(index, carry):
            at = rows(index)
            grad_normed = matmul_nt(grad_pre[at, :], weights[layer, :, : 4 * width])
            norm = normed[layer, at, :].astype(f32)
            gradient[at, :] = gradient[at, :] + hidden_inv[layer, at, :] * (
                grad_normed
                - jnp.mean(grad_normed, axis=1, keepdims=True)
                - norm * jnp.mean(grad_normed * norm, axis=1, keepdims=True)
            )
            return carry

        for at_index in range(0, blocks):
            through_norm(at_index, 0)
        return weigh
    def nothing():
        pass

    backward(1, (nothing, nothing, nothing, nothing))
    weigh_first = backward(0, (lambda: reduce_z(1), nothing, nothing, nothing))


    def give_back(index):
        at = pl.ds(index * 256, 256)
        spot = lax.broadcasted_iota(jnp.int32, (256, 256), 0) + index * 256
        parts = [
            (spot == target_ref[:, first : first + 256]).astype(f32).astype(bf16)
            for first in range(0, length, 256)
        ]
        found[at, :] = matmul(
            jnp.concatenate(parts, axis=1), gradient[...].astype(bf16)
        ).astype(bf16)

    for at_index in range(slots // 256):
        give_back(at_index)

    def send_grads(step, carry):
        other = lax.rem(me + step, owners)
        pltpu.make_async_remote_copy(
            src_ref=found.at[pl.ds(other * capacity, capacity)],
            dst_ref=incoming_ref.at[pl.ds(me * capacity, capacity)],
            send_sem=grad_send,
            recv_sem=grad_recv,
            device_id=device_of(other, emb_count),
            device_id_type=MESH,
        ).start()
        return carry

    lax.fori_loop(1, 33, send_grads, 0)
    weigh_first()
    reduce_z(0)
    reduce_x()
    lax.fori_loop(33, 49, send_grads, 0)
    reduce_y()
    lax.fori_loop(49, 89, send_grads, 0)
    reduce_g()
    lax.fori_loop(89, owners, send_grads, 0)
    incoming_ref[own, :] = found[own, :]
    receive("g", 0)
    pltpu.make_async_copy(found.at[lines], found.at[lines], grad_send).wait()
    pltpu.make_async_copy(incoming_ref.at[lines], incoming_ref.at[lines], grad_recv).wait()


def run_step(owner, offset, w_proj, w_out, table, cotangent, owners, emb_count, capacity):
    f32, bf16, i32 = jnp.float32, jnp.bfloat16, jnp.int32
    layer_count, depth, split = w_proj.shape
    columns = split + w_out.shape[2]
    length, width = cotangent.shape
    slots = owners * capacity
    blocks = length // 256
    pairs = blocks * (blocks + 1) // 2
    heads = width // DH
    two = layer_count
    vmem = pl.BlockSpec(memory_space=pltpu.VMEM)
    sem = pltpu.SemaphoreType.DMA
    scratch = [
        ((1, length), i32),
        ((1, length), i32),
        (w_proj.shape, bf16),
        (w_out.shape, bf16),
        ((length, width), bf16),
        ((slots, width), bf16),
        ((1, length), i32),
        ((two, 4, 2, depth, columns), bf16),
        ((owners, length), bf16),
        ((owners, 1, 128), i32),
        ((owners, 1, 128), i32),
        ((slots, width), bf16),
        ((two, length, width), bf16),
        ((two, length, 1), f32),
        ((two, length, width), bf16),
        ((two, length, split), bf16),
        ((two, length, width), bf16),
        ((two, length, width), bf16),
        ((two, length * heads, width), bf16),
        ((two, length * heads, width), bf16),
        ((two, pairs, 256, 256 * heads), bf16),
        ((two, pairs, 256, 256 * heads), bf16),
        ((two, length, width), f32),
        ((two, length, 1), f32),
        ((two, length, width), bf16),
        ((length, width), f32),
        ((256, width), f32),
        ((length, width), bf16),
        ((length, split), bf16),
        ((width, length), bf16),
        ((width, length), bf16),
        ((width, length), bf16),
        ((width, length), f32),
        ((width, length), f32),
        ((two, 2, 4, depth, columns), bf16),
        ((two, 4, depth, columns), bf16),
        ((two, 3, depth, columns), bf16),
        ((two, 4, 16, columns // 2), bf16),
        ((two, 3, 16, columns // 2), bf16),
        ((two, 4, 16, columns // 2), bf16),
    ]
    return pl.pallas_call(
        functools.partial(step_kernel, owners, emb_count, capacity),
        out_shape=(
            jax.ShapeDtypeStruct((slots, width), bf16),
            jax.ShapeDtypeStruct((1, slots), i32),
            jax.ShapeDtypeStruct((two, 4, 16, columns // 2), bf16),
        ),
        in_specs=[pl.BlockSpec(memory_space=pl.ANY)] * 6,
        out_specs=(vmem,) * 3,
        scratch_shapes=[pltpu.VMEM(*one) for one in scratch]
        + [sem((9,))]
        + [sem] * 6
        + [sem((3,)), sem((3,)), sem((4,)), sem((4,)), sem((two, 13)), sem((two, 13))],
        compiler_params=pltpu.CompilerParams(
            collective_id=1, has_side_effects=True, vmem_limit_bytes=62 << 20
        ),
        name="step",
    )(owner, offset, w_proj, w_out, table, cotangent)


def update_kernel(
    block, scale, table_ref, requested_ref, stale_ref, incoming_ref, total_ref, new_ref, proj_ref, out_ref
):
    @pl.when(pl.program_id(0) == 0)
    def _():
        half = total_ref.shape[3]
        split = proj_ref.shape[2]
        for part in range(4):
            spot = slice(part // 2 * 16, part // 2 * 16 + 16)
            value = total_ref[:, part].astype(jnp.float32) * scale
            if part % 2 == 0:
                proj_ref[:, spot, :half] = value
            else:
                proj_ref[:, spot, half:] = value[:, :, : split - half]
                out_ref[:, spot, :] = value[:, :, split - half :]

    count = requested_ref.shape[1]
    first = pl.program_id(0) * block
    row = first + lax.broadcasted_iota(jnp.int32, (block, count), 0)
    pick = (row == requested_ref[...]).astype(jnp.float32).astype(jnp.bfloat16)
    grad = jnp.dot(pick, incoming_ref[...], preferred_element_type=jnp.float32)
    rate = 0.5 / (1.0 + stale_ref[...].astype(jnp.float32))
    same = lax.broadcasted_iota(jnp.int32, (128, 128), 0) == lax.broadcasted_iota(
        jnp.int32, (128, 128), 1
    )
    for part in range(block // 128):
        rows = slice(part * 128, part * 128 + 128)
        spread = jnp.where(same, rate[0, part : part + 1, :], 0.0)
        column = jnp.sum(spread, axis=1, keepdims=True)
        new_ref[rows, :] = table_ref[rows, :] - column * grad[rows, :]


def update_table(table, requested, staleness, incoming, total, scale):
    rows, width = table.shape
    block = 1024
    count = incoming.shape[0]
    parts = block // 128
    layer_count, _, depth, half = total.shape
    depth *= 2
    split = 2 * half - width
    whole = lambda *dims: pl.BlockSpec(dims, lambda i: (0,) * len(dims))
    return pl.pallas_call(
        functools.partial(update_kernel, block, scale),
        out_shape=(
            jax.ShapeDtypeStruct(table.shape, jnp.float32),
            jax.ShapeDtypeStruct((layer_count, depth, split), jnp.float32),
            jax.ShapeDtypeStruct((layer_count, depth, width), jnp.float32),
        ),
        grid=(rows // block,),
        in_specs=[
            pl.BlockSpec((block, width), lambda i: (i, 0)),
            whole(1, count),
            pl.BlockSpec((1, parts, 128), lambda i: (i, 0, 0)),
            whole(count, width),
            whole(*total.shape),
        ],
        out_specs=(
            pl.BlockSpec((block, width), lambda i: (i, 0)),
            whole(layer_count, depth, split),
            whole(layer_count, depth, width),
        ),
        compiler_params=pltpu.CompilerParams(vmem_limit_bytes=58 << 20),
        name="update_table",
    )(
        table,
        requested,
        staleness.reshape(rows // block, parts, 128),
        incoming,
        total,
    )


def local(item_table, item_owner, item_row, staleness, w_proj, w_out, out_grad):
    emb_count = lax.axis_size("emb")
    owners = lax.axis_size("fsdp") * emb_count
    length = item_row.shape[1]
    capacity = 2 * length // owners
    incoming, requested, total = run_step(
        item_owner.reshape(1, length),
        item_row,
        w_proj,
        w_out,
        item_table,
        out_grad[0],
        owners,
        emb_count,
        capacity,
    )
    norm_scale = (owners * length) ** (-0.5)
    return update_table(item_table, requested, staleness, incoming, total, norm_scale)


def solution(mesh):
    return jax.shard_map(
        local,
        mesh=mesh,
        in_specs=(
            P(("fsdp", "emb"), None),
            P(("fsdp", "emb"), None, None),
            P(("fsdp", "emb"), None),
            P(("fsdp", "emb")),
            P(None, "fsdp", None),
            P(None, "fsdp", None),
            P(("fsdp", "emb"), None, None),
        ),
        out_specs=(P(("fsdp", "emb"), None), P(None, "fsdp", None), P(None, "fsdp", None)),
        check_vma=False,
    )
```
